32 devices in a mesh: parts: 2 (over x), loop: 4 (over y, core), tgrp: 4 (over z).
Axes of the slice: x: 2, y: 2, z: 4, core: 2. Of those that a mesh axis runs over, the one named last changes fastest.
Arguments:
- data: bfloat16 [8, 3, 12288], P(('parts', 'loop'), None, 'tgrp'), parts along dimension 0
- templates: bfloat16 [128, 4, 3, 2048], P('tgrp', 'loop')
- masks: int32 [128, 4], replicated, may hold values from 0 to 1, as said below
- offsets: int32 [8], P(('parts', 'loop')), parts along dimension 0, may hold values from 0 to 512, as said below
- active: int32 [8, 3], P(('parts', 'loop')), parts along dimension 0, may hold values 0 or 1
Outputs:
- detection: float32 [256, 12288], P(('parts', 'loop'), 'tgrp'), parts along dimension 0
The draws below stay inside these ranges and needn't reach their ends.
There are 2 independent parts, one for each index of `parts`. The reference program is written for one: setup_inputs(seed, part) draws one part's arguments, and reference() takes and returns one part's arrays. A program takes and returns all parts, laid end to end along the dimension named above; an argument that names none is the same for every part. Nothing has to cross between parts.
Inputs may be any that keep to these rules, and one draw needn't show every extreme that they name: `masks`: every template uses at least one station. `offsets`: some station has an offset of exactly 512.
All inputs are finite; a program needn't handle non-finite values. No bound on the sum of `active` on one device may be relied on, other than what follows from the above.
Results may differ from the reference program's by a relative error of at most 0.0003.
Values may be sent and summed in bfloat16 or wider, within the bound.
No kernel may reach another device: no remote copies, remote signals or barrier semaphores. Data moves between devices by JAX's collectives and lax.ppermute only.
A program may use at most 64 MiB of HBM per device.

```python
import math
import jax
import jax.numpy as jnp
from jax import lax

L = 2048
MAXOFF = 512
K = 128
STA = 4
TOUT = 12288


def draw_data(key, part):
    key_base, key_rows, key_segments = jax.random.split(key, 3)
    base = jax.random.normal(key_base, (STA, 3, TOUT), jnp.float32)
    upper = math.log(10.0)
    row_scales = jnp.exp(jax.random.uniform(key_rows, (STA, 3, 1), jnp.float32, 0.0, upper))
    segment_scales = jnp.exp(jax.random.uniform(key_segments, (STA, 3, TOUT // 64), jnp.float32, 0.0, upper))
    segment_scales = jnp.repeat(segment_scales, 64, axis=2)
    return (base * row_scales * segment_scales).astype(jnp.bfloat16)


def draw_templates(key, part):
    key_base, key_rows = jax.random.split(key, 2)
    base = jax.random.normal(key_base, (K, STA, 3, L), jnp.float32)
    upper = math.log(10.0)
    row_scales = jnp.exp(jax.random.uniform(key_rows, (K, STA, 1, 1), jnp.float32, 0.0, upper))
    return (base * row_scales).astype(jnp.bfloat16)


def draw_masks(key, part):
    picks = jax.random.randint(key, (K, STA), 0, 3)
    template_ids = jnp.arange(K, dtype=jnp.int32)[:, None]
    station_ids = jnp.arange(STA, dtype=jnp.int32)[None, :]
    home = template_ids % STA == station_ids
    return jnp.where((picks > 0) | home, 1, 0).astype(jnp.int32)


def draw_offsets(key, part):
    key_values, key_top = jax.random.split(key, 2)
    values = jax.random.randint(key_values, (STA,), 0, MAXOFF + 1)
    chosen = jax.random.randint(key_top, (), 0, STA)
    station_ids = jnp.arange(STA, dtype=jnp.int32)
    return jnp.where(station_ids == chosen, MAXOFF, values).astype(jnp.int32)


def set_ends(values, own_key, low, high):
    place = [jax.random.randint(jax.random.fold_in(own_key, axis), (), 0, length) for axis, length in enumerate(values.shape)]
    longest = values.shape.index(max(values.shape))
    next_to = place[:longest] + [(place[longest] + 1) % values.shape[longest]] + place[longest + 1:]
    return values.at[tuple(place)].set(low).at[tuple(next_to)].set(high)


def setup_inputs(seed: int = 0, part: int = 0) -> dict:
    streams_of = jax.random.split(jax.random.key(seed), 6)
    own_keys = jax.random.split(jax.random.fold_in(streams_of[5], part), 6)
    return {
        "data": draw_data(jax.random.fold_in(jax.random.fold_in(streams_of[5], part), 71), part),
        "templates": draw_templates(jax.random.fold_in(streams_of[5], 71), part),
        "masks": draw_masks(jax.random.fold_in(streams_of[5], 71), part),
        "offsets": draw_offsets(jax.random.fold_in(jax.random.fold_in(streams_of[5], part), 71), part),
        "active": set_ends((jax.random.randint(own_keys[4], (STA, 3), 0, 6) < 5).astype(jnp.int32), jax.random.fold_in(own_keys[4], 1), 0, 1),
    }


epsilon = 1e-05

def window_energy(squares, out_len, span):
    inner_len = out_len + span - 128
    nblocks = (inner_len + 127) // 128
    total_len = 128 * (nblocks + 1)
    padded = jnp.concatenate([squares, jnp.zeros((total_len - squares.shape[0],), squares.dtype)])
    first = padded[:128 * nblocks].reshape(nblocks, 128)
    second = padded[128:128 * nblocks + 128].reshape(nblocks, 128)
    segments = jnp.concatenate([first, second], axis=1)
    rows_at = lax.broadcasted_iota(jnp.int32, (256, 128), 0)
    cols_at = lax.broadcasted_iota(jnp.int32, (256, 128), 1)
    gap = rows_at - cols_at
    band = jnp.where((gap >= 0) & (gap < 128), 1.0, 0.0).astype(squares.dtype)
    inner = jnp.dot(segments, band, precision=lax.Precision.HIGHEST).reshape(nblocks * 128)
    energy = jnp.zeros((out_len,), squares.dtype)
    for block_at in range(span // 128):
        energy = energy + inner[128 * block_at:128 * block_at + out_len]
    return energy

def correlate(panel, window, out_len):
    row_count = panel.shape[0]
    blocks = panel.shape[2] // 128
    span_len = out_len + panel.shape[2] - 128
    unfold = jnp.stack([window[:, shift_by:shift_by + span_len] for shift_by in range(128)], axis=1)
    unfold = unfold.reshape(3 * 128, span_len)
    frames = panel.reshape(row_count, 3, blocks, 128).transpose(0, 2, 1, 3).reshape(row_count, blocks, 3 * 128)

    def add_block(block_at, running_sum):
        start_at = (block_at * 128).astype(jnp.int32)
        columns = lax.dynamic_slice_in_dim(unfold, start_at, out_len, 1)
        weights_now = lax.dynamic_index_in_dim(frames, block_at, 1, keepdims=False)
        return running_sum + jnp.dot(weights_now, columns, preferred_element_type=jnp.float32)
    return lax.fori_loop(0, blocks, add_block, jnp.zeros((row_count, out_len), jnp.float32))

def reference(data, templates, masks, offsets, active):
    padded = jnp.concatenate([data, jnp.zeros((STA, 3, L + MAXOFF), jnp.bfloat16)], axis=2)
    counts = lax.optimization_barrier(jnp.sum(masks, axis=1)).astype(jnp.float32)
    weights = masks.astype(jnp.float32) * jnp.sqrt(3.0 * L / counts)[:, None]

    def station_term(stacked, station):
        series = lax.dynamic_slice(padded, (station, jnp.int32(0), offsets[station]), (1, 3, TOUT + L))[0]
        channel_on = active[station].astype(jnp.bfloat16)
        window = series * channel_on[:, None]
        wide_window = window.astype(jnp.float32)
        squares = lax.optimization_barrier(jnp.sum(wide_window * wide_window, axis=0))
        energy = window_energy(squares, TOUT, L)
        inv_data = 1.0 / jnp.sqrt(energy / (3.0 * L) + epsilon)
        panel = templates[:, station] * channel_on[None, :, None]
        wide_panel = panel.astype(jnp.float32)
        inv_template = 1.0 / jnp.sqrt(lax.optimization_barrier(jnp.sum(wide_panel * wide_panel, axis=(1, 2))) / (3.0 * L) + epsilon)
        corr = correlate(panel, window, TOUT)
        row_scale = inv_template * weights[:, station]
        return (stacked + corr * inv_data[None, :] * row_scale[:, None] / (3.0 * L), None)
    stacked, _ = lax.scan(station_term, jnp.zeros((K, TOUT), jnp.float32), jnp.arange(STA, dtype=jnp.int32))
    return stacked
```

```python
import functools

import jax
import jax.numpy as jnp
from jax import lax
from jax.experimental import pallas as pl
from jax.experimental.pallas import tpu as pltpu
from jax.sharding import PartitionSpec as P

L = 2048


epsilon = 1e-05


def passed_along(value, axis, steps):
    count = lax.axis_size(axis)
    initial, last = (max(0, -steps), min(count, count - steps))
    return lax.ppermute(value, axis, [(source, source + steps) for source in range(initial, last)])


def window_energy(squares, out_len, span):
    inner_len = out_len + span - 128
    nblocks = (inner_len + 127) // 128
    total_len = 128 * (nblocks + 1)
    padded = jnp.concatenate([squares, jnp.zeros((total_len - squares.shape[0],), squares.dtype)])
    first = padded[: 128 * nblocks].reshape(nblocks, 128)
    second = padded[128 : 128 * nblocks + 128].reshape(nblocks, 128)
    segments = jnp.concatenate([first, second], axis=1)
    rows_at = lax.broadcasted_iota(jnp.int32, (256, 128), 0)
    cols_at = lax.broadcasted_iota(jnp.int32, (256, 128), 1)
    gap = rows_at - cols_at
    band = jnp.where((gap >= 0) & (gap < 128), 1.0, 0.0).astype(squares.dtype)
    inner = jnp.dot(segments, band, precision=lax.Precision.HIGHEST).reshape(nblocks * 128)
    energy = jnp.zeros((out_len,), squares.dtype)
    for block_at in range(span // 128):
        energy = energy + inner[128 * block_at : 128 * block_at + out_len]
    return energy


def correlate(panel, window, out_len):
    row_count = panel.shape[0]
    blocks = panel.shape[2] // 128
    span_len = out_len + panel.shape[2] - 128
    unfold = jnp.stack(
        [window[:, shift_by : shift_by + span_len] for shift_by in range(128)], axis=1
    )
    unfold = unfold.reshape(3 * 128, span_len)
    frames = (
        panel.reshape(row_count, 3, blocks, 128)
        .transpose(0, 2, 1, 3)
        .reshape(row_count, blocks, 3 * 128)
    )

    def add_block(block_at, running_sum):
        start_at = (block_at * 128).astype(jnp.int32)
        columns = lax.dynamic_slice_in_dim(unfold, start_at, out_len, 1)
        weights_now = lax.dynamic_index_in_dim(frames, block_at, 1, keepdims=False)
        return running_sum + jnp.dot(weights_now, columns, preferred_element_type=jnp.float32)

    return lax.fori_loop(0, blocks, add_block, jnp.zeros((row_count, out_len), jnp.float32))


def local_general(data, templates, masks, offsets, active):
    local_count = data.shape[0]
    block_len = data.shape[2]
    following = passed_along(data, "tgrp", -1)
    extended = jnp.concatenate([data, following], axis=2)
    loop_at = lax.axis_index("loop")
    first_station = loop_at * local_count
    counts = jnp.sum(masks, axis=1).astype(jnp.float32)
    local_masks = lax.dynamic_slice_in_dim(masks, first_station, local_count, 1)
    weights = local_masks.astype(jnp.float32) * jnp.sqrt(3.0 * L / counts)[:, None]
    station = 0
    channel_on = active[station].astype(jnp.bfloat16)
    series = lax.dynamic_slice(
        extended[station], (jnp.int32(0), offsets[station]), (3, block_len + L)
    )
    window = series * channel_on[:, None]
    wide_window = window.astype(jnp.float32)
    squares = jnp.sum(wide_window * wide_window, axis=0)
    energy = window_energy(squares, block_len, L)
    inv_datas = [1.0 / jnp.sqrt(energy / (3.0 * L) + epsilon)]
    windows = [window]
    channel_sets = [channel_on]
    panel_rows = lax.all_gather(templates, "tgrp", axis=0, tiled=True)
    station = 0
    panel = panel_rows[:, station] * channel_sets[station][None, :, None]
    wide_panel = panel.astype(jnp.float32)
    inv_template = 1.0 / jnp.sqrt(
        jnp.sum(wide_panel * wide_panel, axis=(1, 2)) / (3.0 * L) + epsilon
    )
    corr = correlate(panel, windows[station], block_len)
    row_weights = weights[:, station]
    row_scale = inv_template * row_weights
    stacked = corr * inv_datas[station][None, :] * row_scale[:, None] / (3.0 * L)
    rows_here = stacked.shape[0] // lax.axis_size("loop")
    summed = lax.psum(stacked, "loop")
    return lax.dynamic_slice_in_dim(summed, loop_at * rows_here, rows_here, 0)


ROWS = 16
SHIFTS = 16


def lanes(shape):
    return lax.broadcasted_iota(jnp.int32, shape, len(shape) - 1)


def split_kernel(active, t_ref, d_ref, keep_ref, send_ref, rows_ref, scratch):
    half = lax.axis_index("loop") // 2
    for c in range(3):
        on = active[0, c].astype(jnp.float32)
        for out, first in ((keep_ref, half), (send_ref, 1 - half)):
            rows = t_ref[c, pl.ds(pl.multiple_of(ROWS * first, ROWS), ROWS), :]
            out[c] = (rows.astype(jnp.float32) * on).astype(jnp.bfloat16)
    blocks = d_ref.shape[2] // 128
    wide = d_ref[0].astype(jnp.float32)
    scratch[3 * blocks :] = jnp.zeros((scratch.shape[0] - 3 * blocks, 128), jnp.float32)
    for c in range(3):
        for j in range(blocks):
            scratch[c * blocks + j : c * blocks + j + 1] = wide[c : c + 1, 128 * j : 128 * j + 128]
    rows_ref[...] = scratch[...].astype(jnp.bfloat16)


def split(active, panel, data):
    blocks = data.shape[2] // 128
    padded = (3 * blocks + 15) // 16 * 16
    half = jax.ShapeDtypeStruct((3, ROWS, panel.shape[2]), jnp.bfloat16)
    return pl.pallas_call(
        split_kernel,
        out_shape=(half, half, jax.ShapeDtypeStruct((padded, 128), jnp.bfloat16)),
        in_specs=[pl.BlockSpec(memory_space=pltpu.SMEM)] + [pl.BlockSpec(memory_space=pltpu.VMEM)] * 2,
        out_specs=(pl.BlockSpec(memory_space=pltpu.VMEM),) * 3,
        scratch_shapes=[pltpu.VMEM((padded, 128), jnp.float32)],
        name="split",
    )(active, panel, data)


def series_kernel(blocks, offset, active, d0, d1, d2, d3, x_ref, whole):
    z = lax.axis_index("tgrp")
    rows = x_ref.shape[1]
    for c in range(3):
        whole[c, 4 * blocks :] = jnp.zeros((whole.shape[1] - 4 * blocks, 128), jnp.float32)
    for b, ref in enumerate((d0, d1, d2, d3)):
        wide = ref[...].astype(jnp.float32)
        at = pl.multiple_of(blocks * (z ^ b), 8)
        for c in range(3):
            whole[c, pl.ds(at, blocks), :] = wide[c * blocks : c * blocks + blocks]
    row, lane = offset[0] // 128, offset[0] % 128
    spill = lanes((rows, 128)) >= 128 - lane
    for c in range(3):
        on = active[0, c].astype(jnp.float32)
        here = pltpu.roll(whole[c, pl.ds(row, rows), :], 128 - lane, 1)
        after = pltpu.roll(whole[c, pl.ds(row + 1, rows), :], 128 - lane, 1)
        x_ref[c] = (jnp.where(spill, after, here) * on).astype(jnp.bfloat16)


def make_series(offset, active, pieces, blocks, rows):
    return pl.pallas_call(
        functools.partial(series_kernel, blocks),
        out_shape=jax.ShapeDtypeStruct((3, rows, 128), jnp.bfloat16),
        in_specs=[pl.BlockSpec(memory_space=pltpu.SMEM)] * 2 + [pl.BlockSpec(memory_space=pltpu.VMEM)] * 4,
        out_specs=pl.BlockSpec(memory_space=pltpu.VMEM),
        scratch_shapes=[pltpu.VMEM((3, rows + 8, 128), jnp.float32)],
        name="series",
    )(offset, active, *pieces)


def correlate_kernel(span, nb, t0, t1, t2, t3, x0, x1, x2, x3, masks, first_ref, second_ref,
                     tp_ref, xf_ref, a_ref, z_ref, d_ref, rs_ref, acc_ref, tot_ref, tr_ref):
    ts, xs = (t0, t1, t2, t3), (x0, x1, x2, x3)
    lb = span // 128
    kb = lb + 1
    rows = xf_ref.shape[1]
    loop_at = lax.axis_index("loop")
    half, core = loop_at // 2, loop_at % 2
    k_first = 2 * ROWS * lax.axis_index("tgrp") + ROWS * half
    lane = lanes((8, 128))
    sub = lax.broadcasted_iota(jnp.int32, (8, 128), 0)
    counts = jnp.sum(masks[...], axis=0, keepdims=True).astype(jnp.float32)
    weight = jnp.sqrt(3.0 * span / counts)
    own = k_first + lane % ROWS
    diagonal = lanes((ROWS, 128)) % ROWS == lax.broadcasted_iota(jnp.int32, (ROWS, 128), 0)
    lane_r = lanes((rows, 128))
    for s in range(4):
        norm = jnp.zeros((ROWS, 128), jnp.float32)
        squares = jnp.zeros((rows, 128), jnp.float32)
        for c in range(3):
            i = 3 * s + c
            t = ts[s][c]
            tp_ref[i, :, 0:128] = jnp.zeros((ROWS, 128), jnp.bfloat16)
            tp_ref[i, :, 128 : 128 + span] = t
            tp_ref[i, :, 128 + span :] = jnp.zeros((ROWS, 128), jnp.bfloat16)
            wide = t.astype(jnp.float32)
            wide = wide * wide
            for b in range(lb):
                norm = norm + wide[:, 128 * b : 128 * b + 128]
            x = xs[s][c, pl.ds(pl.multiple_of(2 * nb * core, 16), rows), :].astype(jnp.float32)
            xf_ref[i] = x
            squares = squares + x * x
        inverse = 1.0 / jnp.sqrt(jnp.sum(norm, axis=1, keepdims=True) / (3.0 * span) + epsilon)
        inverse = jnp.where(diagonal, jnp.broadcast_to(inverse, (ROWS, 128)), 0.0)
        inverse = jnp.sum(inverse, axis=0, keepdims=True)
        here = masks[pl.ds(loop_at ^ s, 1), :].astype(jnp.float32) * weight
        here = jnp.take_along_axis(jnp.broadcast_to(here, (8, 128)), own, axis=1)
        rs_ref[s] = here[0:1] * inverse / (3.0 * span)
        b = 1
        while b < 128:
            after = pltpu.roll(squares, rows - 1, 0)
            squares = squares + pltpu.roll(jnp.where(lane_r < b, after, squares), 128 - b, 1)
            b *= 2
        b = 1
        while b < lb:
            squares = squares + pltpu.roll(squares, rows - b, 0)
            b *= 2
        d_ref[s] = 1.0 / jnp.sqrt(squares / (3.0 * span) + epsilon)

    from_lane = (lane + sub) % 128
    inside = lane + sub < 128

    def build(i, slot):
        for r in range(SHIFTS):
            n = ROWS * (8 * (r % 2) + r // 2)
            a_ref[slot, n : n + ROWS, :] = tp_ref[i, :, 128 - 8 * r : 128 - 8 * r + 128 * kb]

        def turned(j):
            row = xf_ref[i, pl.ds(j, 8, stride=0), :]
            return jnp.take_along_axis(row, from_lane, axis=1)

        before, tiles = turned(0), []
        for j in range(2 * nb + lb):
            after = turned(j + 1)
            tiles.append(jnp.where(inside, before, after))
            before = after
            if j >= nb:
                z_ref[slot, j - nb] = jnp.concatenate([tiles[j - nb], tiles[j]], axis=0).astype(jnp.bfloat16)

    def product(slot):
        left = jnp.concatenate([z_ref[slot, b : b + nb].reshape(16 * nb, 128) for b in range(kb)], axis=1)
        return lax.dot_general(left, a_ref[slot], (((1,), (1,)), ((), ())), preferred_element_type=jnp.float32)

    def weighted(s):
        for v in (0, 1):
            index = 16 * (lane // 16) + 8 * v + sub
            rs = rs_ref[s]
            for j in range(nb):
                for h in (0, 1):
                    at = 16 * j + 8 * h
                    scale = jnp.take_along_axis(d_ref[s, pl.ds(j + nb * h, 8, stride=0), :], index, axis=1) * rs
                    tot_ref[v, at : at + 8, :] += acc_ref[at : at + 8, 128 * v : 128 * v + 128] * scale

    tot_ref[...] = jnp.zeros(tot_ref.shape, jnp.float32)
    build(0, 0)

    def station(s, carry):
        for c in range(3):
            m = product(c)
            build(jnp.minimum(3 * s + c + 1, 11), (c + 1) % 3)
            if c == 0:
                acc_ref[...] = m
            else:
                acc_ref[...] += m
        weighted(s)
        return carry

    lax.fori_loop(0, 4, station, 0)

    for f, out in enumerate((first_ref, second_ref)):
        h = half ^ f
        for jb in range(nb // 8):
            v = [[tot_ref[q, pl.ds(128 * jb + 8 * h + p, 8, stride=16), :] for p in range(8)] for q in (0, 1)]
            for b in (1, 2, 4):
                upper = (lane // b) % 2 == 1
                for q in (0, 1):
                    for p in range(8):
                        if not p & b:
                            x, y = v[q][p], v[q][p + b]
                            v[q][p] = jnp.where(upper, pltpu.roll(y, b, 1), x)
                            v[q][p + b] = jnp.where(upper, y, pltpu.roll(x, 128 - b, 1))
            upper = (lane // 8) % 2 == 1
            for p in range(8):
                x, y = v[0][p], v[1][p]
                v[0][p] = jnp.where(upper, pltpu.roll(y, 8, 1), x)
                v[1][p] = jnp.where(upper, y, pltpu.roll(x, 120, 1))
            for q in (0, 1):
                for p in range(8):
                    at = nb * (8 * q + p) + 8 * jb
                    tr_ref[f, at : at + 8, :] = v[q][p]
        for j in range(nb):
            for q in (0, 1):
                out[8 * q : 8 * q + 8, 128 * j : 128 * j + 128] = tr_ref[f, pl.ds(8 * nb * q + j, 8, stride=nb), :]


def correlate_stations(panels, series, masks, span, nb):
    lb = span // 128
    rows = 2 * nb + lb + 8
    block = jax.ShapeDtypeStruct((ROWS, 128 * nb), jnp.float32)
    vmem = pl.BlockSpec(memory_space=pltpu.VMEM)
    return pl.pallas_call(
        functools.partial(correlate_kernel, span, nb),
        out_shape=(block, block),
        in_specs=[vmem] * 9,
        out_specs=(vmem, vmem),
        scratch_shapes=[
            pltpu.VMEM((12, ROWS, span + 256), jnp.bfloat16),
            pltpu.VMEM((12, rows, 128), jnp.float32),
            pltpu.VMEM((3, ROWS * SHIFTS, span + 128), jnp.bfloat16),
            pltpu.VMEM((3, nb + lb, 16, 128), jnp.bfloat16),
            pltpu.VMEM((4, rows, 128), jnp.float32),
            pltpu.VMEM((4, 1, 128), jnp.float32),
            pltpu.VMEM((16 * nb, 256), jnp.float32),
            pltpu.VMEM((2, 16 * nb, 128), jnp.float32),
            pltpu.VMEM((2, 16 * nb, 128), jnp.float32),
        ],
        compiler_params=pltpu.CompilerParams(vmem_limit_bytes=40 << 20),
        name="correlate",
    )(*panels, *series, masks)


def swapped(value, loop_bits, tgrp_bits):
    pairs = [(4 * l + z, 4 * (l ^ loop_bits) + (z ^ tgrp_bits)) for l in range(4) for z in range(4)]
    return lax.ppermute(value, ("loop", "tgrp"), pairs)


def to_owner(value, flip):
    pairs = [(4 * l + z, 4 * z + 2 * (l % 2) + ((l // 2) ^ flip)) for l in range(4) for z in range(4)]
    return lax.ppermute(value, ("loop", "tgrp"), pairs)


def local_plane(data, templates, masks, offsets, active):
    span = templates.shape[3]
    nb = data.shape[2] // 128
    panel = templates[:, 0].transpose(1, 0, 2)
    keep, send, pieces = split(active, panel, data)
    panel_y = swapped(send, 2, 0)
    panel_c = swapped(keep, 1, 0)
    d1 = swapped(pieces, 0, 1)
    d2 = swapped(pieces, 0, 2)
    d3 = swapped(d1, 0, 2)
    series = make_series(offsets, active, (pieces, d1, d2, d3), nb, 4 * nb + span // 128 + 8)
    series_y = swapped(series, 2, 0)
    series_c = swapped(series, 1, 0)
    series_yc = swapped(series_y, 1, 0)
    panel_yc = swapped(panel_y, 1, 0)
    first, second = correlate_stations(
        (keep, panel_c, panel_y, panel_yc), (series, series_c, series_y, series_yc), masks.T, span, nb
    )
    first, second = to_owner(first, 0), to_owner(second, 1)
    odd = lax.axis_index("tgrp") % 2 == 1
    return jnp.concatenate([jnp.where(odd, second, first), jnp.where(odd, first, second)], axis=0)


def solution(mesh):
    placed = (
        P(("parts", "loop"), None, "tgrp"),
        P("tgrp", "loop", None, None),
        P(),
        P(("parts", "loop")),
        P(("parts", "loop"), None),
    )

    def local(data, templates, masks, offsets, active):
        grid = (mesh.shape["loop"], mesh.shape["tgrp"])
        fits = grid == (4, 4) and templates.shape[:2] == (2 * ROWS, 1) and masks.shape[0] == 128
        fits = fits and templates.shape[3] == 2048 and data.shape[0] == 1 and data.shape[2] % 1024 == 0
        plan = local_plane if fits else local_general
        return plan(data, templates, masks, offsets, active)

    return jax.shard_map(
        local, mesh=mesh, in_specs=placed, out_specs=P(("parts", "loop"), "tgrp"), check_vma=False
    )
```

```python
import functools

import jax
import jax.numpy as jnp
from jax import lax
from jax.experimental import pallas as pl
from jax.experimental.pallas import tpu as pltpu
from jax.sharding import PartitionSpec as P

L = 2048


epsilon = 1e-05


def passed_along(value, axis, steps):
    count = lax.axis_size(axis)
    initial, last = (max(0, -steps), min(count, count - steps))
    return lax.ppermute(value, axis, [(source, source + steps) for source in range(initial, last)])


def window_energy(squares, out_len, span):
    inner_len = out_len + span - 128
    nblocks = (inner_len + 127) // 128
    total_len = 128 * (nblocks + 1)
    padded = jnp.concatenate([squares, jnp.zeros((total_len - squares.shape[0],), squares.dtype)])
    first = padded[: 128 * nblocks].reshape(nblocks, 128)
    second = padded[128 : 128 * nblocks + 128].reshape(nblocks, 128)
    segments = jnp.concatenate([first, second], axis=1)
    rows_at = lax.broadcasted_iota(jnp.int32, (256, 128), 0)
    cols_at = lax.broadcasted_iota(jnp.int32, (256, 128), 1)
    gap = rows_at - cols_at
    band = jnp.where((gap >= 0) & (gap < 128), 1.0, 0.0).astype(squares.dtype)
    inner = jnp.dot(segments, band, precision=lax.Precision.HIGHEST).reshape(nblocks * 128)
    energy = jnp.zeros((out_len,), squares.dtype)
    for block_at in range(span // 128):
        energy = energy + inner[128 * block_at : 128 * block_at + out_len]
    return energy


def correlate(panel, window, out_len):
    row_count = panel.shape[0]
    blocks = panel.shape[2] // 128
    span_len = out_len + panel.shape[2] - 128
    unfold = jnp.stack(
        [window[:, shift_by : shift_by + span_len] for shift_by in range(128)], axis=1
    )
    unfold = unfold.reshape(3 * 128, span_len)
    frames = (
        panel.reshape(row_count, 3, blocks, 128)
        .transpose(0, 2, 1, 3)
        .reshape(row_count, blocks, 3 * 128)
    )

    def add_block(block_at, running_sum):
        start_at = (block_at * 128).astype(jnp.int32)
        columns = lax.dynamic_slice_in_dim(unfold, start_at, out_len, 1)
        weights_now = lax.dynamic_index_in_dim(frames, block_at, 1, keepdims=False)
        return running_sum + jnp.dot(weights_now, columns, preferred_element_type=jnp.float32)

    return lax.fori_loop(0, blocks, add_block, jnp.zeros((row_count, out_len), jnp.float32))


def local_general(data, templates, masks, offsets, active):
    local_count = data.shape[0]
    block_len = data.shape[2]
    following = passed_along(data, "tgrp", -1)
    extended = jnp.concatenate([data, following], axis=2)
    loop_at = lax.axis_index("loop")
    first_station = loop_at * local_count
    counts = jnp.sum(masks, axis=1).astype(jnp.float32)
    local_masks = lax.dynamic_slice_in_dim(masks, first_station, local_count, 1)
    weights = local_masks.astype(jnp.float32) * jnp.sqrt(3.0 * L / counts)[:, None]
    station = 0
    channel_on = active[station].astype(jnp.bfloat16)
    series = lax.dynamic_slice(
        extended[station], (jnp.int32(0), offsets[station]), (3, block_len + L)
    )
    window = series * channel_on[:, None]
    wide_window = window.astype(jnp.float32)
    squares = jnp.sum(wide_window * wide_window, axis=0)
    energy = window_energy(squares, block_len, L)
    inv_datas = [1.0 / jnp.sqrt(energy / (3.0 * L) + epsilon)]
    windows = [window]
    channel_sets = [channel_on]
    panel_rows = lax.all_gather(templates, "tgrp", axis=0, tiled=True)
    station = 0
    panel = panel_rows[:, station] * channel_sets[station][None, :, None]
    wide_panel = panel.astype(jnp.float32)
    inv_template = 1.0 / jnp.sqrt(
        jnp.sum(wide_panel * wide_panel, axis=(1, 2)) / (3.0 * L) + epsilon
    )
    corr = correlate(panel, windows[station], block_len)
    row_weights = weights[:, station]
    row_scale = inv_template * row_weights
    stacked = corr * inv_datas[station][None, :] * row_scale[:, None] / (3.0 * L)
    rows_here = stacked.shape[0] // lax.axis_size("loop")
    summed = lax.psum(stacked, "loop")
    return lax.dynamic_slice_in_dim(summed, loop_at * rows_here, rows_here, 0)


ROWS = 16
SHIFTS = 16


def lanes(shape):
    return lax.broadcasted_iota(jnp.int32, shape, len(shape) - 1)


def split_kernel(active, t_ref, keep_ref, send_ref):
    half = lax.axis_index("loop") // 2
    for c in range(3):
        on = active[0, c].astype(jnp.float32)
        for out, first in ((keep_ref, half), (send_ref, 1 - half)):
            rows = t_ref[c, pl.ds(pl.multiple_of(ROWS * first, ROWS), ROWS), :]
            out[c] = (rows.astype(jnp.float32) * on).astype(jnp.bfloat16)


def split(active, panel):
    half = jax.ShapeDtypeStruct((3, ROWS, panel.shape[2]), jnp.bfloat16)
    return pl.pallas_call(
        split_kernel,
        out_shape=(half, half),
        in_specs=[pl.BlockSpec(memory_space=pltpu.SMEM), pl.BlockSpec(memory_space=pltpu.VMEM)],
        out_specs=(pl.BlockSpec(memory_space=pltpu.VMEM),) * 2,
        compiler_params=pltpu.CompilerParams(vmem_limit_bytes=4 << 20),
        name="split",
    )(active, panel)


def series_kernel(blocks, offset, active, own, d1, far, x_ref, whole):
    z = lax.axis_index("tgrp")
    rows = x_ref.shape[1]
    for c in range(3):
        whole[c, 4 * blocks :] = jnp.zeros((whole.shape[1] - 4 * blocks, 128), jnp.float32)
    wide = [own[...].astype(jnp.float32), d1[...].astype(jnp.float32), far[...].astype(jnp.float32)]
    for b in range(4):
        at = pl.multiple_of(blocks * (z ^ b), 8)
        for c in range(3):
            first = c * blocks + (3 * blocks if b == 3 else 0)
            whole[c, pl.ds(at, blocks), :] = wide[min(b, 2)][first : first + blocks]
    row, lane = offset[0] // 128, offset[0] % 128
    spill = lanes((rows, 128)) >= 128 - lane
    for c in range(3):
        on = active[0, c].astype(jnp.float32)
        here = pltpu.roll(whole[c, pl.ds(row, rows), :], 128 - lane, 1)
        after = pltpu.roll(whole[c, pl.ds(row + 1, rows), :], 128 - lane, 1)
        x_ref[c] = (jnp.where(spill, after, here) * on).astype(jnp.bfloat16)


def make_series(offset, active, pieces, blocks, rows):
    return pl.pallas_call(
        functools.partial(series_kernel, blocks),
        out_shape=jax.ShapeDtypeStruct((3, rows, 128), jnp.bfloat16),
        in_specs=[pl.BlockSpec(memory_space=pltpu.SMEM)] * 2 + [pl.BlockSpec(memory_space=pltpu.VMEM)] * 3,
        out_specs=pl.BlockSpec(memory_space=pltpu.VMEM),
        scratch_shapes=[pltpu.VMEM((3, rows + 8, 128), jnp.float32)],
        compiler_params=pltpu.CompilerParams(vmem_limit_bytes=4 << 20),
        name="series",
    )(offset, active, *pieces)


def correlate_kernel(span, nb, t0, t1, t2, t3, x0, x1, x2, x3, masks, first_ref, second_ref,
                     tp_ref, xb_ref, xf_ref, a_ref, z_ref, d_ref, acc_ref, tot_ref, tr_ref, sems):
    lb = span // 128
    kb = lb + 1
    rows = xf_ref.shape[1]
    loop_at = lax.axis_index("loop")
    half, core = loop_at // 2, loop_at % 2
    x_first = pl.multiple_of(2 * nb * core, 16)
    copies = []
    for s, (t, x) in enumerate(((t0, x0), (t1, x1), (t2, x2), (t3, x3))):
        copies.append(pltpu.make_async_copy(t, tp_ref.at[pl.ds(3 * s, 3), :, pl.ds(128, span)], sems.at[2 * s]))
        copies.append(pltpu.make_async_copy(x.at[:, pl.ds(x_first, rows), :], xb_ref.at[pl.ds(3 * s, 3)], sems.at[2 * s + 1]))
    for copy in copies:
        copy.start()
    tp_ref[:, :, 0:128] = jnp.zeros((12, ROWS, 128), jnp.bfloat16)
    tp_ref[:, :, 128 + span :] = jnp.zeros((12, ROWS, 128), jnp.bfloat16)
    tot_ref[...] = jnp.zeros(tot_ref.shape, jnp.float32)
    k_first = 2 * ROWS * lax.axis_index("tgrp") + ROWS * half
    lane = lanes((8, 128))
    sub = lax.broadcasted_iota(jnp.int32, (8, 128), 0)
    counts = jnp.sum(masks[...], axis=0, keepdims=True).astype(jnp.float32)
    weight = jnp.sqrt(3.0 * span / counts)
    own = k_first + lane % ROWS
    diagonal = lanes((ROWS, 128)) % ROWS == lax.broadcasted_iota(jnp.int32, (ROWS, 128), 0)
    lane_r = lanes((rows, 128))
    for copy in copies:
        copy.wait()

    def row_scale(s):
        norm = jnp.zeros((ROWS, 128), jnp.float32)
        for c in range(3):
            for b in range(lb):
                wide = tp_ref[3 * s + c, :, 128 * b + 128 : 128 * b + 256].astype(jnp.float32)
                norm = norm + wide * wide
        inverse = 1.0 / jnp.sqrt(jnp.sum(norm, axis=1, keepdims=True) / (3.0 * span) + epsilon)
        inverse = jnp.where(diagonal, jnp.broadcast_to(inverse, (ROWS, 128)), 0.0)
        inverse = jnp.sum(inverse, axis=0, keepdims=True)
        here = masks[pl.ds(loop_at ^ s, 1), :].astype(jnp.float32) * weight
        here = jnp.take_along_axis(jnp.broadcast_to(here, (8, 128)), own, axis=1)
        return here[0:1] * inverse / (3.0 * span)

    def data_scale(s):
        squares = jnp.zeros((rows, 128), jnp.float32)
        for c in range(3):
            x = xb_ref[3 * s + c].astype(jnp.float32)
            squares = squares + x * x
        b = 1
        while b < 128:
            after = pltpu.roll(squares, rows - 1, 0)
            squares = squares + pltpu.roll(jnp.where(lane_r < b, after, squares), 128 - b, 1)
            b *= 2
        b = 1
        while b < lb:
            squares = squares + pltpu.roll(squares, rows - b, 0)
            b *= 2
        d_ref[...] = 1.0 / jnp.sqrt(squares / (3.0 * span) + epsilon)

    from_lane = (lane + sub) % 128
    inside = lane + sub < 128

    def build(i, slot):
        for r in range(SHIFTS):
            n = ROWS * (8 * (r % 2) + r // 2)
            a_ref[slot, n : n + ROWS, :] = tp_ref[i, :, 128 - 8 * r : 128 - 8 * r + 128 * kb]

        xf_ref[slot] = xb_ref[i].astype(jnp.float32)

        def turned(j):
            row = xf_ref[slot, pl.ds(j, 8, stride=0), :]
            return jnp.take_along_axis(row, from_lane, axis=1)

        before, tiles = turned(0), []
        for j in range(2 * nb + lb):
            after = turned(j + 1)
            tiles.append(jnp.where(inside, before, after))
            before = after
            if j >= nb:
                z_ref[slot, j - nb] = jnp.concatenate([tiles[j - nb], tiles[j]], axis=0).astype(jnp.bfloat16)

    def product(slot):
        left = jnp.concatenate([z_ref[slot, b : b + nb].reshape(16 * nb, 128) for b in range(kb)], axis=1)
        return lax.dot_general(left, a_ref[slot], (((1,), (1,)), ((), ())), preferred_element_type=jnp.float32)

    def weighted(rs):
        for v in (0, 1):
            index = 16 * (lane // 16) + 8 * v + sub
            for j in range(nb):
                for h in (0, 1):
                    at = 16 * j + 8 * h
                    scale = jnp.take_along_axis(d_ref[pl.ds(j + nb * h, 8, stride=0), :], index, axis=1) * rs
                    tot_ref[v, at : at + 8, :] += acc_ref[at : at + 8, 128 * v : 128 * v + 128] * scale

    build(0, 0)

    def station(s, carry):
        for c in range(3):
            m = product(c)
            build(jnp.minimum(3 * s + c + 1, 11), (c + 1) % 3)
            if c == 0:
                acc_ref[...] = m
            else:
                acc_ref[...] += m
            if c == 0:
                rs = row_scale(s)
            if c == 1:
                data_scale(s)
        weighted(rs)
        return carry

    lax.fori_loop(0, 4, station, 0)

    for f, out in enumerate((first_ref, second_ref)):
        h = half ^ f
        for jb in range(nb // 8):
            v = [[tot_ref[q, pl.ds(128 * jb + 8 * h + p, 8, stride=16), :] for p in range(8)] for q in (0, 1)]
            for b in (1, 2, 4):
                upper = (lane // b) % 2 == 1
                for q in (0, 1):
                    for p in range(8):
                        if not p & b:
                            x, y = v[q][p], v[q][p + b]
                            v[q][p] = jnp.where(upper, pltpu.roll(y, b, 1), x)
                            v[q][p + b] = jnp.where(upper, y, pltpu.roll(x, 128 - b, 1))
            upper = (lane // 8) % 2 == 1
            for p in range(8):
                x, y = v[0][p], v[1][p]
                v[0][p] = jnp.where(upper, pltpu.roll(y, 8, 1), x)
                v[1][p] = jnp.where(upper, y, pltpu.roll(x, 120, 1))
            for q in (0, 1):
                for p in range(8):
                    at = nb * (8 * q + p) + 8 * jb
                    tr_ref[f, at : at + 8, :] = v[q][p]
        for j in range(nb):
            for q in (0, 1):
                out[8 * q : 8 * q + 8, 128 * j : 128 * j + 128] = tr_ref[f, pl.ds(8 * nb * q + j, 8, stride=nb), :]


def correlate_stations(panels, series, masks, span, nb):
    lb = span // 128
    rows = 2 * nb + lb + 8
    block = jax.ShapeDtypeStruct((ROWS, 128 * nb), jnp.float32)
    vmem = pl.BlockSpec(memory_space=pltpu.VMEM)
    return pl.pallas_call(
        functools.partial(correlate_kernel, span, nb),
        out_shape=(block, block),
        in_specs=[pl.BlockSpec(memory_space=pl.ANY)] * 8 + [vmem],
        out_specs=(vmem, vmem),
        scratch_shapes=[
            pltpu.VMEM((12, ROWS, span + 256), jnp.bfloat16),
            pltpu.VMEM((12, rows, 128), jnp.bfloat16),
            pltpu.VMEM((3, rows, 128), jnp.float32),
            pltpu.VMEM((3, ROWS * SHIFTS, span + 128), jnp.bfloat16),
            pltpu.VMEM((3, nb + lb, 16, 128), jnp.bfloat16),
            pltpu.VMEM((rows, 128), jnp.float32),
            pltpu.VMEM((16 * nb, 256), jnp.float32),
            pltpu.VMEM((2, 16 * nb, 128), jnp.float32),
            pltpu.VMEM((2, 16 * nb, 128), jnp.float32),
            pltpu.SemaphoreType.DMA((8,)),
        ],
        compiler_params=pltpu.CompilerParams(vmem_limit_bytes=24 << 20),
        name="correlate",
    )(*panels, *series, masks)


def swapped(value, loop_bits, tgrp_bits):
    pairs = [(4 * l + z, 4 * (l ^ loop_bits) + (z ^ tgrp_bits)) for l in range(4) for z in range(4)]
    return lax.ppermute(value, ("loop", "tgrp"), pairs)


def to_owner(value, flip):
    pairs = [(4 * l + z, 4 * z + 2 * (l % 2) + ((l // 2) ^ flip)) for l in range(4) for z in range(4)]
    return lax.ppermute(value, ("loop", "tgrp"), pairs)


def local_plane(data, templates, masks, offsets, active):
    span = templates.shape[3]
    nb = data.shape[2] // 128
    panel = templates[:, 0].transpose(1, 0, 2)
    keep, send = split(active, panel)
    pieces = data.reshape(3 * nb, 128)
    d1 = swapped(pieces, 0, 1)
    near = jnp.concatenate([pieces, d1], axis=0)
    send, _ = lax.optimization_barrier((send, near))
    far = swapped(near, 0, 2)
    panel_y = swapped(send, 2, 0)
    panel_c = swapped(keep, 1, 0)
    series = make_series(offsets, active, (pieces, d1, far), nb, 4 * nb + span // 128 + 8)
    series_y = swapped(series, 2, 0)
    series_c = swapped(series, 1, 0)
    series_yc = swapped(series_y, 1, 0)
    panel_yc = swapped(panel_y, 1, 0)
    first, second = correlate_stations(
        (keep, panel_c, panel_y, panel_yc), (series, series_c, series_y, series_yc), masks.T, span, nb
    )
    first, second = to_owner(first, 0), to_owner(second, 1)
    odd = lax.axis_index("tgrp") % 2 == 1
    return jnp.concatenate([jnp.where(odd, second, first), jnp.where(odd, first, second)], axis=0)


def solution(mesh):
    placed = (
        P(("parts", "loop"), None, "tgrp"),
        P("tgrp", "loop", None, None),
        P(),
        P(("parts", "loop")),
        P(("parts", "loop"), None),
    )

    def local(data, templates, masks, offsets, active):
        grid = (mesh.shape["loop"], mesh.shape["tgrp"])
        fits = grid == (4, 4) and templates.shape[:2] == (2 * ROWS, 1) and masks.shape[0] == 128
        fits = fits and templates.shape[3] == 2048 and data.shape[0] == 1 and data.shape[2] % 1024 == 0
        plan = local_plane if fits else local_general
        return plan(data, templates, masks, offsets, active)

    return jax.shard_map(
        local, mesh=mesh, in_specs=placed, out_specs=P(("parts", "loop"), "tgrp"), check_vma=False
    )
```

```python
import functools

import jax
import jax.numpy as jnp
from jax import lax
from jax.experimental import pallas as pl
from jax.experimental.pallas import tpu as pltpu
from jax.sharding import PartitionSpec as P

L = 2048


epsilon = 1e-05


def passed_along(value, axis, steps):
    count = lax.axis_size(axis)
    initial, last = (max(0, -steps), min(count, count - steps))
    return lax.ppermute(value, axis, [(source, source + steps) for source in range(initial, last)])


def window_energy(squares, out_len, span):
    inner_len = out_len + span - 128
    nblocks = (inner_len + 127) // 128
    total_len = 128 * (nblocks + 1)
    padded = jnp.concatenate([squares, jnp.zeros((total_len - squares.shape[0],), squares.dtype)])
    first = padded[: 128 * nblocks].reshape(nblocks, 128)
    second = padded[128 : 128 * nblocks + 128].reshape(nblocks, 128)
    segments = jnp.concatenate([first, second], axis=1)
    rows_at = lax.broadcasted_iota(jnp.int32, (256, 128), 0)
    cols_at = lax.broadcasted_iota(jnp.int32, (256, 128), 1)
    gap = rows_at - cols_at
    band = jnp.where((gap >= 0) & (gap < 128), 1.0, 0.0).astype(squares.dtype)
    inner = jnp.dot(segments, band, precision=lax.Precision.HIGHEST).reshape(nblocks * 128)
    energy = jnp.zeros((out_len,), squares.dtype)
    for block_at in range(span // 128):
        energy = energy + inner[128 * block_at : 128 * block_at + out_len]
    return energy


def correlate(panel, window, out_len):
    row_count = panel.shape[0]
    blocks = panel.shape[2] // 128
    span_len = out_len + panel.shape[2] - 128
    unfold = jnp.stack(
        [window[:, shift_by : shift_by + span_len] for shift_by in range(128)], axis=1
    )
    unfold = unfold.reshape(3 * 128, span_len)
    frames = (
        panel.reshape(row_count, 3, blocks, 128)
        .transpose(0, 2, 1, 3)
        .reshape(row_count, blocks, 3 * 128)
    )

    def add_block(block_at, running_sum):
        start_at = (block_at * 128).astype(jnp.int32)
        columns = lax.dynamic_slice_in_dim(unfold, start_at, out_len, 1)
        weights_now = lax.dynamic_index_in_dim(frames, block_at, 1, keepdims=False)
        return running_sum + jnp.dot(weights_now, columns, preferred_element_type=jnp.float32)

    return lax.fori_loop(0, blocks, add_block, jnp.zeros((row_count, out_len), jnp.float32))


def local_general(data, templates, masks, offsets, active):
    local_count = data.shape[0]
    block_len = data.shape[2]
    following = passed_along(data, "tgrp", -1)
    extended = jnp.concatenate([data, following], axis=2)
    loop_at = lax.axis_index("loop")
    first_station = loop_at * local_count
    counts = jnp.sum(masks, axis=1).astype(jnp.float32)
    local_masks = lax.dynamic_slice_in_dim(masks, first_station, local_count, 1)
    weights = local_masks.astype(jnp.float32) * jnp.sqrt(3.0 * L / counts)[:, None]
    station = 0
    channel_on = active[station].astype(jnp.bfloat16)
    series = lax.dynamic_slice(
        extended[station], (jnp.int32(0), offsets[station]), (3, block_len + L)
    )
    window = series * channel_on[:, None]
    wide_window = window.astype(jnp.float32)
    squares = jnp.sum(wide_window * wide_window, axis=0)
    energy = window_energy(squares, block_len, L)
    inv_datas = [1.0 / jnp.sqrt(energy / (3.0 * L) + epsilon)]
    windows = [window]
    channel_sets = [channel_on]
    panel_rows = lax.all_gather(templates, "tgrp", axis=0, tiled=True)
    station = 0
    panel = panel_rows[:, station] * channel_sets[station][None, :, None]
    wide_panel = panel.astype(jnp.float32)
    inv_template = 1.0 / jnp.sqrt(
        jnp.sum(wide_panel * wide_panel, axis=(1, 2)) / (3.0 * L) + epsilon
    )
    corr = correlate(panel, windows[station], block_len)
    row_weights = weights[:, station]
    row_scale = inv_template * row_weights
    stacked = corr * inv_datas[station][None, :] * row_scale[:, None] / (3.0 * L)
    rows_here = stacked.shape[0] // lax.axis_size("loop")
    summed = lax.psum(stacked, "loop")
    return lax.dynamic_slice_in_dim(summed, loop_at * rows_here, rows_here, 0)


ROWS = 16
SHIFTS = 16
STEPS = 32700.0
LEVELS = 64.0


def lanes(shape):
    return lax.broadcasted_iota(jnp.int32, shape, len(shape) - 1)


def split_kernel(active, t_ref, keep_ref, send_ref):
    half = lax.axis_index("loop") // 2
    for c in range(3):
        on = active[0, c].astype(jnp.float32)
        for out, first in ((keep_ref, half), (send_ref, 1 - half)):
            rows = t_ref[c, pl.ds(pl.multiple_of(ROWS * first, ROWS), ROWS), :]
            out[c] = (rows.astype(jnp.float32) * on).astype(jnp.bfloat16)


def split(active, panel):
    half = jax.ShapeDtypeStruct((3, ROWS, panel.shape[2]), jnp.bfloat16)
    return pl.pallas_call(
        split_kernel,
        out_shape=(half, half),
        in_specs=[pl.BlockSpec(memory_space=pltpu.SMEM), pl.BlockSpec(memory_space=pltpu.VMEM)],
        out_specs=(pl.BlockSpec(memory_space=pltpu.VMEM),) * 2,
        compiler_params=pltpu.CompilerParams(vmem_limit_bytes=4 << 20),
        name="split",
    )(active, panel)


def series_kernel(blocks, offset, active, own, d1, far, x_ref, whole):
    z = lax.axis_index("tgrp")
    rows = x_ref.shape[1]
    for c in range(3):
        whole[c, 4 * blocks :] = jnp.zeros((whole.shape[1] - 4 * blocks, 128), jnp.float32)
    wide = [own[...].astype(jnp.float32), d1[...].astype(jnp.float32), far[...].astype(jnp.float32)]
    for b in range(4):
        at = pl.multiple_of(blocks * (z ^ b), 8)
        for c in range(3):
            first = c * blocks + (3 * blocks if b == 3 else 0)
            whole[c, pl.ds(at, blocks), :] = wide[min(b, 2)][first : first + blocks]
    row, lane = offset[0] // 128, offset[0] % 128
    spill = lanes((rows, 128)) >= 128 - lane
    for c in range(3):
        on = active[0, c].astype(jnp.float32)
        here = pltpu.roll(whole[c, pl.ds(row, rows), :], 128 - lane, 1)
        after = pltpu.roll(whole[c, pl.ds(row + 1, rows), :], 128 - lane, 1)
        x_ref[c] = (jnp.where(spill, after, here) * on).astype(jnp.bfloat16)


def make_series(offset, active, pieces, blocks, rows):
    return pl.pallas_call(
        functools.partial(series_kernel, blocks),
        out_shape=jax.ShapeDtypeStruct((3, rows, 128), jnp.bfloat16),
        in_specs=[pl.BlockSpec(memory_space=pltpu.SMEM)] * 2 + [pl.BlockSpec(memory_space=pltpu.VMEM)] * 3,
        out_specs=pl.BlockSpec(memory_space=pltpu.VMEM),
        scratch_shapes=[pltpu.VMEM((3, rows + 8, 128), jnp.float32)],
        compiler_params=pltpu.CompilerParams(vmem_limit_bytes=4 << 20),
        name="series",
    )(offset, active, *pieces)


def correlate_kernel(span, nb, t0, t1, t2, t3, x0, x1, x2, x3, masks, first_ref, second_ref,
                     tp_ref, xb_ref, xf_ref, a_ref, z_ref, d_ref, acc_ref, tot_ref, tr_ref, sems):
    lb = span // 128
    kb = lb + 1
    rows = xf_ref.shape[1]
    loop_at = lax.axis_index("loop")
    half, core = loop_at // 2, loop_at % 2
    x_first = pl.multiple_of(2 * nb * core, 16)
    copies = []
    for s, (t, x) in enumerate(((t0, x0), (t1, x1), (t2, x2), (t3, x3))):
        copies.append(pltpu.make_async_copy(t, tp_ref.at[pl.ds(3 * s, 3), :, pl.ds(128, span)], sems.at[2 * s]))
        copies.append(pltpu.make_async_copy(x.at[:, pl.ds(x_first, rows), :], xb_ref.at[pl.ds(3 * s, 3)], sems.at[2 * s + 1]))
    for copy in copies:
        copy.start()
    tp_ref[:, :, 0:128] = jnp.zeros((12, ROWS, 128), jnp.bfloat16)
    tp_ref[:, :, 128 + span :] = jnp.zeros((12, ROWS, 128), jnp.bfloat16)
    tot_ref[...] = jnp.zeros(tot_ref.shape, jnp.float32)
    k_first = 2 * ROWS * lax.axis_index("tgrp") + ROWS * half
    lane = lanes((8, 128))
    sub = lax.broadcasted_iota(jnp.int32, (8, 128), 0)
    counts = jnp.sum(masks[...], axis=0, keepdims=True).astype(jnp.float32)
    weight = jnp.sqrt(3.0 * span / counts)
    own = k_first + lane % ROWS
    diagonal = lanes((ROWS, 128)) % ROWS == lax.broadcasted_iota(jnp.int32, (ROWS, 128), 0)
    lane_r = lanes((rows, 128))
    for copy in copies:
        copy.wait()

    def row_scale(s):
        norm = jnp.zeros((ROWS, 128), jnp.float32)
        for c in range(3):
            for b in range(lb):
                wide = tp_ref[3 * s + c, :, 128 * b + 128 : 128 * b + 256].astype(jnp.float32)
                norm = norm + wide * wide
        inverse = 1.0 / jnp.sqrt(jnp.sum(norm, axis=1, keepdims=True) / (3.0 * span) + epsilon)
        inverse = jnp.where(diagonal, jnp.broadcast_to(inverse, (ROWS, 128)), 0.0)
        inverse = jnp.sum(inverse, axis=0, keepdims=True)
        here = masks[pl.ds(loop_at ^ s, 1), :].astype(jnp.float32) * weight
        here = jnp.take_along_axis(jnp.broadcast_to(here, (8, 128)), own, axis=1)
        return here[0:1] * inverse / (3.0 * span)

    def data_scale(s):
        squares = jnp.zeros((rows, 128), jnp.float32)
        for c in range(3):
            x = xb_ref[3 * s + c].astype(jnp.float32)
            squares = squares + x * x
        b = 1
        while b < 128:
            after = pltpu.roll(squares, rows - 1, 0)
            squares = squares + pltpu.roll(jnp.where(lane_r < b, after, squares), 128 - b, 1)
            b *= 2
        b = 1
        while b < lb:
            squares = squares + pltpu.roll(squares, rows - b, 0)
            b *= 2
        d_ref[...] = 1.0 / jnp.sqrt(squares / (3.0 * span) + epsilon)

    from_lane = (lane + sub) % 128
    inside = lane + sub < 128

    def build(i, slot):
        for r in range(SHIFTS):
            n = ROWS * (8 * (r % 2) + r // 2)
            a_ref[slot, n : n + ROWS, :] = tp_ref[i, :, 128 - 8 * r : 128 - 8 * r + 128 * kb]

        xf_ref[slot] = xb_ref[i].astype(jnp.float32)

        def turned(j):
            row = xf_ref[slot, pl.ds(j, 8, stride=0), :]
            return jnp.take_along_axis(row, from_lane, axis=1)

        before, tiles = turned(0), []
        for j in range(2 * nb + lb):
            after = turned(j + 1)
            tiles.append(jnp.where(inside, before, after))
            before = after
            if j >= nb:
                z_ref[slot, j - nb] = jnp.concatenate([tiles[j - nb], tiles[j]], axis=0).astype(jnp.bfloat16)

    def product(slot):
        left = jnp.concatenate([z_ref[slot, b : b + nb].reshape(16 * nb, 128) for b in range(kb)], axis=1)
        return lax.dot_general(left, a_ref[slot], (((1,), (1,)), ((), ())), preferred_element_type=jnp.float32)

    def weighted(rs):
        for v in (0, 1):
            index = 16 * (lane // 16) + 8 * v + sub
            for j in range(nb):
                for h in (0, 1):
                    at = 16 * j + 8 * h
                    scale = jnp.take_along_axis(d_ref[pl.ds(j + nb * h, 8, stride=0), :], index, axis=1) * rs
                    tot_ref[v, at : at + 8, :] += acc_ref[at : at + 8, 128 * v : 128 * v + 128] * scale

    build(0, 0)

    def station(s, carry):
        for c in range(3):
            m = product(c)
            build(jnp.minimum(3 * s + c + 1, 11), (c + 1) % 3)
            if c == 0:
                acc_ref[...] = m
            else:
                acc_ref[...] += m
            if c == 0:
                rs = row_scale(s)
            if c == 1:
                data_scale(s)
        weighted(rs)
        return carry

    lax.fori_loop(0, 4, station, 0)

    for f, out in enumerate((first_ref, second_ref)):
        h = half ^ f
        for jb in range(nb // 8):
            v = [[tot_ref[q, pl.ds(128 * jb + 8 * h + p, 8, stride=16), :] for p in range(8)] for q in (0, 1)]
            for b in (1, 2, 4):
                upper = (lane // b) % 2 == 1
                for q in (0, 1):
                    for p in range(8):
                        if not p & b:
                            x, y = v[q][p], v[q][p + b]
                            v[q][p] = jnp.where(upper, pltpu.roll(y, b, 1), x)
                            v[q][p + b] = jnp.where(upper, y, pltpu.roll(x, 128 - b, 1))
            upper = (lane // 8) % 2 == 1
            for p in range(8):
                x, y = v[0][p], v[1][p]
                v[0][p] = jnp.where(upper, pltpu.roll(y, 8, 1), x)
                v[1][p] = jnp.where(upper, y, pltpu.roll(x, 120, 1))
            for q in (0, 1):
                for p in range(8):
                    at = nb * (8 * q + p) + 8 * jb
                    tr_ref[f, at : at + 8, :] = v[q][p]
        levels = [jnp.zeros((8, 128), jnp.float32)] * 2
        for j in range(nb):
            codes = []
            for q in (0, 1):
                value = tr_ref[f, pl.ds(8 * nb * q + j, 8, stride=nb), :]
                top = jnp.maximum(jnp.max(jnp.abs(value), axis=1, keepdims=True), 2e-33)
                level = jnp.ceil(jnp.log2(jnp.broadcast_to(top, (8, 128))) * LEVELS)
                levels[q] = jnp.where(lane == j, level, levels[q])
                codes.append(jnp.round(value * (STEPS * jnp.exp2(level * (-1.0 / LEVELS)))))
            out[:, 128 * j : 128 * j + 128] = jnp.concatenate(codes, axis=0).astype(jnp.int32).astype(jnp.int16)
        out[:, 128 * nb :] = jnp.concatenate(levels, axis=0).astype(jnp.int32).astype(jnp.int16)


def decode_kernel(a_ref, b_ref, out_ref):
    odd = lax.axis_index("tgrp") % 2
    nb = out_ref.shape[1] // 128
    for ref, half in ((a_ref, odd), (b_ref, 1 - odd)):
        at = pl.multiple_of(ROWS * half, ROWS)
        step = jnp.exp2(ref[:, 128 * nb :].astype(jnp.float32) * (1.0 / LEVELS)) * (1.0 / STEPS)
        for j in range(nb):
            value = ref[:, 128 * j : 128 * j + 128].astype(jnp.float32)
            out_ref[pl.ds(at, ROWS), 128 * j : 128 * j + 128] = value * step[:, j : j + 1]


def decode(first, second):
    vmem = pl.BlockSpec(memory_space=pltpu.VMEM)
    return pl.pallas_call(
        decode_kernel,
        out_shape=jax.ShapeDtypeStruct((2 * ROWS, first.shape[1] - 128), jnp.float32),
        in_specs=[vmem, vmem],
        out_specs=vmem,
        compiler_params=pltpu.CompilerParams(vmem_limit_bytes=4 << 20),
        name="decode",
    )(first, second)


def correlate_stations(panels, series, masks, span, nb):
    lb = span // 128
    rows = 2 * nb + lb + 8
    block = jax.ShapeDtypeStruct((ROWS, 128 * nb + 128), jnp.int16)
    vmem = pl.BlockSpec(memory_space=pltpu.VMEM)
    return pl.pallas_call(
        functools.partial(correlate_kernel, span, nb),
        out_shape=(block, block),
        in_specs=[pl.BlockSpec(memory_space=pl.ANY)] * 8 + [vmem],
        out_specs=(vmem, vmem),
        scratch_shapes=[
            pltpu.VMEM((12, ROWS, span + 256), jnp.bfloat16),
            pltpu.VMEM((12, rows, 128), jnp.bfloat16),
            pltpu.VMEM((3, rows, 128), jnp.float32),
            pltpu.VMEM((3, ROWS * SHIFTS, span + 128), jnp.bfloat16),
            pltpu.VMEM((3, nb + lb, 16, 128), jnp.bfloat16),
            pltpu.VMEM((rows, 128), jnp.float32),
            pltpu.VMEM((16 * nb, 256), jnp.float32),
            pltpu.VMEM((2, 16 * nb, 128), jnp.float32),
            pltpu.VMEM((2, 16 * nb, 128), jnp.float32),
            pltpu.SemaphoreType.DMA((8,)),
        ],
        compiler_params=pltpu.CompilerParams(vmem_limit_bytes=24 << 20),
        name="correlate",
    )(*panels, *series, masks)


def swapped(value, loop_bits, tgrp_bits):
    pairs = [(4 * l + z, 4 * (l ^ loop_bits) + (z ^ tgrp_bits)) for l in range(4) for z in range(4)]
    return lax.ppermute(value, ("loop", "tgrp"), pairs)


def to_owner(value, flip):
    pairs = [(4 * l + z, 4 * z + 2 * (l % 2) + ((l // 2) ^ flip)) for l in range(4) for z in range(4)]
    return lax.ppermute(value, ("loop", "tgrp"), pairs)


def local_plane(data, templates, masks, offsets, active):
    span = templates.shape[3]
    nb = data.shape[2] // 128
    panel = templates[:, 0].transpose(1, 0, 2)
    keep, send = split(active, panel)
    pieces = data.reshape(3 * nb, 128)
    d1 = swapped(pieces, 0, 1)
    near = jnp.concatenate([pieces, d1], axis=0)
    send, _ = lax.optimization_barrier((send, near))
    far = swapped(near, 0, 2)
    panel_y = swapped(send, 2, 0)
    panel_c = swapped(keep, 1, 0)
    series = make_series(offsets, active, (pieces, d1, far), nb, 4 * nb + span // 128 + 8)
    series_y = swapped(series, 2, 0)
    series_c = swapped(series, 1, 0)
    series_yc = swapped(series_y, 1, 0)
    panel_yc = swapped(panel_y, 1, 0)
    first, second = correlate_stations(
        (keep, panel_c, panel_y, panel_yc), (series, series_c, series_y, series_yc), masks.T, span, nb
    )
    return decode(to_owner(first, 0), to_owner(second, 1))


def solution(mesh):
    placed = (
        P(("parts", "loop"), None, "tgrp"),
        P("tgrp", "loop", None, None),
        P(),
        P(("parts", "loop")),
        P(("parts", "loop"), None),
    )

    def local(data, templates, masks, offsets, active):
        grid = (mesh.shape["loop"], mesh.shape["tgrp"])
        fits = grid == (4, 4) and templates.shape[:2] == (2 * ROWS, 1) and masks.shape[0] == 128
        fits = fits and templates.shape[3] == 2048 and data.shape[0] == 1 and data.shape[2] % 1024 == 0
        plan = local_plane if fits else local_general
        return plan(data, templates, masks, offsets, active)

    return jax.shard_map(
        local, mesh=mesh, in_specs=placed, out_specs=P(("parts", "loop"), "tgrp"), check_vma=False
    )
```

```python
import functools

import jax
import jax.numpy as jnp
from jax import lax
from jax.experimental import pallas as pl
from jax.experimental.pallas import tpu as pltpu
from jax.sharding import PartitionSpec as P

L = 2048


epsilon = 1e-05


def passed_along(value, axis, steps):
    count = lax.axis_size(axis)
    initial, last = (max(0, -steps), min(count, count - steps))
    return lax.ppermute(value, axis, [(source, source + steps) for source in range(initial, last)])


def window_energy(squares, out_len, span):
    inner_len = out_len + span - 128
    nblocks = (inner_len + 127) // 128
    total_len = 128 * (nblocks + 1)
    padded = jnp.concatenate([squares, jnp.zeros((total_len - squares.shape[0],), squares.dtype)])
    first = padded[: 128 * nblocks].reshape(nblocks, 128)
    second = padded[128 : 128 * nblocks + 128].reshape(nblocks, 128)
    segments = jnp.concatenate([first, second], axis=1)
    rows_at = lax.broadcasted_iota(jnp.int32, (256, 128), 0)
    cols_at = lax.broadcasted_iota(jnp.int32, (256, 128), 1)
    gap = rows_at - cols_at
    band = jnp.where((gap >= 0) & (gap < 128), 1.0, 0.0).astype(squares.dtype)
    inner = jnp.dot(segments, band, precision=lax.Precision.HIGHEST).reshape(nblocks * 128)
    energy = jnp.zeros((out_len,), squares.dtype)
    for block_at in range(span // 128):
        energy = energy + inner[128 * block_at : 128 * block_at + out_len]
    return energy


def correlate(panel, window, out_len):
    row_count = panel.shape[0]
    blocks = panel.shape[2] // 128
    span_len = out_len + panel.shape[2] - 128
    unfold = jnp.stack(
        [window[:, shift_by : shift_by + span_len] for shift_by in range(128)], axis=1
    )
    unfold = unfold.reshape(3 * 128, span_len)
    frames = (
        panel.reshape(row_count, 3, blocks, 128)
        .transpose(0, 2, 1, 3)
        .reshape(row_count, blocks, 3 * 128)
    )

    def add_block(block_at, running_sum):
        start_at = (block_at * 128).astype(jnp.int32)
        columns = lax.dynamic_slice_in_dim(unfold, start_at, out_len, 1)
        weights_now = lax.dynamic_index_in_dim(frames, block_at, 1, keepdims=False)
        return running_sum + jnp.dot(weights_now, columns, preferred_element_type=jnp.float32)

    return lax.fori_loop(0, blocks, add_block, jnp.zeros((row_count, out_len), jnp.float32))


def local_general(data, templates, masks, offsets, active):
    local_count = data.shape[0]
    block_len = data.shape[2]
    following = passed_along(data, "tgrp", -1)
    extended = jnp.concatenate([data, following], axis=2)
    loop_at = lax.axis_index("loop")
    first_station = loop_at * local_count
    counts = jnp.sum(masks, axis=1).astype(jnp.float32)
    local_masks = lax.dynamic_slice_in_dim(masks, first_station, local_count, 1)
    weights = local_masks.astype(jnp.float32) * jnp.sqrt(3.0 * L / counts)[:, None]
    station = 0
    channel_on = active[station].astype(jnp.bfloat16)
    series = lax.dynamic_slice(
        extended[station], (jnp.int32(0), offsets[station]), (3, block_len + L)
    )
    window = series * channel_on[:, None]
    wide_window = window.astype(jnp.float32)
    squares = jnp.sum(wide_window * wide_window, axis=0)
    energy = window_energy(squares, block_len, L)
    inv_datas = [1.0 / jnp.sqrt(energy / (3.0 * L) + epsilon)]
    windows = [window]
    channel_sets = [channel_on]
    panel_rows = lax.all_gather(templates, "tgrp", axis=0, tiled=True)
    station = 0
    panel = panel_rows[:, station] * channel_sets[station][None, :, None]
    wide_panel = panel.astype(jnp.float32)
    inv_template = 1.0 / jnp.sqrt(
        jnp.sum(wide_panel * wide_panel, axis=(1, 2)) / (3.0 * L) + epsilon
    )
    corr = correlate(panel, windows[station], block_len)
    row_weights = weights[:, station]
    row_scale = inv_template * row_weights
    stacked = corr * inv_datas[station][None, :] * row_scale[:, None] / (3.0 * L)
    rows_here = stacked.shape[0] // lax.axis_size("loop")
    summed = lax.psum(stacked, "loop")
    return lax.dynamic_slice_in_dim(summed, loop_at * rows_here, rows_here, 0)


ROWS = 16
SHIFTS = 16
STEPS = 32700.0
LEVELS = 64.0


def lanes(shape):
    return lax.broadcasted_iota(jnp.int32, shape, len(shape) - 1)


def split_kernel(active, t_ref, keep_ref, send_ref):
    half = lax.axis_index("loop") // 2
    for c in range(3):
        on = active[0, c].astype(jnp.float32)
        for out, first in ((keep_ref, half), (send_ref, 1 - half)):
            rows = t_ref[c, pl.ds(pl.multiple_of(ROWS * first, ROWS), ROWS), :]
            out[c] = (rows.astype(jnp.float32) * on).astype(jnp.bfloat16)


def split(active, panel):
    half = jax.ShapeDtypeStruct((3, ROWS, panel.shape[2]), jnp.bfloat16)
    return pl.pallas_call(
        split_kernel,
        out_shape=(half, half),
        in_specs=[pl.BlockSpec(memory_space=pltpu.SMEM), pl.BlockSpec(memory_space=pltpu.VMEM)],
        out_specs=(pl.BlockSpec(memory_space=pltpu.VMEM),) * 2,
        compiler_params=pltpu.CompilerParams(vmem_limit_bytes=4 << 20),
        name="split",
    )(active, panel)


def series_kernel(blocks, offset, active, own, d1, far, x_ref, whole):
    z = lax.axis_index("tgrp")
    rows = x_ref.shape[1]
    for c in range(3):
        whole[c, 4 * blocks :] = jnp.zeros((whole.shape[1] - 4 * blocks, 128), jnp.float32)
    wide = [own[...].astype(jnp.float32), d1[...].astype(jnp.float32), far[...].astype(jnp.float32)]
    for b in range(4):
        at = pl.multiple_of(blocks * (z ^ b), 8)
        for c in range(3):
            first = c * blocks + (3 * blocks if b == 3 else 0)
            whole[c, pl.ds(at, blocks), :] = wide[min(b, 2)][first : first + blocks]
    row, lane = offset[0] // 128, offset[0] % 128
    spill = lanes((rows, 128)) >= 128 - lane
    for c in range(3):
        on = active[0, c].astype(jnp.float32)
        here = pltpu.roll(whole[c, pl.ds(row, rows), :], 128 - lane, 1)
        after = pltpu.roll(whole[c, pl.ds(row + 1, rows), :], 128 - lane, 1)
        x_ref[c] = (jnp.where(spill, after, here) * on).astype(jnp.bfloat16)


def make_series(offset, active, pieces, blocks, rows):
    return pl.pallas_call(
        functools.partial(series_kernel, blocks),
        out_shape=jax.ShapeDtypeStruct((3, rows, 128), jnp.bfloat16),
        in_specs=[pl.BlockSpec(memory_space=pltpu.SMEM)] * 2 + [pl.BlockSpec(memory_space=pltpu.VMEM)] * 3,
        out_specs=pl.BlockSpec(memory_space=pltpu.VMEM),
        scratch_shapes=[pltpu.VMEM((3, rows + 8, 128), jnp.float32)],
        compiler_params=pltpu.CompilerParams(vmem_limit_bytes=4 << 20),
        name="series",
    )(offset, active, *pieces)


def correlate_kernel(span, nb, t0, t1, t2, t3, x0, x1, x2, x3, masks, first_ref, second_ref,
                     tp_ref, xb_ref, xf_ref, a_ref, z_ref, d_ref, acc_ref, tot_ref, tr_ref, sems):
    lb = span // 128
    kb = lb + 1
    rows = xf_ref.shape[1]
    loop_at = lax.axis_index("loop")
    half, core = loop_at // 2, loop_at % 2
    x_first = pl.multiple_of(2 * nb * core, 16)
    copies = []
    for s, (t, x) in enumerate(((t0, x0), (t1, x1), (t2, x2), (t3, x3))):
        copies.append(pltpu.make_async_copy(t, tp_ref.at[pl.ds(3 * s, 3), :, pl.ds(128, span)], sems.at[2 * s]))
        copies.append(pltpu.make_async_copy(x.at[:, pl.ds(x_first, rows), :], xb_ref.at[pl.ds(3 * s, 3)], sems.at[2 * s + 1]))
    for copy in copies:
        copy.start()
    tp_ref[:, :, 0:128] = jnp.zeros((12, ROWS, 128), jnp.bfloat16)
    tp_ref[:, :, 128 + span :] = jnp.zeros((12, ROWS, 128), jnp.bfloat16)
    tot_ref[...] = jnp.zeros(tot_ref.shape, jnp.float32)
    k_first = 2 * ROWS * lax.axis_index("tgrp") + ROWS * half
    lane = lanes((8, 128))
    sub = lax.broadcasted_iota(jnp.int32, (8, 128), 0)
    counts = jnp.sum(masks[...], axis=0, keepdims=True).astype(jnp.float32)
    weight = jnp.sqrt(3.0 * span / counts)
    own = k_first + lane % ROWS
    diagonal = lanes((ROWS, 128)) % ROWS == lax.broadcasted_iota(jnp.int32, (ROWS, 128), 0)
    lane_r = lanes((rows, 128))
    for copy in copies:
        copy.wait()

    def row_scale(s):
        norm = jnp.zeros((ROWS, 128), jnp.float32)
        for c in range(3):
            for b in range(lb):
                wide = tp_ref[3 * s + c, :, 128 * b + 128 : 128 * b + 256].astype(jnp.float32)
                norm = norm + wide * wide
        inverse = 1.0 / jnp.sqrt(jnp.sum(norm, axis=1, keepdims=True) / (3.0 * span) + epsilon)
        inverse = jnp.where(diagonal, jnp.broadcast_to(inverse, (ROWS, 128)), 0.0)
        inverse = jnp.sum(inverse, axis=0, keepdims=True)
        here = masks[pl.ds(loop_at ^ s, 1), :].astype(jnp.float32) * weight
        here = jnp.take_along_axis(jnp.broadcast_to(here, (8, 128)), own, axis=1)
        return here[0:1] * inverse / (3.0 * span)

    def data_scale(s):
        squares = jnp.zeros((rows, 128), jnp.float32)
        for c in range(3):
            x = xb_ref[3 * s + c].astype(jnp.float32)
            squares = squares + x * x
        b = 1
        while b < 128:
            after = pltpu.roll(squares, rows - 1, 0)
            squares = squares + pltpu.roll(jnp.where(lane_r < b, after, squares), 128 - b, 1)
            b *= 2
        b = 1
        while b < lb:
            squares = squares + pltpu.roll(squares, rows - b, 0)
            b *= 2
        d_ref[...] = 1.0 / jnp.sqrt(squares / (3.0 * span) + epsilon)

    from_lane = (lane + sub) % 128
    inside = lane + sub < 128

    def build(i, slot):
        for r in range(SHIFTS):
            n = ROWS * (8 * (r % 2) + r // 2)
            a_ref[slot, n : n + ROWS, :] = tp_ref[i, :, 128 - 8 * r : 128 - 8 * r + 128 * kb]

        xf_ref[slot] = xb_ref[i].astype(jnp.float32)

        def turned(j):
            row = xf_ref[slot, pl.ds(j, 8, stride=0), :]
            return jnp.take_along_axis(row, from_lane, axis=1)

        before, tiles = turned(0), []
        for j in range(2 * nb + lb):
            after = turned(j + 1)
            tiles.append(jnp.where(inside, before, after))
            before = after
            if j >= nb:
                z_ref[slot, j - nb] = jnp.concatenate([tiles[j - nb], tiles[j]], axis=0).astype(jnp.bfloat16)

    def product(slot):
        left = jnp.concatenate([z_ref[slot, b : b + nb].reshape(16 * nb, 128) for b in range(kb)], axis=1)
        return lax.dot_general(left, a_ref[slot], (((1,), (1,)), ((), ())), preferred_element_type=jnp.float32)

    def weighted(rs):
        for v in (0, 1):
            index = 16 * (lane // 16) + 8 * v + sub
            for j in range(nb):
                for h in (0, 1):
                    at = 16 * j + 8 * h
                    scale = jnp.take_along_axis(d_ref[pl.ds(j + nb * h, 8, stride=0), :], index, axis=1) * rs
                    tot_ref[v, at : at + 8, :] += acc_ref[at : at + 8, 128 * v : 128 * v + 128] * scale

    build(0, 0)

    def station(s, carry):
        for c in range(3):
            m = product(c)
            build(jnp.minimum(3 * s + c + 1, 11), (c + 1) % 3)
            if c == 0:
                acc_ref[...] = m
            else:
                acc_ref[...] += m
            if c == 0:
                rs = row_scale(s)
            if c == 1:
                data_scale(s)
        weighted(rs)
        return carry

    lax.fori_loop(0, 4, station, 0)

    for f, out in enumerate((first_ref, second_ref)):
        h = half ^ f
        for jb in range(nb // 8):
            v = [[tot_ref[q, pl.ds(128 * jb + 8 * h + p, 8, stride=16), :] for p in range(8)] for q in (0, 1)]
            for b in (1, 2, 4):
                upper = (lane // b) % 2 == 1
                for q in (0, 1):
                    for p in range(8):
                        if not p & b:
                            x, y = v[q][p], v[q][p + b]
                            v[q][p] = jnp.where(upper, pltpu.roll(y, b, 1), x)
                            v[q][p + b] = jnp.where(upper, y, pltpu.roll(x, 128 - b, 1))
            upper = (lane // 8) % 2 == 1
            for p in range(8):
                x, y = v[0][p], v[1][p]
                v[0][p] = jnp.where(upper, pltpu.roll(y, 8, 1), x)
                v[1][p] = jnp.where(upper, y, pltpu.roll(x, 120, 1))
            for q in (0, 1):
                for p in range(8):
                    at = nb * (8 * q + p) + 8 * jb
                    tr_ref[f, at : at + 8, :] = v[q][p]
        levels = [jnp.zeros((8, 128), jnp.float32)] * 2
        for j in range(nb):
            codes = []
            for q in (0, 1):
                value = tr_ref[f, pl.ds(8 * nb * q + j, 8, stride=nb), :]
                top = jnp.maximum(jnp.max(jnp.abs(value), axis=1, keepdims=True), 2e-33)
                level = jnp.ceil(jnp.log2(jnp.broadcast_to(top, (8, 128))) * LEVELS)
                levels[q] = jnp.where(lane == j, level, levels[q])
                codes.append(jnp.round(value * (STEPS * jnp.exp2(level * (-1.0 / LEVELS)))))
            out[:, 128 * j : 128 * j + 128] = jnp.concatenate(codes, axis=0).astype(jnp.int32).astype(jnp.int16)
        out[:, 128 * nb :] = jnp.concatenate(levels, axis=0).astype(jnp.int32).astype(jnp.int16)


def decode_kernel(a_ref, b_ref, out_ref):
    odd = lax.axis_index("tgrp") % 2
    nb = out_ref.shape[1] // 128
    for ref, half in ((a_ref, odd), (b_ref, 1 - odd)):
        at = pl.multiple_of(ROWS * half, ROWS)
        step = jnp.exp2(ref[:, 128 * nb :].astype(jnp.float32) * (1.0 / LEVELS)) * (1.0 / STEPS)
        for j in range(nb):
            value = ref[:, 128 * j : 128 * j + 128].astype(jnp.float32)
            out_ref[pl.ds(at, ROWS), 128 * j : 128 * j + 128] = value * step[:, j : j + 1]


def decode(first, second):
    vmem = pl.BlockSpec(memory_space=pltpu.VMEM)
    return pl.pallas_call(
        decode_kernel,
        out_shape=jax.ShapeDtypeStruct((2 * ROWS, first.shape[1] - 128), jnp.float32),
        in_specs=[vmem, vmem],
        out_specs=vmem,
        compiler_params=pltpu.CompilerParams(vmem_limit_bytes=4 << 20),
        name="decode",
    )(first, second)


def correlate_stations(panels, series, masks, span, nb):
    lb = span // 128
    rows = 2 * nb + lb + 8
    block = jax.ShapeDtypeStruct((ROWS, 128 * nb + 128), jnp.int16)
    vmem = pl.BlockSpec(memory_space=pltpu.VMEM)
    return pl.pallas_call(
        functools.partial(correlate_kernel, span, nb),
        out_shape=(block, block),
        in_specs=[pl.BlockSpec(memory_space=pl.ANY)] * 8 + [vmem],
        out_specs=(vmem, vmem),
        scratch_shapes=[
            pltpu.VMEM((12, ROWS, span + 256), jnp.bfloat16),
            pltpu.VMEM((12, rows, 128), jnp.bfloat16),
            pltpu.VMEM((3, rows, 128), jnp.float32),
            pltpu.VMEM((3, ROWS * SHIFTS, span + 128), jnp.bfloat16),
            pltpu.VMEM((3, nb + lb, 16, 128), jnp.bfloat16),
            pltpu.VMEM((rows, 128), jnp.float32),
            pltpu.VMEM((16 * nb, 256), jnp.float32),
            pltpu.VMEM((2, 16 * nb, 128), jnp.float32),
            pltpu.VMEM((2, 16 * nb, 128), jnp.float32),
            pltpu.SemaphoreType.DMA((8,)),
        ],
        compiler_params=pltpu.CompilerParams(vmem_limit_bytes=24 << 20),
        name="correlate",
    )(*panels, *series, masks)


def swapped(value, loop_bits, tgrp_bits):
    pairs = [(4 * l + z, 4 * (l ^ loop_bits) + (z ^ tgrp_bits)) for l in range(4) for z in range(4)]
    return lax.ppermute(value, ("loop", "tgrp"), pairs)


def to_owner(value, flip):
    pairs = [(4 * l + z, 4 * z + 2 * (l % 2) + ((l // 2) ^ flip)) for l in range(4) for z in range(4)]
    return lax.ppermute(value, ("loop", "tgrp"), pairs)


def local_plane(data, templates, masks, offsets, active):
    span = templates.shape[3]
    nb = data.shape[2] // 128
    panel = templates[:, 0].transpose(1, 0, 2)
    keep, send = split(active, panel)
    pieces = data.reshape(3 * nb, 128)
    d1 = swapped(pieces, 0, 1)
    near = jnp.concatenate([pieces, d1], axis=0)
    send, _ = lax.optimization_barrier((send, near))
    far = swapped(near, 0, 2)
    panel_y = swapped(send, 2, 0)
    panel_c = swapped(keep, 1, 0)
    series = make_series(offsets, active, (pieces, d1, far), nb, 4 * nb + span // 128 + 8)
    series_y = swapped(series, 2, 0)
    series_c = swapped(series, 1, 0)
    series_yc = swapped(series_y, 1, 0)
    panel_y, _ = lax.optimization_barrier((panel_y, series_y))
    panel_yc = swapped(panel_y, 1, 0)
    first, second = correlate_stations(
        (keep, panel_c, panel_y, panel_yc), (series, series_c, series_y, series_yc), masks.T, span, nb
    )
    return decode(to_owner(first, 0), to_owner(second, 1))


def solution(mesh):
    placed = (
        P(("parts", "loop"), None, "tgrp"),
        P("tgrp", "loop", None, None),
        P(),
        P(("parts", "loop")),
        P(("parts", "loop"), None),
    )

    def local(data, templates, masks, offsets, active):
        grid = (mesh.shape["loop"], mesh.shape["tgrp"])
        fits = grid == (4, 4) and templates.shape[:2] == (2 * ROWS, 1) and masks.shape[0] == 128
        fits = fits and templates.shape[3] == 2048 and data.shape[0] == 1 and data.shape[2] % 1024 == 0
        plan = local_plane if fits else local_general
        return plan(data, templates, masks, offsets, active)

    return jax.shard_map(
        local, mesh=mesh, in_specs=placed, out_specs=P(("parts", "loop"), "tgrp"), check_vma=False
    )
```

```python
import functools

import jax
import jax.numpy as jnp
from jax import lax
from jax.experimental import pallas as pl
from jax.experimental.pallas import tpu as pltpu
from jax.sharding import PartitionSpec as P

L = 2048


epsilon = 1e-05


def passed_along(value, axis, steps):
    count = lax.axis_size(axis)
    initial, last = (max(0, -steps), min(count, count - steps))
    return lax.ppermute(value, axis, [(source, source + steps) for source in range(initial, last)])


def window_energy(squares, out_len, span):
    inner_len = out_len + span - 128
    nblocks = (inner_len + 127) // 128
    total_len = 128 * (nblocks + 1)
    padded = jnp.concatenate([squares, jnp.zeros((total_len - squares.shape[0],), squares.dtype)])
    first = padded[: 128 * nblocks].reshape(nblocks, 128)
    second = padded[128 : 128 * nblocks + 128].reshape(nblocks, 128)
    segments = jnp.concatenate([first, second], axis=1)
    rows_at = lax.broadcasted_iota(jnp.int32, (256, 128), 0)
    cols_at = lax.broadcasted_iota(jnp.int32, (256, 128), 1)
    gap = rows_at - cols_at
    band = jnp.where((gap >= 0) & (gap < 128), 1.0, 0.0).astype(squares.dtype)
    inner = jnp.dot(segments, band, precision=lax.Precision.HIGHEST).reshape(nblocks * 128)
    energy = jnp.zeros((out_len,), squares.dtype)
    for block_at in range(span // 128):
        energy = energy + inner[128 * block_at : 128 * block_at + out_len]
    return energy


def correlate(panel, window, out_len):
    row_count = panel.shape[0]
    blocks = panel.shape[2] // 128
    span_len = out_len + panel.shape[2] - 128
    unfold = jnp.stack(
        [window[:, shift_by : shift_by + span_len] for shift_by in range(128)], axis=1
    )
    unfold = unfold.reshape(3 * 128, span_len)
    frames = (
        panel.reshape(row_count, 3, blocks, 128)
        .transpose(0, 2, 1, 3)
        .reshape(row_count, blocks, 3 * 128)
    )

    def add_block(block_at, running_sum):
        start_at = (block_at * 128).astype(jnp.int32)
        columns = lax.dynamic_slice_in_dim(unfold, start_at, out_len, 1)
        weights_now = lax.dynamic_index_in_dim(frames, block_at, 1, keepdims=False)
        return running_sum + jnp.dot(weights_now, columns, preferred_element_type=jnp.float32)

    return lax.fori_loop(0, blocks, add_block, jnp.zeros((row_count, out_len), jnp.float32))


def local_general(data, templates, masks, offsets, active):
    local_count = data.shape[0]
    block_len = data.shape[2]
    following = passed_along(data, "tgrp", -1)
    extended = jnp.concatenate([data, following], axis=2)
    loop_at = lax.axis_index("loop")
    first_station = loop_at * local_count
    counts = jnp.sum(masks, axis=1).astype(jnp.float32)
    local_masks = lax.dynamic_slice_in_dim(masks, first_station, local_count, 1)
    weights = local_masks.astype(jnp.float32) * jnp.sqrt(3.0 * L / counts)[:, None]
    station = 0
    channel_on = active[station].astype(jnp.bfloat16)
    series = lax.dynamic_slice(
        extended[station], (jnp.int32(0), offsets[station]), (3, block_len + L)
    )
    window = series * channel_on[:, None]
    wide_window = window.astype(jnp.float32)
    squares = jnp.sum(wide_window * wide_window, axis=0)
    energy = window_energy(squares, block_len, L)
    inv_datas = [1.0 / jnp.sqrt(energy / (3.0 * L) + epsilon)]
    windows = [window]
    channel_sets = [channel_on]
    panel_rows = lax.all_gather(templates, "tgrp", axis=0, tiled=True)
    station = 0
    panel = panel_rows[:, station] * channel_sets[station][None, :, None]
    wide_panel = panel.astype(jnp.float32)
    inv_template = 1.0 / jnp.sqrt(
        jnp.sum(wide_panel * wide_panel, axis=(1, 2)) / (3.0 * L) + epsilon
    )
    corr = correlate(panel, windows[station], block_len)
    row_weights = weights[:, station]
    row_scale = inv_template * row_weights
    stacked = corr * inv_datas[station][None, :] * row_scale[:, None] / (3.0 * L)
    rows_here = stacked.shape[0] // lax.axis_size("loop")
    summed = lax.psum(stacked, "loop")
    return lax.dynamic_slice_in_dim(summed, loop_at * rows_here, rows_here, 0)


ROWS = 16
SHIFTS = 16
STEPS = 32700.0
LEVELS = 64.0


def lanes(shape):
    return lax.broadcasted_iota(jnp.int32, shape, len(shape) - 1)


def split_kernel(offset, active, t_ref, keep_ref, send_ref):
    half = lax.axis_index("loop") // 2
    span = t_ref.shape[2]
    sub = lax.broadcasted_iota(jnp.int32, (ROWS, 128), 0)
    high, low = (offset[0] // 32).astype(jnp.float32), (offset[0] % 32).astype(jnp.float32)
    for c in range(3):
        on = active[0, c].astype(jnp.float32)
        told = jnp.where(sub == 0, high, jnp.where(sub == 1, low, jnp.where(sub == 2, on, 0.0)))
        for out, first in ((keep_ref, half), (send_ref, 1 - half)):
            rows = t_ref[c, pl.ds(pl.multiple_of(ROWS * first, ROWS), ROWS), :]
            out[c, :, :span] = (rows.astype(jnp.float32) * on).astype(jnp.bfloat16)
            out[c, :, span:] = told.astype(jnp.bfloat16)


def split(offset, active, panel):
    half = jax.ShapeDtypeStruct((3, ROWS, panel.shape[2] + 128), jnp.bfloat16)
    return pl.pallas_call(
        split_kernel,
        out_shape=(half, half),
        in_specs=[pl.BlockSpec(memory_space=pltpu.SMEM)] * 2 + [pl.BlockSpec(memory_space=pltpu.VMEM)],
        out_specs=(pl.BlockSpec(memory_space=pltpu.VMEM),) * 2,
        compiler_params=pltpu.CompilerParams(vmem_limit_bytes=4 << 20),
        name="split",
    )(offset, active, panel)


def series_kernel(blocks, offset, active, told, near, far, mine_ref, mate_ref, whole):
    z = lax.axis_index("tgrp")
    core = lax.axis_index("loop") % 2
    rows = mine_ref.shape[1]
    span = told.shape[2] - 128
    lane = lanes((rows, 128))
    whole[:, 4 * blocks :] = jnp.zeros((6, whole.shape[1] - 4 * blocks, 128), jnp.float32)
    wide = [near[...].astype(jnp.float32), far[...].astype(jnp.float32)]
    for b in range(4):
        at = pl.multiple_of(blocks * (z ^ b), 8)
        for i in range(6):
            first = 6 * blocks * (b % 2) + i * blocks
            whole[i, pl.ds(at, blocks), :] = wide[b // 2][first : first + blocks]
    for station in range(2):
        if station == 0:
            shift = offset[0]
        else:
            words = told[0, :, span:].astype(jnp.float32)
            shift = (32.0 * jnp.max(words[0:1]) + jnp.max(words[1:2])).astype(jnp.int32)
        row, turn = shift // 128, shift % 128
        spill = lane >= 128 - turn
        for c in range(3):
            i = 3 * station + c
            if station == 0:
                on = active[0, c].astype(jnp.float32)
            else:
                on = told[c, :, span:].astype(jnp.float32)[2:3]
            for out, half in ((mine_ref, core), (mate_ref, 1 - core)):
                at = row + 2 * blocks * half
                here = pltpu.roll(whole[i, pl.ds(at, rows), :], 128 - turn, 1)
                after = pltpu.roll(whole[i, pl.ds(at + 1, rows), :], 128 - turn, 1)
                out[i] = (jnp.where(spill, after, here) * on).astype(jnp.bfloat16)


def make_series(offset, active, told, near, far, blocks, rows):
    window = jax.ShapeDtypeStruct((6, rows, 128), jnp.bfloat16)
    vmem = pl.BlockSpec(memory_space=pltpu.VMEM)
    return pl.pallas_call(
        functools.partial(series_kernel, blocks),
        out_shape=(window, window),
        in_specs=[pl.BlockSpec(memory_space=pltpu.SMEM)] * 2 + [vmem] * 3,
        out_specs=(vmem, vmem),
        scratch_shapes=[pltpu.VMEM((6, 2 * blocks + rows + 8, 128), jnp.float32)],
        compiler_params=pltpu.CompilerParams(vmem_limit_bytes=4 << 20),
        name="series",
    )(offset, active, told, near, far)


def correlate_kernel(span, nb, t0, t1, t2, t3, mine, mate, masks, first_ref, second_ref,
                     tp_ref, xb_ref, xf_ref, a_ref, z_ref, d_ref, acc_ref, tot_ref, tr_ref, sems):
    lb = span // 128
    kb = lb + 1
    rows = xf_ref.shape[1]
    loop_at = lax.axis_index("loop")
    half = loop_at // 2
    copies = []
    for s, t in enumerate((t0, t1, t2, t3)):
        x = (mine, mate)[s % 2].at[pl.ds(3 * (s // 2), 3)]
        t = t.at[:, :, pl.ds(0, span)]
        copies.append(pltpu.make_async_copy(t, tp_ref.at[pl.ds(3 * s, 3), :, pl.ds(128, span)], sems.at[2 * s]))
        copies.append(pltpu.make_async_copy(x, xb_ref.at[pl.ds(3 * s, 3)], sems.at[2 * s + 1]))
    for copy in copies:
        copy.start()
    tp_ref[:, :, 0:128] = jnp.zeros((12, ROWS, 128), jnp.bfloat16)
    tp_ref[:, :, 128 + span :] = jnp.zeros((12, ROWS, 128), jnp.bfloat16)
    tot_ref[...] = jnp.zeros(tot_ref.shape, jnp.float32)
    k_first = 2 * ROWS * lax.axis_index("tgrp") + ROWS * half
    lane = lanes((8, 128))
    sub = lax.broadcasted_iota(jnp.int32, (8, 128), 0)
    counts = jnp.sum(masks[...], axis=0, keepdims=True).astype(jnp.float32)
    weight = jnp.sqrt(3.0 * span / counts)
    own = k_first + lane % ROWS
    diagonal = lanes((ROWS, 128)) % ROWS == lax.broadcasted_iota(jnp.int32, (ROWS, 128), 0)
    lane_r = lanes((rows, 128))
    for copy in copies:
        copy.wait()

    def row_scale(s):
        norm = jnp.zeros((ROWS, 128), jnp.float32)
        for c in range(3):
            for b in range(lb):
                wide = tp_ref[3 * s + c, :, 128 * b + 128 : 128 * b + 256].astype(jnp.float32)
                norm = norm + wide * wide
        inverse = 1.0 / jnp.sqrt(jnp.sum(norm, axis=1, keepdims=True) / (3.0 * span) + epsilon)
        inverse = jnp.where(diagonal, jnp.broadcast_to(inverse, (ROWS, 128)), 0.0)
        inverse = jnp.sum(inverse, axis=0, keepdims=True)
        here = masks[pl.ds(loop_at ^ s, 1), :].astype(jnp.float32) * weight
        here = jnp.take_along_axis(jnp.broadcast_to(here, (8, 128)), own, axis=1)
        return here[0:1] * inverse / (3.0 * span)

    def data_scale(s):
        squares = jnp.zeros((rows, 128), jnp.float32)
        for c in range(3):
            x = xb_ref[3 * s + c].astype(jnp.float32)
            squares = squares + x * x
        b = 1
        while b < 128:
            after = pltpu.roll(squares, rows - 1, 0)
            squares = squares + pltpu.roll(jnp.where(lane_r < b, after, squares), 128 - b, 1)
            b *= 2
        b = 1
        while b < lb:
            squares = squares + pltpu.roll(squares, rows - b, 0)
            b *= 2
        d_ref[...] = 1.0 / jnp.sqrt(squares / (3.0 * span) + epsilon)

    from_lane = (lane + sub) % 128
    inside = lane + sub < 128

    def build(i, slot):
        for r in range(SHIFTS):
            n = ROWS * (8 * (r % 2) + r // 2)
            a_ref[slot, n : n + ROWS, :] = tp_ref[i, :, 128 - 8 * r : 128 - 8 * r + 128 * kb]

        xf_ref[slot] = xb_ref[i].astype(jnp.float32)

        def turned(j):
            row = xf_ref[slot, pl.ds(j, 8, stride=0), :]
            return jnp.take_along_axis(row, from_lane, axis=1)

        before, tiles = turned(0), []
        for j in range(2 * nb + lb):
            after = turned(j + 1)
            tiles.append(jnp.where(inside, before, after))
            before = after
            if j >= nb:
                z_ref[slot, j - nb] = jnp.concatenate([tiles[j - nb], tiles[j]], axis=0).astype(jnp.bfloat16)

    def product(slot):
        left = jnp.concatenate([z_ref[slot, b : b + nb].reshape(16 * nb, 128) for b in range(kb)], axis=1)
        return lax.dot_general(left, a_ref[slot], (((1,), (1,)), ((), ())), preferred_element_type=jnp.float32)

    def weighted(rs):
        for v in (0, 1):
            index = 16 * (lane // 16) + 8 * v + sub
            for j in range(nb):
                for h in (0, 1):
                    at = 16 * j + 8 * h
                    scale = jnp.take_along_axis(d_ref[pl.ds(j + nb * h, 8, stride=0), :], index, axis=1) * rs
                    tot_ref[v, at : at + 8, :] += acc_ref[at : at + 8, 128 * v : 128 * v + 128] * scale

    build(0, 0)

    def station(s, carry):
        for c in range(3):
            m = product(c)
            build(jnp.minimum(3 * s + c + 1, 11), (c + 1) % 3)
            if c == 0:
                acc_ref[...] = m
            else:
                acc_ref[...] += m
            if c == 0:
                rs = row_scale(s)
            if c == 1:
                data_scale(s)
        weighted(rs)
        return carry

    lax.fori_loop(0, 4, station, 0)

    for f, out in enumerate((first_ref, second_ref)):
        h = half ^ f
        for jb in range(nb // 8):
            v = [[tot_ref[q, pl.ds(128 * jb + 8 * h + p, 8, stride=16), :] for p in range(8)] for q in (0, 1)]
            for b in (1, 2, 4):
                upper = (lane // b) % 2 == 1
                for q in (0, 1):
                    for p in range(8):
                        if not p & b:
                            x, y = v[q][p], v[q][p + b]
                            v[q][p] = jnp.where(upper, pltpu.roll(y, b, 1), x)
                            v[q][p + b] = jnp.where(upper, y, pltpu.roll(x, 128 - b, 1))
            upper = (lane // 8) % 2 == 1
            for p in range(8):
                x, y = v[0][p], v[1][p]
                v[0][p] = jnp.where(upper, pltpu.roll(y, 8, 1), x)
                v[1][p] = jnp.where(upper, y, pltpu.roll(x, 120, 1))
            for q in (0, 1):
                for p in range(8):
                    at = nb * (8 * q + p) + 8 * jb
                    tr_ref[f, at : at + 8, :] = v[q][p]
        levels = [jnp.zeros((8, 128), jnp.float32)] * 2
        for j in range(nb):
            codes = []
            for q in (0, 1):
                value = tr_ref[f, pl.ds(8 * nb * q + j, 8, stride=nb), :]
                top = jnp.maximum(jnp.max(jnp.abs(value), axis=1, keepdims=True), 2e-33)
                level = jnp.ceil(jnp.log2(jnp.broadcast_to(top, (8, 128))) * LEVELS)
                levels[q] = jnp.where(lane == j, level, levels[q])
                codes.append(jnp.round(value * (STEPS * jnp.exp2(level * (-1.0 / LEVELS)))))
            out[:, 128 * j : 128 * j + 128] = jnp.concatenate(codes, axis=0).astype(jnp.int32).astype(jnp.int16)
        out[:, 128 * nb :] = jnp.concatenate(levels, axis=0).astype(jnp.int32).astype(jnp.int16)


def decode_kernel(a_ref, b_ref, out_ref):
    odd = lax.axis_index("tgrp") % 2
    nb = out_ref.shape[1] // 128
    for ref, half in ((a_ref, odd), (b_ref, 1 - odd)):
        at = pl.multiple_of(ROWS * half, ROWS)
        step = jnp.exp2(ref[:, 128 * nb :].astype(jnp.float32) * (1.0 / LEVELS)) * (1.0 / STEPS)
        for j in range(nb):
            value = ref[:, 128 * j : 128 * j + 128].astype(jnp.float32)
            out_ref[pl.ds(at, ROWS), 128 * j : 128 * j + 128] = value * step[:, j : j + 1]


def decode(first, second):
    vmem = pl.BlockSpec(memory_space=pltpu.VMEM)
    return pl.pallas_call(
        decode_kernel,
        out_shape=jax.ShapeDtypeStruct((2 * ROWS, first.shape[1] - 128), jnp.float32),
        in_specs=[vmem, vmem],
        out_specs=vmem,
        compiler_params=pltpu.CompilerParams(vmem_limit_bytes=4 << 20),
        name="decode",
    )(first, second)


def correlate_stations(panels, series, masks, span, nb):
    lb = span // 128
    rows = series[0].shape[1]
    block = jax.ShapeDtypeStruct((ROWS, 128 * nb + 128), jnp.int16)
    vmem = pl.BlockSpec(memory_space=pltpu.VMEM)
    return pl.pallas_call(
        functools.partial(correlate_kernel, span, nb),
        out_shape=(block, block),
        in_specs=[pl.BlockSpec(memory_space=pl.ANY)] * 6 + [vmem],
        out_specs=(vmem, vmem),
        scratch_shapes=[
            pltpu.VMEM((12, ROWS, span + 256), jnp.bfloat16),
            pltpu.VMEM((12, rows, 128), jnp.bfloat16),
            pltpu.VMEM((3, rows, 128), jnp.float32),
            pltpu.VMEM((3, ROWS * SHIFTS, span + 128), jnp.bfloat16),
            pltpu.VMEM((3, nb + lb, 16, 128), jnp.bfloat16),
            pltpu.VMEM((rows, 128), jnp.float32),
            pltpu.VMEM((16 * nb, 256), jnp.float32),
            pltpu.VMEM((2, 16 * nb, 128), jnp.float32),
            pltpu.VMEM((2, 16 * nb, 128), jnp.float32),
            pltpu.SemaphoreType.DMA((8,)),
        ],
        compiler_params=pltpu.CompilerParams(vmem_limit_bytes=24 << 20),
        name="correlate",
    )(*panels, *series, masks)


def swapped(value, loop_bits, tgrp_bits):
    pairs = [(4 * l + z, 4 * (l ^ loop_bits) + (z ^ tgrp_bits)) for l in range(4) for z in range(4)]
    return lax.ppermute(value, ("loop", "tgrp"), pairs)


def to_owner(value, flip):
    pairs = [(4 * l + z, 4 * z + 2 * (l % 2) + ((l // 2) ^ flip)) for l in range(4) for z in range(4)]
    return lax.ppermute(value, ("loop", "tgrp"), pairs)


def local_plane(data, templates, masks, offsets, active):
    span = templates.shape[3]
    nb = data.shape[2] // 128
    panel = templates[:, 0].transpose(1, 0, 2)
    keep, send = split(offsets, active, panel)
    panel_y = swapped(send, 2, 0)
    panel_c = swapped(keep, 1, 0)
    pieces = data.reshape(3 * nb, 128)
    pair = jnp.concatenate([pieces, swapped(pieces, 2, 0)], axis=0)
    near = jnp.concatenate([pair, swapped(pair, 0, 1)], axis=0)
    far = swapped(near, 0, 2)
    mine, mate = make_series(offsets, active, panel_y, near, far, nb, 2 * nb + span // 128 + 8)
    mate = swapped(mate, 1, 0)
    panel_late, _ = lax.optimization_barrier((panel_y, far))
    panel_yc = swapped(panel_late, 1, 0)
    first, second = correlate_stations(
        (keep, panel_c, panel_y, panel_yc), (mine, mate), masks.T, span, nb
    )
    return decode(to_owner(first, 0), to_owner(second, 1))


def solution(mesh):
    placed = (
        P(("parts", "loop"), None, "tgrp"),
        P("tgrp", "loop", None, None),
        P(),
        P(("parts", "loop")),
        P(("parts", "loop"), None),
    )

    def local(data, templates, masks, offsets, active):
        grid = (mesh.shape["loop"], mesh.shape["tgrp"])
        fits = grid == (4, 4) and templates.shape[:2] == (2 * ROWS, 1) and masks.shape[0] == 128
        fits = fits and templates.shape[3] == 2048 and data.shape[0] == 1 and data.shape[2] % 1024 == 0
        plan = local_plane if fits else local_general
        return plan(data, templates, masks, offsets, active)

    return jax.shard_map(
        local, mesh=mesh, in_specs=placed, out_specs=P(("parts", "loop"), "tgrp"), check_vma=False
    )
```

```python
import functools

import jax
import jax.numpy as jnp
from jax import lax
from jax.experimental import pallas as pl
from jax.experimental.pallas import tpu as pltpu
from jax.sharding import PartitionSpec as P

L = 2048


epsilon = 1e-05


def passed_along(value, axis, steps):
    count = lax.axis_size(axis)
    initial, last = (max(0, -steps), min(count, count - steps))
    return lax.ppermute(value, axis, [(source, source + steps) for source in range(initial, last)])


def window_energy(squares, out_len, span):
    inner_len = out_len + span - 128
    nblocks = (inner_len + 127) // 128
    total_len = 128 * (nblocks + 1)
    padded = jnp.concatenate([squares, jnp.zeros((total_len - squares.shape[0],), squares.dtype)])
    first = padded[: 128 * nblocks].reshape(nblocks, 128)
    second = padded[128 : 128 * nblocks + 128].reshape(nblocks, 128)
    segments = jnp.concatenate([first, second], axis=1)
    rows_at = lax.broadcasted_iota(jnp.int32, (256, 128), 0)
    cols_at = lax.broadcasted_iota(jnp.int32, (256, 128), 1)
    gap = rows_at - cols_at
    band = jnp.where((gap >= 0) & (gap < 128), 1.0, 0.0).astype(squares.dtype)
    inner = jnp.dot(segments, band, precision=lax.Precision.HIGHEST).reshape(nblocks * 128)
    energy = jnp.zeros((out_len,), squares.dtype)
    for block_at in range(span // 128):
        energy = energy + inner[128 * block_at : 128 * block_at + out_len]
    return energy


def correlate(panel, window, out_len):
    row_count = panel.shape[0]
    blocks = panel.shape[2] // 128
    span_len = out_len + panel.shape[2] - 128
    unfold = jnp.stack(
        [window[:, shift_by : shift_by + span_len] for shift_by in range(128)], axis=1
    )
    unfold = unfold.reshape(3 * 128, span_len)
    frames = (
        panel.reshape(row_count, 3, blocks, 128)
        .transpose(0, 2, 1, 3)
        .reshape(row_count, blocks, 3 * 128)
    )

    def add_block(block_at, running_sum):
        start_at = (block_at * 128).astype(jnp.int32)
        columns = lax.dynamic_slice_in_dim(unfold, start_at, out_len, 1)
        weights_now = lax.dynamic_index_in_dim(frames, block_at, 1, keepdims=False)
        return running_sum + jnp.dot(weights_now, columns, preferred_element_type=jnp.float32)

    return lax.fori_loop(0, blocks, add_block, jnp.zeros((row_count, out_len), jnp.float32))


def local_general(data, templates, masks, offsets, active):
    local_count = data.shape[0]
    block_len = data.shape[2]
    following = passed_along(data, "tgrp", -1)
    extended = jnp.concatenate([data, following], axis=2)
    loop_at = lax.axis_index("loop")
    first_station = loop_at * local_count
    counts = jnp.sum(masks, axis=1).astype(jnp.float32)
    local_masks = lax.dynamic_slice_in_dim(masks, first_station, local_count, 1)
    weights = local_masks.astype(jnp.float32) * jnp.sqrt(3.0 * L / counts)[:, None]
    station = 0
    channel_on = active[station].astype(jnp.bfloat16)
    series = lax.dynamic_slice(
        extended[station], (jnp.int32(0), offsets[station]), (3, block_len + L)
    )
    window = series * channel_on[:, None]
    wide_window = window.astype(jnp.float32)
    squares = jnp.sum(wide_window * wide_window, axis=0)
    energy = window_energy(squares, block_len, L)
    inv_datas = [1.0 / jnp.sqrt(energy / (3.0 * L) + epsilon)]
    windows = [window]
    channel_sets = [channel_on]
    panel_rows = lax.all_gather(templates, "tgrp", axis=0, tiled=True)
    station = 0
    panel = panel_rows[:, station] * channel_sets[station][None, :, None]
    wide_panel = panel.astype(jnp.float32)
    inv_template = 1.0 / jnp.sqrt(
        jnp.sum(wide_panel * wide_panel, axis=(1, 2)) / (3.0 * L) + epsilon
    )
    corr = correlate(panel, windows[station], block_len)
    row_weights = weights[:, station]
    row_scale = inv_template * row_weights
    stacked = corr * inv_datas[station][None, :] * row_scale[:, None] / (3.0 * L)
    rows_here = stacked.shape[0] // lax.axis_size("loop")
    summed = lax.psum(stacked, "loop")
    return lax.dynamic_slice_in_dim(summed, loop_at * rows_here, rows_here, 0)


ROWS = 16
SHIFTS = 16
STEPS = 32700.0
LEVELS = 64.0


def lanes(shape):
    return lax.broadcasted_iota(jnp.int32, shape, len(shape) - 1)


def split_kernel(offset_in, active_in, t_in, keep_ref, send_ref, offset, active, t_ref, sems):
    copies = [
        pltpu.make_async_copy(t_in, t_ref, sems.at[0]),
        pltpu.make_async_copy(offset_in, offset, sems.at[1]),
        pltpu.make_async_copy(active_in, active, sems.at[2]),
    ]
    for copy in copies:
        copy.start()
    for copy in copies:
        copy.wait()
    half = lax.axis_index("loop") // 2
    span = t_ref.shape[2]
    sub = lax.broadcasted_iota(jnp.int32, (ROWS, 128), 0)
    high, low = (offset[0] // 32).astype(jnp.float32), (offset[0] % 32).astype(jnp.float32)
    for c in range(3):
        on = active[0, c].astype(jnp.float32)
        told = jnp.where(sub == 0, high, jnp.where(sub == 1, low, jnp.where(sub == 2, on, 0.0)))
        for out, first in ((keep_ref, half), (send_ref, 1 - half)):
            rows = t_ref[c, pl.ds(pl.multiple_of(ROWS * first, ROWS), ROWS), :]
            out[c, :, :span] = (rows.astype(jnp.float32) * on).astype(jnp.bfloat16)
            out[c, :, span:] = told.astype(jnp.bfloat16)


def split(offset, active, panel):
    half = jax.ShapeDtypeStruct((3, ROWS, panel.shape[2] + 128), jnp.bfloat16)
    return pl.pallas_call(
        split_kernel,
        out_shape=(half, half),
        in_specs=[pl.BlockSpec(memory_space=pltpu.HBM)] * 3,
        out_specs=(pl.BlockSpec(memory_space=pltpu.VMEM),) * 2,
        scratch_shapes=[
            pltpu.SMEM(offset.shape, jnp.int32),
            pltpu.SMEM(active.shape, jnp.int32),
            pltpu.VMEM(panel.shape, jnp.bfloat16),
            pltpu.SemaphoreType.DMA((3,)),
        ],
        compiler_params=pltpu.CompilerParams(vmem_limit_bytes=4 << 20),
        name="split",
    )(offset, active, panel)


def series_kernel(blocks, own, told, near, far, mine_ref, mate_ref, whole):
    z = lax.axis_index("tgrp")
    core = lax.axis_index("loop") % 2
    rows = mine_ref.shape[1]
    span = told.shape[2] - 128
    lane = lanes((rows, 128))
    whole[:, 4 * blocks :] = jnp.zeros((6, whole.shape[1] - 4 * blocks, 128), jnp.float32)
    wide = [near[...].astype(jnp.float32), far[...].astype(jnp.float32)]
    for b in range(4):
        at = pl.multiple_of(blocks * (z ^ b), 8)
        for i in range(6):
            first = 6 * blocks * (b % 2) + i * blocks
            whole[i, pl.ds(at, blocks), :] = wide[b // 2][first : first + blocks]
    for station in range(2):
        words = (own, told)[station]
        first = words[0, :, span:].astype(jnp.float32)
        shift = (32.0 * jnp.max(first[0:1]) + jnp.max(first[1:2])).astype(jnp.int32)
        row, turn = shift // 128, shift % 128
        spill = lane >= 128 - turn
        for c in range(3):
            i = 3 * station + c
            on = words[c, :, span:].astype(jnp.float32)[2:3]
            for out, half in ((mine_ref, core), (mate_ref, 1 - core)):
                at = row + 2 * blocks * half
                here = pltpu.roll(whole[i, pl.ds(at, rows), :], 128 - turn, 1)
                after = pltpu.roll(whole[i, pl.ds(at + 1, rows), :], 128 - turn, 1)
                out[i] = (jnp.where(spill, after, here) * on).astype(jnp.bfloat16)


def make_series(own, told, near, far, blocks, rows):
    window = jax.ShapeDtypeStruct((6, rows, 128), jnp.bfloat16)
    vmem = pl.BlockSpec(memory_space=pltpu.VMEM)
    return pl.pallas_call(
        functools.partial(series_kernel, blocks),
        out_shape=(window, window),
        in_specs=[vmem] * 4,
        out_specs=(vmem, vmem),
        scratch_shapes=[pltpu.VMEM((6, 2 * blocks + rows + 8, 128), jnp.float32)],
        compiler_params=pltpu.CompilerParams(vmem_limit_bytes=4 << 20),
        name="series",
    )(own, told, near, far)


def correlate_kernel(span, nb, t0, t1, t2, t3, mine, mate, masks, first_ref, second_ref,
                     tp_ref, xb_ref, xf_ref, a_ref, z_ref, d_ref, acc_ref, tot_ref, tr_ref, sems):
    lb = span // 128
    kb = lb + 1
    rows = xf_ref.shape[1]
    loop_at = lax.axis_index("loop")
    half = loop_at // 2
    copies = []
    for s, t in enumerate((t0, t1, t2, t3)):
        x = (mine, mate)[s % 2].at[pl.ds(3 * (s // 2), 3)]
        t = t.at[:, :, pl.ds(0, span)]
        copies.append(pltpu.make_async_copy(t, tp_ref.at[pl.ds(3 * s, 3), :, pl.ds(128, span)], sems.at[2 * s]))
        copies.append(pltpu.make_async_copy(x, xb_ref.at[pl.ds(3 * s, 3)], sems.at[2 * s + 1]))
    for copy in copies:
        copy.start()
    tp_ref[:, :, 0:128] = jnp.zeros((12, ROWS, 128), jnp.bfloat16)
    tp_ref[:, :, 128 + span :] = jnp.zeros((12, ROWS, 128), jnp.bfloat16)
    tot_ref[...] = jnp.zeros(tot_ref.shape, jnp.float32)
    k_first = 2 * ROWS * lax.axis_index("tgrp") + ROWS * half
    lane = lanes((8, 128))
    sub = lax.broadcasted_iota(jnp.int32, (8, 128), 0)
    counts = jnp.sum(masks[...], axis=0, keepdims=True).astype(jnp.float32)
    weight = jnp.sqrt(3.0 * span / counts)
    own = k_first + lane % ROWS
    diagonal = lanes((ROWS, 128)) % ROWS == lax.broadcasted_iota(jnp.int32, (ROWS, 128), 0)
    lane_r = lanes((rows, 128))
    for copy in copies:
        copy.wait()

    def row_scale(s):
        norm = jnp.zeros((ROWS, 128), jnp.float32)
        for c in range(3):
            for b in range(lb):
                wide = tp_ref[3 * s + c, :, 128 * b + 128 : 128 * b + 256].astype(jnp.float32)
                norm = norm + wide * wide
        inverse = 1.0 / jnp.sqrt(jnp.sum(norm, axis=1, keepdims=True) / (3.0 * span) + epsilon)
        inverse = jnp.where(diagonal, jnp.broadcast_to(inverse, (ROWS, 128)), 0.0)
        inverse = jnp.sum(inverse, axis=0, keepdims=True)
        here = masks[pl.ds(loop_at ^ s, 1), :].astype(jnp.float32) * weight
        here = jnp.take_along_axis(jnp.broadcast_to(here, (8, 128)), own, axis=1)
        return here[0:1] * inverse / (3.0 * span)

    def data_scale(s):
        squares = jnp.zeros((rows, 128), jnp.float32)
        for c in range(3):
            x = xb_ref[3 * s + c].astype(jnp.float32)
            squares = squares + x * x
        b = 1
        while b < 128:
            after = pltpu.roll(squares, rows - 1, 0)
            squares = squares + pltpu.roll(jnp.where(lane_r < b, after, squares), 128 - b, 1)
            b *= 2
        b = 1
        while b < lb:
            squares = squares + pltpu.roll(squares, rows - b, 0)
            b *= 2
        d_ref[...] = 1.0 / jnp.sqrt(squares / (3.0 * span) + epsilon)

    from_lane = (lane + sub) % 128
    inside = lane + sub < 128

    def build(i, slot):
        for r in range(SHIFTS):
            n = ROWS * (8 * (r % 2) + r // 2)
            a_ref[slot, n : n + ROWS, :] = tp_ref[i, :, 128 - 8 * r : 128 - 8 * r + 128 * kb]

        xf_ref[slot] = xb_ref[i].astype(jnp.float32)

        def turned(j):
            row = xf_ref[slot, pl.ds(j, 8, stride=0), :]
            return jnp.take_along_axis(row, from_lane, axis=1)

        before, tiles = turned(0), []
        for j in range(2 * nb + lb):
            after = turned(j + 1)
            tiles.append(jnp.where(inside, before, after))
            before = after
            if j >= nb:
                z_ref[slot, j - nb] = jnp.concatenate([tiles[j - nb], tiles[j]], axis=0).astype(jnp.bfloat16)

    def product(slot):
        left = jnp.concatenate([z_ref[slot, b : b + nb].reshape(16 * nb, 128) for b in range(kb)], axis=1)
        return lax.dot_general(left, a_ref[slot], (((1,), (1,)), ((), ())), preferred_element_type=jnp.float32)

    def weighted(rs):
        for v in (0, 1):
            index = 16 * (lane // 16) + 8 * v + sub
            for j in range(nb):
                for h in (0, 1):
                    at = 16 * j + 8 * h
                    scale = jnp.take_along_axis(d_ref[pl.ds(j + nb * h, 8, stride=0), :], index, axis=1) * rs
                    tot_ref[v, at : at + 8, :] += acc_ref[at : at + 8, 128 * v : 128 * v + 128] * scale

    build(0, 0)

    def station(s, carry):
        for c in range(3):
            m = product(c)
            build(jnp.minimum(3 * s + c + 1, 11), (c + 1) % 3)
            if c == 0:
                acc_ref[...] = m
            else:
                acc_ref[...] += m
            if c == 0:
                rs = row_scale(s)
            if c == 1:
                data_scale(s)
        weighted(rs)
        return carry

    lax.fori_loop(0, 4, station, 0)

    for f, out in enumerate((first_ref, second_ref)):
        h = half ^ f
        for jb in range(nb // 8):
            v = [[tot_ref[q, pl.ds(128 * jb + 8 * h + p, 8, stride=16), :] for p in range(8)] for q in (0, 1)]
            for b in (1, 2, 4):
                upper = (lane // b) % 2 == 1
                for q in (0, 1):
                    for p in range(8):
                        if not p & b:
                            x, y = v[q][p], v[q][p + b]
                            v[q][p] = jnp.where(upper, pltpu.roll(y, b, 1), x)
                            v[q][p + b] = jnp.where(upper, y, pltpu.roll(x, 128 - b, 1))
            upper = (lane // 8) % 2 == 1
            for p in range(8):
                x, y = v[0][p], v[1][p]
                v[0][p] = jnp.where(upper, pltpu.roll(y, 8, 1), x)
                v[1][p] = jnp.where(upper, y, pltpu.roll(x, 120, 1))
            for q in (0, 1):
                for p in range(8):
                    at = nb * (8 * q + p) + 8 * jb
                    tr_ref[f, at : at + 8, :] = v[q][p]
        levels = [jnp.zeros((8, 128), jnp.float32)] * 2
        for j in range(nb):
            codes = []
            for q in (0, 1):
                value = tr_ref[f, pl.ds(8 * nb * q + j, 8, stride=nb), :]
                top = jnp.maximum(jnp.max(jnp.abs(value), axis=1, keepdims=True), 2e-33)
                level = jnp.ceil(jnp.log2(jnp.broadcast_to(top, (8, 128))) * LEVELS)
                levels[q] = jnp.where(lane == j, level, levels[q])
                codes.append(jnp.round(value * (STEPS * jnp.exp2(level * (-1.0 / LEVELS)))))
            out[:, 128 * j : 128 * j + 128] = jnp.concatenate(codes, axis=0).astype(jnp.int32).astype(jnp.int16)
        out[:, 128 * nb :] = jnp.concatenate(levels, axis=0).astype(jnp.int32).astype(jnp.int16)


def decode_kernel(a_ref, b_ref, out_ref):
    odd = lax.axis_index("tgrp") % 2
    nb = out_ref.shape[1] // 128
    for ref, half in ((a_ref, odd), (b_ref, 1 - odd)):
        at = pl.multiple_of(ROWS * half, ROWS)
        step = jnp.exp2(ref[:, 128 * nb :].astype(jnp.float32) * (1.0 / LEVELS)) * (1.0 / STEPS)
        for j in range(nb):
            value = ref[:, 128 * j : 128 * j + 128].astype(jnp.float32)
            out_ref[pl.ds(at, ROWS), 128 * j : 128 * j + 128] = value * step[:, j : j + 1]


def decode(first, second):
    vmem = pl.BlockSpec(memory_space=pltpu.VMEM)
    return pl.pallas_call(
        decode_kernel,
        out_shape=jax.ShapeDtypeStruct((2 * ROWS, first.shape[1] - 128), jnp.float32),
        in_specs=[vmem, vmem],
        out_specs=vmem,
        compiler_params=pltpu.CompilerParams(vmem_limit_bytes=4 << 20),
        name="decode",
    )(first, second)


def correlate_stations(panels, series, masks, span, nb):
    lb = span // 128
    rows = series[0].shape[1]
    block = jax.ShapeDtypeStruct((ROWS, 128 * nb + 128), jnp.int16)
    vmem = pl.BlockSpec(memory_space=pltpu.VMEM)
    return pl.pallas_call(
        functools.partial(correlate_kernel, span, nb),
        out_shape=(block, block),
        in_specs=[pl.BlockSpec(memory_space=pl.ANY)] * 6 + [vmem],
        out_specs=(vmem, vmem),
        scratch_shapes=[
            pltpu.VMEM((12, ROWS, span + 256), jnp.bfloat16),
            pltpu.VMEM((12, rows, 128), jnp.bfloat16),
            pltpu.VMEM((3, rows, 128), jnp.float32),
            pltpu.VMEM((3, ROWS * SHIFTS, span + 128), jnp.bfloat16),
            pltpu.VMEM((3, nb + lb, 16, 128), jnp.bfloat16),
            pltpu.VMEM((rows, 128), jnp.float32),
            pltpu.VMEM((16 * nb, 256), jnp.float32),
            pltpu.VMEM((2, 16 * nb, 128), jnp.float32),
            pltpu.VMEM((2, 16 * nb, 128), jnp.float32),
            pltpu.SemaphoreType.DMA((8,)),
        ],
        compiler_params=pltpu.CompilerParams(vmem_limit_bytes=24 << 20),
        name="correlate",
    )(*panels, *series, masks)


def swapped(value, loop_bits, tgrp_bits):
    pairs = [(4 * l + z, 4 * (l ^ loop_bits) + (z ^ tgrp_bits)) for l in range(4) for z in range(4)]
    return lax.ppermute(value, ("loop", "tgrp"), pairs)


def to_owner(value, flip):
    pairs = [(4 * l + z, 4 * z + 2 * (l % 2) + ((l // 2) ^ flip)) for l in range(4) for z in range(4)]
    return lax.ppermute(value, ("loop", "tgrp"), pairs)


def local_plane(data, templates, masks, offsets, active):
    span = templates.shape[3]
    nb = data.shape[2] // 128
    panel = templates[:, 0].transpose(1, 0, 2)
    pieces = data.reshape(3 * nb, 128)
    pair = jnp.concatenate([pieces, swapped(pieces, 2, 0)], axis=0)
    panel, _ = lax.optimization_barrier((panel, pair))
    keep, send = split(offsets, active, panel)
    panel_c = swapped(keep, 1, 0)
    near = jnp.concatenate([pair, swapped(pair, 0, 1)], axis=0)
    far = swapped(near, 0, 2)
    send, _ = lax.optimization_barrier((send, near))
    panel_y = swapped(send, 2, 0)
    mine, mate = make_series(keep, panel_y, near, far, nb, 2 * nb + span // 128 + 8)
    mate = swapped(mate, 1, 0)
    panel_late, _ = lax.optimization_barrier((panel_y, far))
    panel_yc = swapped(panel_late, 1, 0)
    first, second = correlate_stations(
        (keep, panel_c, panel_y, panel_yc), (mine, mate), masks.T, span, nb
    )
    return decode(to_owner(first, 0), to_owner(second, 1))


def solution(mesh):
    placed = (
        P(("parts", "loop"), None, "tgrp"),
        P("tgrp", "loop", None, None),
        P(),
        P(("parts", "loop")),
        P(("parts", "loop"), None),
    )

    def local(data, templates, masks, offsets, active):
        grid = (mesh.shape["loop"], mesh.shape["tgrp"])
        fits = grid == (4, 4) and templates.shape[:2] == (2 * ROWS, 1) and masks.shape[0] == 128
        fits = fits and templates.shape[3] == 2048 and data.shape[0] == 1 and data.shape[2] % 1024 == 0
        plan = local_plane if fits else local_general
        return plan(data, templates, masks, offsets, active)

    return jax.shard_map(
        local, mesh=mesh, in_specs=placed, out_specs=P(("parts", "loop"), "tgrp"), check_vma=False
    )
```

```python
import functools

import jax
import jax.numpy as jnp
from jax import lax
from jax.experimental import pallas as pl
from jax.experimental.pallas import tpu as pltpu
from jax.sharding import PartitionSpec as P

L = 2048


epsilon = 1e-05


def passed_along(value, axis, steps):
    count = lax.axis_size(axis)
    initial, last = (max(0, -steps), min(count, count - steps))
    return lax.ppermute(value, axis, [(source, source + steps) for source in range(initial, last)])


def window_energy(squares, out_len, span):
    inner_len = out_len + span - 128
    nblocks = (inner_len + 127) // 128
    total_len = 128 * (nblocks + 1)
    padded = jnp.concatenate([squares, jnp.zeros((total_len - squares.shape[0],), squares.dtype)])
    first = padded[: 128 * nblocks].reshape(nblocks, 128)
    second = padded[128 : 128 * nblocks + 128].reshape(nblocks, 128)
    segments = jnp.concatenate([first, second], axis=1)
    rows_at = lax.broadcasted_iota(jnp.int32, (256, 128), 0)
    cols_at = lax.broadcasted_iota(jnp.int32, (256, 128), 1)
    gap = rows_at - cols_at
    band = jnp.where((gap >= 0) & (gap < 128), 1.0, 0.0).astype(squares.dtype)
    inner = jnp.dot(segments, band, precision=lax.Precision.HIGHEST).reshape(nblocks * 128)
    energy = jnp.zeros((out_len,), squares.dtype)
    for block_at in range(span // 128):
        energy = energy + inner[128 * block_at : 128 * block_at + out_len]
    return energy


def correlate(panel, window, out_len):
    row_count = panel.shape[0]
    blocks = panel.shape[2] // 128
    span_len = out_len + panel.shape[2] - 128
    unfold = jnp.stack(
        [window[:, shift_by : shift_by + span_len] for shift_by in range(128)], axis=1
    )
    unfold = unfold.reshape(3 * 128, span_len)
    frames = (
        panel.reshape(row_count, 3, blocks, 128)
        .transpose(0, 2, 1, 3)
        .reshape(row_count, blocks, 3 * 128)
    )

    def add_block(block_at, running_sum):
        start_at = (block_at * 128).astype(jnp.int32)
        columns = lax.dynamic_slice_in_dim(unfold, start_at, out_len, 1)
        weights_now = lax.dynamic_index_in_dim(frames, block_at, 1, keepdims=False)
        return running_sum + jnp.dot(weights_now, columns, preferred_element_type=jnp.float32)

    return lax.fori_loop(0, blocks, add_block, jnp.zeros((row_count, out_len), jnp.float32))


def local_general(data, templates, masks, offsets, active):
    local_count = data.shape[0]
    block_len = data.shape[2]
    following = passed_along(data, "tgrp", -1)
    extended = jnp.concatenate([data, following], axis=2)
    loop_at = lax.axis_index("loop")
    first_station = loop_at * local_count
    counts = jnp.sum(masks, axis=1).astype(jnp.float32)
    local_masks = lax.dynamic_slice_in_dim(masks, first_station, local_count, 1)
    weights = local_masks.astype(jnp.float32) * jnp.sqrt(3.0 * L / counts)[:, None]
    station = 0
    channel_on = active[station].astype(jnp.bfloat16)
    series = lax.dynamic_slice(
        extended[station], (jnp.int32(0), offsets[station]), (3, block_len + L)
    )
    window = series * channel_on[:, None]
    wide_window = window.astype(jnp.float32)
    squares = jnp.sum(wide_window * wide_window, axis=0)
    energy = window_energy(squares, block_len, L)
    inv_datas = [1.0 / jnp.sqrt(energy / (3.0 * L) + epsilon)]
    windows = [window]
    channel_sets = [channel_on]
    panel_rows = lax.all_gather(templates, "tgrp", axis=0, tiled=True)
    station = 0
    panel = panel_rows[:, station] * channel_sets[station][None, :, None]
    wide_panel = panel.astype(jnp.float32)
    inv_template = 1.0 / jnp.sqrt(
        jnp.sum(wide_panel * wide_panel, axis=(1, 2)) / (3.0 * L) + epsilon
    )
    corr = correlate(panel, windows[station], block_len)
    row_weights = weights[:, station]
    row_scale = inv_template * row_weights
    stacked = corr * inv_datas[station][None, :] * row_scale[:, None] / (3.0 * L)
    rows_here = stacked.shape[0] // lax.axis_size("loop")
    summed = lax.psum(stacked, "loop")
    return lax.dynamic_slice_in_dim(summed, loop_at * rows_here, rows_here, 0)


ROWS = 16
SHIFTS = 16
STEPS = 32700.0
LEVELS = 64.0


def lanes(shape):
    return lax.broadcasted_iota(jnp.int32, shape, len(shape) - 1)


def split_kernel(offset_in, active_in, t_in, keep_ref, send_ref, offset, active, t_ref, sems):
    copies = [
        pltpu.make_async_copy(t_in, t_ref, sems.at[0]),
        pltpu.make_async_copy(offset_in, offset, sems.at[1]),
        pltpu.make_async_copy(active_in, active, sems.at[2]),
    ]
    for copy in copies:
        copy.start()
    for copy in copies:
        copy.wait()
    half = lax.axis_index("loop") // 2
    span = t_ref.shape[2]
    sub = lax.broadcasted_iota(jnp.int32, (ROWS, 128), 0)
    high, low = (offset[0] // 32).astype(jnp.float32), (offset[0] % 32).astype(jnp.float32)
    for c in range(3):
        on = active[0, c].astype(jnp.float32)
        told = jnp.where(sub == 0, high, jnp.where(sub == 1, low, jnp.where(sub == 2, on, 0.0)))
        for out, first in ((keep_ref, half), (send_ref, 1 - half)):
            rows = t_ref[c, pl.ds(pl.multiple_of(ROWS * first, ROWS), ROWS), :]
            out[c, :, :span] = (rows.astype(jnp.float32) * on).astype(jnp.bfloat16)
            out[c, :, span:] = told.astype(jnp.bfloat16)


def split(offset, active, panel):
    half = jax.ShapeDtypeStruct((3, ROWS, panel.shape[2] + 128), jnp.bfloat16)
    return pl.pallas_call(
        split_kernel,
        out_shape=(half, half),
        in_specs=[pl.BlockSpec(memory_space=pltpu.HBM)] * 3,
        out_specs=(pl.BlockSpec(memory_space=pltpu.VMEM),) * 2,
        scratch_shapes=[
            pltpu.SMEM(offset.shape, jnp.int32),
            pltpu.SMEM(active.shape, jnp.int32),
            pltpu.VMEM(panel.shape, jnp.bfloat16),
            pltpu.SemaphoreType.DMA((3,)),
        ],
        compiler_params=pltpu.CompilerParams(vmem_limit_bytes=4 << 20),
        name="split",
    )(offset, active, panel)


def series_kernel(blocks, own, told, near, far, mine_ref, mate_ref, whole):
    z = lax.axis_index("tgrp")
    core = lax.axis_index("loop") % 2
    rows = mine_ref.shape[1]
    span = told.shape[2] - 128
    lane = lanes((rows, 128))
    whole[:, 4 * blocks :] = jnp.zeros((6, whole.shape[1] - 4 * blocks, 128), jnp.float32)
    wide = [near[...].astype(jnp.float32), far[...].astype(jnp.float32)]
    for b in range(4):
        at = pl.multiple_of(blocks * (z ^ b), 8)
        for i in range(6):
            first = 6 * blocks * (b % 2) + i * blocks
            whole[i, pl.ds(at, blocks), :] = wide[b // 2][first : first + blocks]
    for station in range(2):
        words = (own, told)[station]
        first = words[0, :, span:].astype(jnp.float32)
        shift = (32.0 * jnp.max(first[0:1]) + jnp.max(first[1:2])).astype(jnp.int32)
        row, turn = shift // 128, shift % 128
        spill = lane >= 128 - turn
        for c in range(3):
            i = 3 * station + c
            on = words[c, :, span:].astype(jnp.float32)[2:3]
            for out, half in ((mine_ref, core), (mate_ref, 1 - core)):
                at = row + 2 * blocks * half
                here = pltpu.roll(whole[i, pl.ds(at, rows), :], 128 - turn, 1)
                after = pltpu.roll(whole[i, pl.ds(at + 1, rows), :], 128 - turn, 1)
                out[i] = (jnp.where(spill, after, here) * on).astype(jnp.bfloat16)


def make_series(own, told, near, far, blocks, rows):
    window = jax.ShapeDtypeStruct((6, rows, 128), jnp.bfloat16)
    vmem = pl.BlockSpec(memory_space=pltpu.VMEM)
    return pl.pallas_call(
        functools.partial(series_kernel, blocks),
        out_shape=(window, window),
        in_specs=[vmem] * 4,
        out_specs=(vmem, vmem),
        scratch_shapes=[pltpu.VMEM((6, 2 * blocks + rows + 8, 128), jnp.float32)],
        compiler_params=pltpu.CompilerParams(vmem_limit_bytes=4 << 20),
        name="series",
    )(own, told, near, far)


def correlate_kernel(span, nb, t0, t1, t2, t3, mine, mate, masks, first_ref, second_ref,
                     tp_ref, xb_ref, xf_ref, a_ref, z_ref, d_ref, acc_ref, tot_ref, tr_ref, sems):
    lb = span // 128
    kb = lb + 1
    rows = xf_ref.shape[1]
    loop_at = lax.axis_index("loop")
    half = loop_at // 2
    copies = []
    for s, t in enumerate((t0, t1, t2, t3)):
        x = (mine, mate)[s % 2].at[pl.ds(3 * (s // 2), 3)]
        t = t.at[:, :, pl.ds(0, span)]
        copies.append(pltpu.make_async_copy(t, tp_ref.at[pl.ds(3 * s, 3), :, pl.ds(128, span)], sems.at[2 * s]))
        copies.append(pltpu.make_async_copy(x, xb_ref.at[pl.ds(3 * s, 3)], sems.at[2 * s + 1]))
    for copy in copies:
        copy.start()
    tp_ref[:, :, 0:128] = jnp.zeros((12, ROWS, 128), jnp.bfloat16)
    tp_ref[:, :, 128 + span :] = jnp.zeros((12, ROWS, 128), jnp.bfloat16)
    tot_ref[...] = jnp.zeros(tot_ref.shape, jnp.float32)
    k_first = 2 * ROWS * lax.axis_index("tgrp") + ROWS * half
    lane = lanes((8, 128))
    sub = lax.broadcasted_iota(jnp.int32, (8, 128), 0)
    counts = jnp.sum(masks[...], axis=0, keepdims=True).astype(jnp.float32)
    weight = jnp.sqrt(3.0 * span / counts)
    own = k_first + lane % ROWS
    diagonal = lanes((ROWS, 128)) % ROWS == lax.broadcasted_iota(jnp.int32, (ROWS, 128), 0)
    lane_r = lanes((rows, 128))
    for copy in copies:
        copy.wait()

    def row_scale(s):
        norm = jnp.zeros((ROWS, 128), jnp.float32)
        for c in range(3):
            for b in range(lb):
                wide = tp_ref[3 * s + c, :, 128 * b + 128 : 128 * b + 256].astype(jnp.float32)
                norm = norm + wide * wide
        inverse = 1.0 / jnp.sqrt(jnp.sum(norm, axis=1, keepdims=True) / (3.0 * span) + epsilon)
        inverse = jnp.where(diagonal, jnp.broadcast_to(inverse, (ROWS, 128)), 0.0)
        inverse = jnp.sum(inverse, axis=0, keepdims=True)
        here = masks[pl.ds(loop_at ^ s, 1), :].astype(jnp.float32) * weight
        here = jnp.take_along_axis(jnp.broadcast_to(here, (8, 128)), own, axis=1)
        return here[0:1] * inverse / (3.0 * span)

    def data_scale(s):
        squares = jnp.zeros((rows, 128), jnp.float32)
        for c in range(3):
            x = xb_ref[3 * s + c].astype(jnp.float32)
            squares = squares + x * x
        b = 1
        while b < 128:
            after = pltpu.roll(squares, rows - 1, 0)
            squares = squares + pltpu.roll(jnp.where(lane_r < b, after, squares), 128 - b, 1)
            b *= 2
        b = 1
        while b < lb:
            squares = squares + pltpu.roll(squares, rows - b, 0)
            b *= 2
        d_ref[...] = 1.0 / jnp.sqrt(squares / (3.0 * span) + epsilon)

    from_lane = (lane + sub) % 128
    inside = lane + sub < 128

    def build(i, slot):
        for r in range(SHIFTS):
            n = ROWS * (8 * (r % 2) + r // 2)
            a_ref[slot, n : n + ROWS, :] = tp_ref[i, :, 128 - 8 * r : 128 - 8 * r + 128 * kb]

        xf_ref[slot] = xb_ref[i].astype(jnp.float32)

        def turned(j):
            row = xf_ref[slot, pl.ds(j, 8, stride=0), :]
            return jnp.take_along_axis(row, from_lane, axis=1)

        before, tiles = turned(0), []
        for j in range(2 * nb + lb):
            after = turned(j + 1)
            tiles.append(jnp.where(inside, before, after))
            before = after
            if j >= nb:
                z_ref[slot, j - nb] = jnp.concatenate([tiles[j - nb], tiles[j]], axis=0).astype(jnp.bfloat16)

    def product(slot):
        left = jnp.concatenate([z_ref[slot, b : b + nb].reshape(16 * nb, 128) for b in range(kb)], axis=1)
        return lax.dot_general(left, a_ref[slot], (((1,), (1,)), ((), ())), preferred_element_type=jnp.float32)

    def weighted(rs):
        for v in (0, 1):
            index = 16 * (lane // 16) + 8 * v + sub
            for j in range(nb):
                for h in (0, 1):
                    at = 16 * j + 8 * h
                    scale = jnp.take_along_axis(d_ref[pl.ds(j + nb * h, 8, stride=0), :], index, axis=1) * rs
                    tot_ref[v, at : at + 8, :] += acc_ref[at : at + 8, 128 * v : 128 * v + 128] * scale

    build(0, 0)

    def station(s, carry):
        for c in range(3):
            m = product(c)
            build(jnp.minimum(3 * s + c + 1, 11), (c + 1) % 3)
            if c == 0:
                acc_ref[...] = m
            else:
                acc_ref[...] += m
            if c == 0:
                rs = row_scale(s)
            if c == 1:
                data_scale(s)
        weighted(rs)
        return carry

    lax.fori_loop(0, 4, station, 0)

    for f, out in enumerate((first_ref, second_ref)):
        h = half ^ f
        for jb in range(nb // 8):
            v = [[tot_ref[q, pl.ds(128 * jb + 8 * h + p, 8, stride=16), :] for p in range(8)] for q in (0, 1)]
            for b in (1, 2, 4):
                upper = (lane // b) % 2 == 1
                for q in (0, 1):
                    for p in range(8):
                        if not p & b:
                            x, y = v[q][p], v[q][p + b]
                            v[q][p] = jnp.where(upper, pltpu.roll(y, b, 1), x)
                            v[q][p + b] = jnp.where(upper, y, pltpu.roll(x, 128 - b, 1))
            upper = (lane // 8) % 2 == 1
            for p in range(8):
                x, y = v[0][p], v[1][p]
                v[0][p] = jnp.where(upper, pltpu.roll(y, 8, 1), x)
                v[1][p] = jnp.where(upper, y, pltpu.roll(x, 120, 1))
            for q in (0, 1):
                for p in range(8):
                    at = nb * (8 * q + p) + 8 * jb
                    tr_ref[f, at : at + 8, :] = v[q][p]
        levels = [jnp.zeros((8, 128), jnp.float32)] * 2
        for j in range(nb):
            codes = []
            for q in (0, 1):
                value = tr_ref[f, pl.ds(8 * nb * q + j, 8, stride=nb), :]
                top = jnp.maximum(jnp.max(jnp.abs(value), axis=1, keepdims=True), 2e-33)
                level = jnp.ceil(jnp.log2(jnp.broadcast_to(top, (8, 128))) * LEVELS)
                levels[q] = jnp.where(lane == j, level, levels[q])
                codes.append(jnp.round(value * (STEPS * jnp.exp2(level * (-1.0 / LEVELS)))))
            out[:, 128 * j : 128 * j + 128] = jnp.concatenate(codes, axis=0).astype(jnp.int32).astype(jnp.int16)
        out[:, 128 * nb :] = jnp.concatenate(levels, axis=0).astype(jnp.int32).astype(jnp.int16)


def decode_kernel(a_ref, b_ref, out_ref):
    odd = lax.axis_index("tgrp") % 2
    nb = out_ref.shape[1] // 128
    for ref, half in ((a_ref, odd), (b_ref, 1 - odd)):
        at = pl.multiple_of(ROWS * half, ROWS)
        step = jnp.exp2(ref[:, 128 * nb :].astype(jnp.float32) * (1.0 / LEVELS)) * (1.0 / STEPS)
        for j in range(nb):
            value = ref[:, 128 * j : 128 * j + 128].astype(jnp.float32)
            out_ref[pl.ds(at, ROWS), 128 * j : 128 * j + 128] = value * step[:, j : j + 1]


def decode(first, second):
    vmem = pl.BlockSpec(memory_space=pltpu.VMEM)
    return pl.pallas_call(
        decode_kernel,
        out_shape=jax.ShapeDtypeStruct((2 * ROWS, first.shape[1] - 128), jnp.float32),
        in_specs=[vmem, vmem],
        out_specs=vmem,
        compiler_params=pltpu.CompilerParams(vmem_limit_bytes=4 << 20),
        name="decode",
    )(first, second)


def correlate_stations(panels, series, masks, span, nb):
    lb = span // 128
    rows = series[0].shape[1]
    block = jax.ShapeDtypeStruct((ROWS, 128 * nb + 128), jnp.int16)
    vmem = pl.BlockSpec(memory_space=pltpu.VMEM)
    return pl.pallas_call(
        functools.partial(correlate_kernel, span, nb),
        out_shape=(block, block),
        in_specs=[pl.BlockSpec(memory_space=pl.ANY)] * 6 + [vmem],
        out_specs=(vmem, vmem),
        scratch_shapes=[
            pltpu.VMEM((12, ROWS, span + 256), jnp.bfloat16),
            pltpu.VMEM((12, rows, 128), jnp.bfloat16),
            pltpu.VMEM((3, rows, 128), jnp.float32),
            pltpu.VMEM((3, ROWS * SHIFTS, span + 128), jnp.bfloat16),
            pltpu.VMEM((3, nb + lb, 16, 128), jnp.bfloat16),
            pltpu.VMEM((rows, 128), jnp.float32),
            pltpu.VMEM((16 * nb, 256), jnp.float32),
            pltpu.VMEM((2, 16 * nb, 128), jnp.float32),
            pltpu.VMEM((2, 16 * nb, 128), jnp.float32),
            pltpu.SemaphoreType.DMA((8,)),
        ],
        compiler_params=pltpu.CompilerParams(vmem_limit_bytes=24 << 20),
        name="correlate",
    )(*panels, *series, masks)


def swapped(value, loop_bits, tgrp_bits):
    pairs = [(4 * l + z, 4 * (l ^ loop_bits) + (z ^ tgrp_bits)) for l in range(4) for z in range(4)]
    return lax.ppermute(value, ("loop", "tgrp"), pairs)


def to_owner(value, flip):
    pairs = [(4 * l + z, 4 * z + 2 * (l % 2) + ((l // 2) ^ flip)) for l in range(4) for z in range(4)]
    return lax.ppermute(value, ("loop", "tgrp"), pairs)


def local_plane(data, templates, masks, offsets, active):
    span = templates.shape[3]
    nb = data.shape[2] // 128
    panel = templates[:, 0].transpose(1, 0, 2)
    keep, send = split(offsets, active, panel)
    panel_c = swapped(keep, 1, 0)
    pieces = data.reshape(3 * nb, 128)
    pair = jnp.concatenate([pieces, swapped(pieces, 2, 0)], axis=0)
    near = jnp.concatenate([pair, swapped(pair, 0, 1)], axis=0)
    far = swapped(near, 0, 2)
    send, _ = lax.optimization_barrier((send, near))
    panel_y = swapped(send, 2, 0)
    mine, mate = make_series(keep, panel_y, near, far, nb, 2 * nb + span // 128 + 8)
    mate = swapped(mate, 1, 0)
    panel_late, _ = lax.optimization_barrier((panel_y, far))
    panel_yc = swapped(panel_late, 1, 0)
    first, second = correlate_stations(
        (keep, panel_c, panel_y, panel_yc), (mine, mate), masks.T, span, nb
    )
    return decode(to_owner(first, 0), to_owner(second, 1))


def solution(mesh):
    placed = (
        P(("parts", "loop"), None, "tgrp"),
        P("tgrp", "loop", None, None),
        P(),
        P(("parts", "loop")),
        P(("parts", "loop"), None),
    )

    def local(data, templates, masks, offsets, active):
        grid = (mesh.shape["loop"], mesh.shape["tgrp"])
        fits = grid == (4, 4) and templates.shape[:2] == (2 * ROWS, 1) and masks.shape[0] == 128
        fits = fits and templates.shape[3] == 2048 and data.shape[0] == 1 and data.shape[2] % 1024 == 0
        plan = local_plane if fits else local_general
        return plan(data, templates, masks, offsets, active)

    return jax.shard_map(
        local, mesh=mesh, in_specs=placed, out_specs=P(("parts", "loop"), "tgrp"), check_vma=False
    )
```

```python
import functools

import jax
import jax.numpy as jnp
from jax import lax
from jax.experimental import pallas as pl
from jax.experimental.pallas import tpu as pltpu
from jax.sharding import PartitionSpec as P

L = 2048


epsilon = 1e-05


def passed_along(value, axis, steps):
    count = lax.axis_size(axis)
    initial, last = (max(0, -steps), min(count, count - steps))
    return lax.ppermute(value, axis, [(source, source + steps) for source in range(initial, last)])


def window_energy(squares, out_len, span):
    inner_len = out_len + span - 128
    nblocks = (inner_len + 127) // 128
    total_len = 128 * (nblocks + 1)
    padded = jnp.concatenate([squares, jnp.zeros((total_len - squares.shape[0],), squares.dtype)])
    first = padded[: 128 * nblocks].reshape(nblocks, 128)
    second = padded[128 : 128 * nblocks + 128].reshape(nblocks, 128)
    segments = jnp.concatenate([first, second], axis=1)
    rows_at = lax.broadcasted_iota(jnp.int32, (256, 128), 0)
    cols_at = lax.broadcasted_iota(jnp.int32, (256, 128), 1)
    gap = rows_at - cols_at
    band = jnp.where((gap >= 0) & (gap < 128), 1.0, 0.0).astype(squares.dtype)
    inner = jnp.dot(segments, band, precision=lax.Precision.HIGHEST).reshape(nblocks * 128)
    energy = jnp.zeros((out_len,), squares.dtype)
    for block_at in range(span // 128):
        energy = energy + inner[128 * block_at : 128 * block_at + out_len]
    return energy


def correlate(panel, window, out_len):
    row_count = panel.shape[0]
    blocks = panel.shape[2] // 128
    span_len = out_len + panel.shape[2] - 128
    unfold = jnp.stack(
        [window[:, shift_by : shift_by + span_len] for shift_by in range(128)], axis=1
    )
    unfold = unfold.reshape(3 * 128, span_len)
    frames = (
        panel.reshape(row_count, 3, blocks, 128)
        .transpose(0, 2, 1, 3)
        .reshape(row_count, blocks, 3 * 128)
    )

    def add_block(block_at, running_sum):
        start_at = (block_at * 128).astype(jnp.int32)
        columns = lax.dynamic_slice_in_dim(unfold, start_at, out_len, 1)
        weights_now = lax.dynamic_index_in_dim(frames, block_at, 1, keepdims=False)
        return running_sum + jnp.dot(weights_now, columns, preferred_element_type=jnp.float32)

    return lax.fori_loop(0, blocks, add_block, jnp.zeros((row_count, out_len), jnp.float32))


def local_general(data, templates, masks, offsets, active):
    local_count = data.shape[0]
    block_len = data.shape[2]
    following = passed_along(data, "tgrp", -1)
    extended = jnp.concatenate([data, following], axis=2)
    loop_at = lax.axis_index("loop")
    first_station = loop_at * local_count
    counts = jnp.sum(masks, axis=1).astype(jnp.float32)
    local_masks = lax.dynamic_slice_in_dim(masks, first_station, local_count, 1)
    weights = local_masks.astype(jnp.float32) * jnp.sqrt(3.0 * L / counts)[:, None]
    station = 0
    channel_on = active[station].astype(jnp.bfloat16)
    series = lax.dynamic_slice(
        extended[station], (jnp.int32(0), offsets[station]), (3, block_len + L)
    )
    window = series * channel_on[:, None]
    wide_window = window.astype(jnp.float32)
    squares = jnp.sum(wide_window * wide_window, axis=0)
    energy = window_energy(squares, block_len, L)
    inv_datas = [1.0 / jnp.sqrt(energy / (3.0 * L) + epsilon)]
    windows = [window]
    channel_sets = [channel_on]
    panel_rows = lax.all_gather(templates, "tgrp", axis=0, tiled=True)
    station = 0
    panel = panel_rows[:, station] * channel_sets[station][None, :, None]
    wide_panel = panel.astype(jnp.float32)
    inv_template = 1.0 / jnp.sqrt(
        jnp.sum(wide_panel * wide_panel, axis=(1, 2)) / (3.0 * L) + epsilon
    )
    corr = correlate(panel, windows[station], block_len)
    row_weights = weights[:, station]
    row_scale = inv_template * row_weights
    stacked = corr * inv_datas[station][None, :] * row_scale[:, None] / (3.0 * L)
    rows_here = stacked.shape[0] // lax.axis_size("loop")
    summed = lax.psum(stacked, "loop")
    return lax.dynamic_slice_in_dim(summed, loop_at * rows_here, rows_here, 0)


ROWS = 16
SHIFTS = 16
STEPS = 32700.0
LEVELS = 64.0


def lanes(shape):
    return lax.broadcasted_iota(jnp.int32, shape, len(shape) - 1)


def split_kernel(offset_in, active_in, t_in, keep_ref, send_ref, offset, active, t_ref, sems):
    copies = [
        pltpu.make_async_copy(t_in, t_ref, sems.at[0]),
        pltpu.make_async_copy(offset_in, offset, sems.at[1]),
        pltpu.make_async_copy(active_in, active, sems.at[2]),
    ]
    for copy in copies:
        copy.start()
    for copy in copies:
        copy.wait()
    half = lax.axis_index("loop") // 2
    span = t_ref.shape[2]
    sub = lax.broadcasted_iota(jnp.int32, (ROWS, 128), 0)
    high, low = (offset[0] // 32).astype(jnp.float32), (offset[0] % 32).astype(jnp.float32)
    for c in range(3):
        on = active[0, c].astype(jnp.float32)
        told = jnp.where(sub == 0, high, jnp.where(sub == 1, low, jnp.where(sub == 2, on, 0.0)))
        for out, first in ((keep_ref, half), (send_ref, 1 - half)):
            rows = t_ref[c, pl.ds(pl.multiple_of(ROWS * first, ROWS), ROWS), :]
            out[c, :, :span] = (rows.astype(jnp.float32) * on).astype(jnp.bfloat16)
            out[c, :, span:] = told.astype(jnp.bfloat16)


def split(offset, active, panel):
    half = jax.ShapeDtypeStruct((3, ROWS, panel.shape[2] + 128), jnp.bfloat16)
    return pl.pallas_call(
        split_kernel,
        out_shape=(half, half),
        in_specs=[pl.BlockSpec(memory_space=pltpu.HBM)] * 3,
        out_specs=(pl.BlockSpec(memory_space=pltpu.VMEM),) * 2,
        scratch_shapes=[
            pltpu.SMEM(offset.shape, jnp.int32),
            pltpu.SMEM(active.shape, jnp.int32),
            pltpu.VMEM(panel.shape, jnp.bfloat16),
            pltpu.SemaphoreType.DMA((3,)),
        ],
        compiler_params=pltpu.CompilerParams(vmem_limit_bytes=4 << 20),
        name="split",
    )(offset, active, panel)


def series_kernel(blocks, own, told, near, far, mine_ref, mate_ref, whole):
    z = lax.axis_index("tgrp")
    core = lax.axis_index("loop") % 2
    rows = mine_ref.shape[1]
    span = told.shape[2] - 128
    lane = lanes((rows, 128))
    whole[:, 4 * blocks :] = jnp.zeros((6, whole.shape[1] - 4 * blocks, 128), jnp.float32)
    wide = [near[...].astype(jnp.float32), far[...].astype(jnp.float32)]
    for b in range(4):
        at = pl.multiple_of(blocks * (z ^ b), 8)
        for i in range(6):
            first = 6 * blocks * (b % 2) + i * blocks
            whole[i, pl.ds(at, blocks), :] = wide[b // 2][first : first + blocks]
    for station in range(2):
        words = (own, told)[station]
        first = words[0, :, span:].astype(jnp.float32)
        shift = (32.0 * jnp.max(first[0:1]) + jnp.max(first[1:2])).astype(jnp.int32)
        row, turn = shift // 128, shift % 128
        spill = lane >= 128 - turn
        for c in range(3):
            i = 3 * station + c
            on = words[c, :, span:].astype(jnp.float32)[2:3]
            for out, half in ((mine_ref, core), (mate_ref, 1 - core)):
                at = row + 2 * blocks * half
                here = pltpu.roll(whole[i, pl.ds(at, rows), :], 128 - turn, 1)
                after = pltpu.roll(whole[i, pl.ds(at + 1, rows), :], 128 - turn, 1)
                out[i] = (jnp.where(spill, after, here) * on).astype(jnp.bfloat16)


def make_series(own, told, near, far, blocks, rows):
    window = jax.ShapeDtypeStruct((6, rows, 128), jnp.bfloat16)
    vmem = pl.BlockSpec(memory_space=pltpu.VMEM)
    return pl.pallas_call(
        functools.partial(series_kernel, blocks),
        out_shape=(window, window),
        in_specs=[vmem] * 4,
        out_specs=(vmem, vmem),
        scratch_shapes=[pltpu.VMEM((6, 2 * blocks + rows + 8, 128), jnp.float32)],
        compiler_params=pltpu.CompilerParams(vmem_limit_bytes=4 << 20),
        name="series",
    )(own, told, near, far)


def correlate_kernel(span, nb, t0, t1, t2, t3, mine, mate, masks, first_ref, second_ref,
                     tp_ref, xb_ref, xf_ref, a_ref, z_ref, d_ref, acc_ref, tot_ref, tr_ref, sems):
    lb = span // 128
    kb = lb + 1
    rows = xf_ref.shape[1]
    loop_at = lax.axis_index("loop")
    half = loop_at // 2
    copies = []
    for s, t in enumerate((t0, t1, t2, t3)):
        x = (mine, mate)[s % 2].at[pl.ds(3 * (s // 2), 3)]
        t = t.at[:, :, pl.ds(0, span)]
        copies.append(pltpu.make_async_copy(t, tp_ref.at[pl.ds(3 * s, 3), :, pl.ds(128, span)], sems.at[2 * s]))
        copies.append(pltpu.make_async_copy(x, xb_ref.at[pl.ds(3 * s, 3)], sems.at[2 * s + 1]))
    for copy in copies:
        copy.start()
    tp_ref[:, :, 0:128] = jnp.zeros((12, ROWS, 128), jnp.bfloat16)
    tp_ref[:, :, 128 + span :] = jnp.zeros((12, ROWS, 128), jnp.bfloat16)
    tot_ref[...] = jnp.zeros(tot_ref.shape, jnp.float32)
    k_first = 2 * ROWS * lax.axis_index("tgrp") + ROWS * half
    lane = lanes((8, 128))
    sub = lax.broadcasted_iota(jnp.int32, (8, 128), 0)
    counts = jnp.sum(masks[...], axis=0, keepdims=True).astype(jnp.float32)
    weight = jnp.sqrt(3.0 * span / counts)
    own = k_first + lane % ROWS
    diagonal = lanes((ROWS, 128)) % ROWS == lax.broadcasted_iota(jnp.int32, (ROWS, 128), 0)
    lane_r = lanes((rows, 128))
    for copy in copies:
        copy.wait()

    def row_scale(s):
        norm = jnp.zeros((ROWS, 128), jnp.float32)
        for c in range(3):
            for b in range(lb):
                wide = tp_ref[3 * s + c, :, 128 * b + 128 : 128 * b + 256].astype(jnp.float32)
                norm = norm + wide * wide
        inverse = 1.0 / jnp.sqrt(jnp.sum(norm, axis=1, keepdims=True) / (3.0 * span) + epsilon)
        inverse = jnp.where(diagonal, jnp.broadcast_to(inverse, (ROWS, 128)), 0.0)
        inverse = jnp.sum(inverse, axis=0, keepdims=True)
        here = masks[pl.ds(loop_at ^ s, 1), :].astype(jnp.float32) * weight
        here = jnp.take_along_axis(jnp.broadcast_to(here, (8, 128)), own, axis=1)
        return here[0:1] * inverse / (3.0 * span)

    def data_scale(s):
        squares = jnp.zeros((rows, 128), jnp.float32)
        for c in range(3):
            x = xb_ref[3 * s + c].astype(jnp.float32)
            squares = squares + x * x
        b = 1
        while b < 128:
            after = pltpu.roll(squares, rows - 1, 0)
            squares = squares + pltpu.roll(jnp.where(lane_r < b, after, squares), 128 - b, 1)
            b *= 2
        b = 1
        while b < lb:
            squares = squares + pltpu.roll(squares, rows - b, 0)
            b *= 2
        d_ref[...] = 1.0 / jnp.sqrt(squares / (3.0 * span) + epsilon)

    from_lane = (lane + sub) % 128
    inside = lane + sub < 128

    def build(i, slot):
        for r in range(SHIFTS):
            n = ROWS * (8 * (r % 2) + r // 2)
            a_ref[slot, n : n + ROWS, :] = tp_ref[i, :, 128 - 8 * r : 128 - 8 * r + 128 * kb]

        xf_ref[slot] = xb_ref[i].astype(jnp.float32)

        def turned(j):
            row = xf_ref[slot, pl.ds(j, 8, stride=0), :]
            return jnp.take_along_axis(row, from_lane, axis=1)

        before, tiles = turned(0), []
        for j in range(2 * nb + lb):
            after = turned(j + 1)
            tiles.append(jnp.where(inside, before, after))
            before = after
            if j >= nb:
                z_ref[slot, j - nb] = jnp.concatenate([tiles[j - nb], tiles[j]], axis=0).astype(jnp.bfloat16)

    def product(slot):
        left = jnp.concatenate([z_ref[slot, b : b + nb].reshape(16 * nb, 128) for b in range(kb)], axis=1)
        return lax.dot_general(left, a_ref[slot], (((1,), (1,)), ((), ())), preferred_element_type=jnp.float32)

    def weighted(rs):
        for v in (0, 1):
            index = 16 * (lane // 16) + 8 * v + sub
            for j in range(nb):
                for h in (0, 1):
                    at = 16 * j + 8 * h
                    scale = jnp.take_along_axis(d_ref[pl.ds(j + nb * h, 8, stride=0), :], index, axis=1) * rs
                    tot_ref[v, at : at + 8, :] += acc_ref[at : at + 8, 128 * v : 128 * v + 128] * scale

    build(0, 0)

    def station(s, carry):
        for c in range(3):
            m = product(c)
            build(jnp.minimum(3 * s + c + 1, 11), (c + 1) % 3)
            if c == 0:
                acc_ref[...] = m
            else:
                acc_ref[...] += m
            if c == 0:
                rs = row_scale(s)
            if c == 1:
                data_scale(s)
        weighted(rs)
        return carry

    lax.fori_loop(0, 4, station, 0)

    for f, out in enumerate((first_ref, second_ref)):
        h = half ^ f
        for jb in range(nb // 8):
            v = [[tot_ref[q, pl.ds(128 * jb + 8 * h + p, 8, stride=16), :] for p in range(8)] for q in (0, 1)]
            for b in (1, 2, 4):
                upper = (lane // b) % 2 == 1
                for q in (0, 1):
                    for p in range(8):
                        if not p & b:
                            x, y = v[q][p], v[q][p + b]
                            v[q][p] = jnp.where(upper, pltpu.roll(y, b, 1), x)
                            v[q][p + b] = jnp.where(upper, y, pltpu.roll(x, 128 - b, 1))
            upper = (lane // 8) % 2 == 1
            for p in range(8):
                x, y = v[0][p], v[1][p]
                v[0][p] = jnp.where(upper, pltpu.roll(y, 8, 1), x)
                v[1][p] = jnp.where(upper, y, pltpu.roll(x, 120, 1))
            for q in (0, 1):
                for p in range(8):
                    at = nb * (8 * q + p) + 8 * jb
                    tr_ref[f, at : at + 8, :] = v[q][p]
        levels = [jnp.zeros((8, 128), jnp.float32)] * 2
        for j in range(nb):
            codes = []
            for q in (0, 1):
                value = tr_ref[f, pl.ds(8 * nb * q + j, 8, stride=nb), :]
                top = jnp.maximum(jnp.max(jnp.abs(value), axis=1, keepdims=True), 2e-33)
                level = jnp.ceil(jnp.log2(jnp.broadcast_to(top, (8, 128))) * LEVELS)
                levels[q] = jnp.where(lane == j, level, levels[q])
                codes.append(jnp.round(value * (STEPS * jnp.exp2(level * (-1.0 / LEVELS)))))
            out[:, 128 * j : 128 * j + 128] = jnp.concatenate(codes, axis=0).astype(jnp.int32).astype(jnp.int16)
        out[:, 128 * nb :] = jnp.concatenate(levels, axis=0).astype(jnp.int32).astype(jnp.int16)


def decode_kernel(a_ref, b_ref, out_ref):
    odd = lax.axis_index("tgrp") % 2
    nb = out_ref.shape[1] // 128
    for ref, half in ((a_ref, odd), (b_ref, 1 - odd)):
        at = pl.multiple_of(ROWS * half, ROWS)
        step = jnp.exp2(ref[:, 128 * nb :].astype(jnp.float32) * (1.0 / LEVELS)) * (1.0 / STEPS)
        for j in range(nb):
            value = ref[:, 128 * j : 128 * j + 128].astype(jnp.float32)
            out_ref[pl.ds(at, ROWS), 128 * j : 128 * j + 128] = value * step[:, j : j + 1]


def decode(first, second):
    vmem = pl.BlockSpec(memory_space=pltpu.VMEM)
    return pl.pallas_call(
        decode_kernel,
        out_shape=jax.ShapeDtypeStruct((2 * ROWS, first.shape[1] - 128), jnp.float32),
        in_specs=[vmem, vmem],
        out_specs=vmem,
        compiler_params=pltpu.CompilerParams(vmem_limit_bytes=4 << 20),
        name="decode",
    )(first, second)


def correlate_stations(panels, series, masks, span, nb):
    lb = span // 128
    rows = series[0].shape[1]
    block = jax.ShapeDtypeStruct((ROWS, 128 * nb + 128), jnp.int16)
    vmem = pl.BlockSpec(memory_space=pltpu.VMEM)
    return pl.pallas_call(
        functools.partial(correlate_kernel, span, nb),
        out_shape=(block, block),
        in_specs=[pl.BlockSpec(memory_space=pl.ANY)] * 6 + [vmem],
        out_specs=(vmem, vmem),
        scratch_shapes=[
            pltpu.VMEM((12, ROWS, span + 256), jnp.bfloat16),
            pltpu.VMEM((12, rows, 128), jnp.bfloat16),
            pltpu.VMEM((3, rows, 128), jnp.float32),
            pltpu.VMEM((3, ROWS * SHIFTS, span + 128), jnp.bfloat16),
            pltpu.VMEM((3, nb + lb, 16, 128), jnp.bfloat16),
            pltpu.VMEM((rows, 128), jnp.float32),
            pltpu.VMEM((16 * nb, 256), jnp.float32),
            pltpu.VMEM((2, 16 * nb, 128), jnp.float32),
            pltpu.VMEM((2, 16 * nb, 128), jnp.float32),
            pltpu.SemaphoreType.DMA((8,)),
        ],
        compiler_params=pltpu.CompilerParams(vmem_limit_bytes=24 << 20),
        name="correlate",
    )(*panels, *series, masks)


def swapped(value, loop_bits, tgrp_bits):
    pairs = [(4 * l + z, 4 * (l ^ loop_bits) + (z ^ tgrp_bits)) for l in range(4) for z in range(4)]
    return lax.ppermute(value, ("loop", "tgrp"), pairs)


def to_owner(value, flip):
    pairs = [(4 * l + z, 4 * z + 2 * (l % 2) + ((l // 2) ^ flip)) for l in range(4) for z in range(4)]
    return lax.ppermute(value, ("loop", "tgrp"), pairs)


def local_plane(data, templates, masks, offsets, active):
    span = templates.shape[3]
    nb = data.shape[2] // 128
    panel = templates[:, 0].transpose(1, 0, 2)
    keep, send = split(offsets, active, panel)
    panel_c = swapped(keep, 1, 0)
    pieces = data.reshape(3 * nb, 128)
    pieces_y, send = lax.optimization_barrier((swapped(pieces, 2, 0), send))
    pair = jnp.concatenate([pieces, pieces_y], axis=0)
    panel_y = swapped(send, 2, 0)
    near = jnp.concatenate([pair, swapped(pair, 0, 1)], axis=0)
    far = swapped(near, 0, 2)
    mine, mate = make_series(keep, panel_y, near, far, nb, 2 * nb + span // 128 + 8)
    mate = swapped(mate, 1, 0)
    panel_late, _ = lax.optimization_barrier((panel_y, far))
    panel_yc = swapped(panel_late, 1, 0)
    first, second = correlate_stations(
        (keep, panel_c, panel_y, panel_yc), (mine, mate), masks.T, span, nb
    )
    return decode(to_owner(first, 0), to_owner(second, 1))


def solution(mesh):
    placed = (
        P(("parts", "loop"), None, "tgrp"),
        P("tgrp", "loop", None, None),
        P(),
        P(("parts", "loop")),
        P(("parts", "loop"), None),
    )

    def local(data, templates, masks, offsets, active):
        grid = (mesh.shape["loop"], mesh.shape["tgrp"])
        fits = grid == (4, 4) and templates.shape[:2] == (2 * ROWS, 1) and masks.shape[0] == 128
        fits = fits and templates.shape[3] == 2048 and data.shape[0] == 1 and data.shape[2] % 1024 == 0
        plan = local_plane if fits else local_general
        return plan(data, templates, masks, offsets, active)

    return jax.shard_map(
        local, mesh=mesh, in_specs=placed, out_specs=P(("parts", "loop"), "tgrp"), check_vma=False
    )
```

```python
import functools

import jax
import jax.numpy as jnp
from jax import lax
from jax.experimental import pallas as pl
from jax.experimental.pallas import tpu as pltpu
from jax.sharding import PartitionSpec as P

L = 2048


epsilon = 1e-05


def passed_along(value, axis, steps):
    count = lax.axis_size(axis)
    initial, last = (max(0, -steps), min(count, count - steps))
    return lax.ppermute(value, axis, [(source, source + steps) for source in range(initial, last)])


def window_energy(squares, out_len, span):
    inner_len = out_len + span - 128
    nblocks = (inner_len + 127) // 128
    total_len = 128 * (nblocks + 1)
    padded = jnp.concatenate([squares, jnp.zeros((total_len - squares.shape[0],), squares.dtype)])
    first = padded[: 128 * nblocks].reshape(nblocks, 128)
    second = padded[128 : 128 * nblocks + 128].reshape(nblocks, 128)
    segments = jnp.concatenate([first, second], axis=1)
    rows_at = lax.broadcasted_iota(jnp.int32, (256, 128), 0)
    cols_at = lax.broadcasted_iota(jnp.int32, (256, 128), 1)
    gap = rows_at - cols_at
    band = jnp.where((gap >= 0) & (gap < 128), 1.0, 0.0).astype(squares.dtype)
    inner = jnp.dot(segments, band, precision=lax.Precision.HIGHEST).reshape(nblocks * 128)
    energy = jnp.zeros((out_len,), squares.dtype)
    for block_at in range(span // 128):
        energy = energy + inner[128 * block_at : 128 * block_at + out_len]
    return energy


def correlate(panel, window, out_len):
    row_count = panel.shape[0]
    blocks = panel.shape[2] // 128
    span_len = out_len + panel.shape[2] - 128
    unfold = jnp.stack(
        [window[:, shift_by : shift_by + span_len] for shift_by in range(128)], axis=1
    )
    unfold = unfold.reshape(3 * 128, span_len)
    frames = (
        panel.reshape(row_count, 3, blocks, 128)
        .transpose(0, 2, 1, 3)
        .reshape(row_count, blocks, 3 * 128)
    )

    def add_block(block_at, running_sum):
        start_at = (block_at * 128).astype(jnp.int32)
        columns = lax.dynamic_slice_in_dim(unfold, start_at, out_len, 1)
        weights_now = lax.dynamic_index_in_dim(frames, block_at, 1, keepdims=False)
        return running_sum + jnp.dot(weights_now, columns, preferred_element_type=jnp.float32)

    return lax.fori_loop(0, blocks, add_block, jnp.zeros((row_count, out_len), jnp.float32))


def local_general(data, templates, masks, offsets, active):
    local_count = data.shape[0]
    block_len = data.shape[2]
    following = passed_along(data, "tgrp", -1)
    extended = jnp.concatenate([data, following], axis=2)
    loop_at = lax.axis_index("loop")
    first_station = loop_at * local_count
    counts = jnp.sum(masks, axis=1).astype(jnp.float32)
    local_masks = lax.dynamic_slice_in_dim(masks, first_station, local_count, 1)
    weights = local_masks.astype(jnp.float32) * jnp.sqrt(3.0 * L / counts)[:, None]
    station = 0
    channel_on = active[station].astype(jnp.bfloat16)
    series = lax.dynamic_slice(
        extended[station], (jnp.int32(0), offsets[station]), (3, block_len + L)
    )
    window = series * channel_on[:, None]
    wide_window = window.astype(jnp.float32)
    squares = jnp.sum(wide_window * wide_window, axis=0)
    energy = window_energy(squares, block_len, L)
    inv_datas = [1.0 / jnp.sqrt(energy / (3.0 * L) + epsilon)]
    windows = [window]
    channel_sets = [channel_on]
    panel_rows = lax.all_gather(templates, "tgrp", axis=0, tiled=True)
    station = 0
    panel = panel_rows[:, station] * channel_sets[station][None, :, None]
    wide_panel = panel.astype(jnp.float32)
    inv_template = 1.0 / jnp.sqrt(
        jnp.sum(wide_panel * wide_panel, axis=(1, 2)) / (3.0 * L) + epsilon
    )
    corr = correlate(panel, windows[station], block_len)
    row_weights = weights[:, station]
    row_scale = inv_template * row_weights
    stacked = corr * inv_datas[station][None, :] * row_scale[:, None] / (3.0 * L)
    rows_here = stacked.shape[0] // lax.axis_size("loop")
    summed = lax.psum(stacked, "loop")
    return lax.dynamic_slice_in_dim(summed, loop_at * rows_here, rows_here, 0)


ROWS = 16
SHIFTS = 16
STEPS = 32700.0
LEVELS = 64.0


def lanes(shape):
    return lax.broadcasted_iota(jnp.int32, shape, len(shape) - 1)


def split_kernel(offset_in, active_in, t_in, keep_ref, send_ref, offset, active, t_ref, sems):
    copies = [
        pltpu.make_async_copy(t_in, t_ref, sems.at[0]),
        pltpu.make_async_copy(offset_in, offset, sems.at[1]),
        pltpu.make_async_copy(active_in, active, sems.at[2]),
    ]
    for copy in copies:
        copy.start()
    for copy in copies:
        copy.wait()
    half = lax.axis_index("loop") // 2
    span = t_ref.shape[2]
    sub = lax.broadcasted_iota(jnp.int32, (ROWS, 128), 0)
    high, low = (offset[0] // 32).astype(jnp.float32), (offset[0] % 32).astype(jnp.float32)
    for c in range(3):
        on = active[0, c].astype(jnp.float32)
        told = jnp.where(sub == 0, high, jnp.where(sub == 1, low, jnp.where(sub == 2, on, 0.0)))
        for out, first in ((keep_ref, half), (send_ref, 1 - half)):
            rows = t_ref[c, pl.ds(pl.multiple_of(ROWS * first, ROWS), ROWS), :]
            out[c, :, :span] = (rows.astype(jnp.float32) * on).astype(jnp.bfloat16)
            out[c, :, span:] = told.astype(jnp.bfloat16)


def split(offset, active, panel):
    half = jax.ShapeDtypeStruct((3, ROWS, panel.shape[2] + 128), jnp.bfloat16)
    return pl.pallas_call(
        split_kernel,
        out_shape=(half, half),
        in_specs=[pl.BlockSpec(memory_space=pltpu.HBM)] * 3,
        out_specs=(pl.BlockSpec(memory_space=pltpu.VMEM),) * 2,
        scratch_shapes=[
            pltpu.SMEM(offset.shape, jnp.int32),
            pltpu.SMEM(active.shape, jnp.int32),
            pltpu.VMEM(panel.shape, jnp.bfloat16),
            pltpu.SemaphoreType.DMA((3,)),
        ],
        compiler_params=pltpu.CompilerParams(vmem_limit_bytes=4 << 20),
        name="split",
    )(offset, active, panel)


def series_kernel(blocks, own, told, near, far, mine_ref, mate_ref, whole):
    z = lax.axis_index("tgrp")
    core = lax.axis_index("loop") % 2
    rows = mine_ref.shape[1]
    span = told.shape[2] - 128
    lane = lanes((rows, 128))
    whole[:, 4 * blocks :] = jnp.zeros((6, whole.shape[1] - 4 * blocks, 128), jnp.float32)
    wide = [near[...].astype(jnp.float32), far[...].astype(jnp.float32)]
    for b in range(4):
        at = pl.multiple_of(blocks * (z ^ b), 8)
        for i in range(6):
            first = 6 * blocks * (b // 2) + i * blocks
            whole[i, pl.ds(at, blocks), :] = wide[b % 2][first : first + blocks]
    for station in range(2):
        words = (own, told)[station]
        first = words[0, :, span:].astype(jnp.float32)
        shift = (32.0 * jnp.max(first[0:1]) + jnp.max(first[1:2])).astype(jnp.int32)
        row, turn = shift // 128, shift % 128
        spill = lane >= 128 - turn
        for c in range(3):
            i = 3 * station + c
            on = words[c, :, span:].astype(jnp.float32)[2:3]
            for out, half in ((mine_ref, core), (mate_ref, 1 - core)):
                at = row + 2 * blocks * half
                here = pltpu.roll(whole[i, pl.ds(at, rows), :], 128 - turn, 1)
                after = pltpu.roll(whole[i, pl.ds(at + 1, rows), :], 128 - turn, 1)
                out[i] = (jnp.where(spill, after, here) * on).astype(jnp.bfloat16)


def make_series(own, told, near, far, blocks, rows):
    window = jax.ShapeDtypeStruct((6, rows, 128), jnp.bfloat16)
    vmem = pl.BlockSpec(memory_space=pltpu.VMEM)
    return pl.pallas_call(
        functools.partial(series_kernel, blocks),
        out_shape=(window, window),
        in_specs=[vmem] * 4,
        out_specs=(vmem, vmem),
        scratch_shapes=[pltpu.VMEM((6, 2 * blocks + rows + 8, 128), jnp.float32)],
        compiler_params=pltpu.CompilerParams(vmem_limit_bytes=4 << 20),
        name="series",
    )(own, told, near, far)


def correlate_kernel(span, nb, t0, t1, t2, t3, mine, mate, masks, first_ref, second_ref,
                     tp_ref, xb_ref, xf_ref, a_ref, z_ref, d_ref, acc_ref, tot_ref, tr_ref, sems):
    lb = span // 128
    kb = lb + 1
    rows = xf_ref.shape[1]
    loop_at = lax.axis_index("loop")
    half = loop_at // 2
    copies = []
    for s, t in enumerate((t0, t1, t2, t3)):
        x = (mine, mate)[s % 2].at[pl.ds(3 * (s // 2), 3)]
        t = t.at[:, :, pl.ds(0, span)]
        copies.append(pltpu.make_async_copy(t, tp_ref.at[pl.ds(3 * s, 3), :, pl.ds(128, span)], sems.at[2 * s]))
        copies.append(pltpu.make_async_copy(x, xb_ref.at[pl.ds(3 * s, 3)], sems.at[2 * s + 1]))
    for copy in copies:
        copy.start()
    tp_ref[:, :, 0:128] = jnp.zeros((12, ROWS, 128), jnp.bfloat16)
    tp_ref[:, :, 128 + span :] = jnp.zeros((12, ROWS, 128), jnp.bfloat16)
    tot_ref[...] = jnp.zeros(tot_ref.shape, jnp.float32)
    k_first = 2 * ROWS * lax.axis_index("tgrp") + ROWS * half
    lane = lanes((8, 128))
    sub = lax.broadcasted_iota(jnp.int32, (8, 128), 0)
    counts = jnp.sum(masks[...], axis=0, keepdims=True).astype(jnp.float32)
    weight = jnp.sqrt(3.0 * span / counts)
    own = k_first + lane % ROWS
    diagonal = lanes((ROWS, 128)) % ROWS == lax.broadcasted_iota(jnp.int32, (ROWS, 128), 0)
    lane_r = lanes((rows, 128))
    for copy in copies:
        copy.wait()

    def row_scale(s):
        norm = jnp.zeros((ROWS, 128), jnp.float32)
        for c in range(3):
            for b in range(lb):
                wide = tp_ref[3 * s + c, :, 128 * b + 128 : 128 * b + 256].astype(jnp.float32)
                norm = norm + wide * wide
        inverse = 1.0 / jnp.sqrt(jnp.sum(norm, axis=1, keepdims=True) / (3.0 * span) + epsilon)
        inverse = jnp.where(diagonal, jnp.broadcast_to(inverse, (ROWS, 128)), 0.0)
        inverse = jnp.sum(inverse, axis=0, keepdims=True)
        here = masks[pl.ds(loop_at ^ s, 1), :].astype(jnp.float32) * weight
        here = jnp.take_along_axis(jnp.broadcast_to(here, (8, 128)), own, axis=1)
        return here[0:1] * inverse / (3.0 * span)

    def data_scale(s):
        squares = jnp.zeros((rows, 128), jnp.float32)
        for c in range(3):
            x = xb_ref[3 * s + c].astype(jnp.float32)
            squares = squares + x * x
        b = 1
        while b < 128:
            after = pltpu.roll(squares, rows - 1, 0)
            squares = squares + pltpu.roll(jnp.where(lane_r < b, after, squares), 128 - b, 1)
            b *= 2
        b = 1
        while b < lb:
            squares = squares + pltpu.roll(squares, rows - b, 0)
            b *= 2
        d_ref[...] = 1.0 / jnp.sqrt(squares / (3.0 * span) + epsilon)

    from_lane = (lane + sub) % 128
    inside = lane + sub < 128

    def build(i, slot):
        for r in range(SHIFTS):
            n = ROWS * (8 * (r % 2) + r // 2)
            a_ref[slot, n : n + ROWS, :] = tp_ref[i, :, 128 - 8 * r : 128 - 8 * r + 128 * kb]

        xf_ref[slot] = xb_ref[i].astype(jnp.float32)

        def turned(j):
            row = xf_ref[slot, pl.ds(j, 8, stride=0), :]
            return jnp.take_along_axis(row, from_lane, axis=1)

        before, tiles = turned(0), []
        for j in range(2 * nb + lb):
            after = turned(j + 1)
            tiles.append(jnp.where(inside, before, after))
            before = after
            if j >= nb:
                z_ref[slot, j - nb] = jnp.concatenate([tiles[j - nb], tiles[j]], axis=0).astype(jnp.bfloat16)

    def product(slot):
        left = jnp.concatenate([z_ref[slot, b : b + nb].reshape(16 * nb, 128) for b in range(kb)], axis=1)
        return lax.dot_general(left, a_ref[slot], (((1,), (1,)), ((), ())), preferred_element_type=jnp.float32)

    def weighted(rs):
        for v in (0, 1):
            index = 16 * (lane // 16) + 8 * v + sub
            for j in range(nb):
                for h in (0, 1):
                    at = 16 * j + 8 * h
                    scale = jnp.take_along_axis(d_ref[pl.ds(j + nb * h, 8, stride=0), :], index, axis=1) * rs
                    tot_ref[v, at : at + 8, :] += acc_ref[at : at + 8, 128 * v : 128 * v + 128] * scale

    build(0, 0)

    def station(s, carry):
        for c in range(3):
            m = product(c)
            build(jnp.minimum(3 * s + c + 1, 11), (c + 1) % 3)
            if c == 0:
                acc_ref[...] = m
            else:
                acc_ref[...] += m
            if c == 0:
                rs = row_scale(s)
            if c == 1:
                data_scale(s)
        weighted(rs)
        return carry

    lax.fori_loop(0, 4, station, 0)

    for f, out in enumerate((first_ref, second_ref)):
        h = half ^ f
        for jb in range(nb // 8):
            v = [[tot_ref[q, pl.ds(128 * jb + 8 * h + p, 8, stride=16), :] for p in range(8)] for q in (0, 1)]
            for b in (1, 2, 4):
                upper = (lane // b) % 2 == 1
                for q in (0, 1):
                    for p in range(8):
                        if not p & b:
                            x, y = v[q][p], v[q][p + b]
                            v[q][p] = jnp.where(upper, pltpu.roll(y, b, 1), x)
                            v[q][p + b] = jnp.where(upper, y, pltpu.roll(x, 128 - b, 1))
            upper = (lane // 8) % 2 == 1
            for p in range(8):
                x, y = v[0][p], v[1][p]
                v[0][p] = jnp.where(upper, pltpu.roll(y, 8, 1), x)
                v[1][p] = jnp.where(upper, y, pltpu.roll(x, 120, 1))
            for q in (0, 1):
                for p in range(8):
                    at = nb * (8 * q + p) + 8 * jb
                    tr_ref[f, at : at + 8, :] = v[q][p]
        levels = [jnp.zeros((8, 128), jnp.float32)] * 2
        for j in range(nb):
            codes = []
            for q in (0, 1):
                value = tr_ref[f, pl.ds(8 * nb * q + j, 8, stride=nb), :]
                top = jnp.maximum(jnp.max(jnp.abs(value), axis=1, keepdims=True), 2e-33)
                level = jnp.ceil(jnp.log2(jnp.broadcast_to(top, (8, 128))) * LEVELS)
                levels[q] = jnp.where(lane == j, level, levels[q])
                codes.append(jnp.round(value * (STEPS * jnp.exp2(level * (-1.0 / LEVELS)))))
            out[:, 128 * j : 128 * j + 128] = jnp.concatenate(codes, axis=0).astype(jnp.int32).astype(jnp.int16)
        out[:, 128 * nb :] = jnp.concatenate(levels, axis=0).astype(jnp.int32).astype(jnp.int16)


def decode_kernel(a_ref, b_ref, out_ref):
    odd = lax.axis_index("tgrp") % 2
    nb = out_ref.shape[1] // 128
    for ref, half in ((a_ref, odd), (b_ref, 1 - odd)):
        at = pl.multiple_of(ROWS * half, ROWS)
        step = jnp.exp2(ref[:, 128 * nb :].astype(jnp.float32) * (1.0 / LEVELS)) * (1.0 / STEPS)
        for j in range(nb):
            value = ref[:, 128 * j : 128 * j + 128].astype(jnp.float32)
            out_ref[pl.ds(at, ROWS), 128 * j : 128 * j + 128] = value * step[:, j : j + 1]


def decode(first, second):
    vmem = pl.BlockSpec(memory_space=pltpu.VMEM)
    return pl.pallas_call(
        decode_kernel,
        out_shape=jax.ShapeDtypeStruct((2 * ROWS, first.shape[1] - 128), jnp.float32),
        in_specs=[vmem, vmem],
        out_specs=vmem,
        compiler_params=pltpu.CompilerParams(vmem_limit_bytes=4 << 20),
        name="decode",
    )(first, second)


def correlate_stations(panels, series, masks, span, nb):
    lb = span // 128
    rows = series[0].shape[1]
    block = jax.ShapeDtypeStruct((ROWS, 128 * nb + 128), jnp.int16)
    vmem = pl.BlockSpec(memory_space=pltpu.VMEM)
    return pl.pallas_call(
        functools.partial(correlate_kernel, span, nb),
        out_shape=(block, block),
        in_specs=[pl.BlockSpec(memory_space=pl.ANY)] * 6 + [vmem],
        out_specs=(vmem, vmem),
        scratch_shapes=[
            pltpu.VMEM((12, ROWS, span + 256), jnp.bfloat16),
            pltpu.VMEM((12, rows, 128), jnp.bfloat16),
            pltpu.VMEM((3, rows, 128), jnp.float32),
            pltpu.VMEM((3, ROWS * SHIFTS, span + 128), jnp.bfloat16),
            pltpu.VMEM((3, nb + lb, 16, 128), jnp.bfloat16),
            pltpu.VMEM((rows, 128), jnp.float32),
            pltpu.VMEM((16 * nb, 256), jnp.float32),
            pltpu.VMEM((2, 16 * nb, 128), jnp.float32),
            pltpu.VMEM((2, 16 * nb, 128), jnp.float32),
            pltpu.SemaphoreType.DMA((8,)),
        ],
        compiler_params=pltpu.CompilerParams(vmem_limit_bytes=24 << 20),
        name="correlate",
    )(*panels, *series, masks)


def swapped(value, loop_bits, tgrp_bits):
    pairs = [(4 * l + z, 4 * (l ^ loop_bits) + (z ^ tgrp_bits)) for l in range(4) for z in range(4)]
    return lax.ppermute(value, ("loop", "tgrp"), pairs)


def to_owner(value, flip):
    pairs = [(4 * l + z, 4 * z + 2 * (l % 2) + ((l // 2) ^ flip)) for l in range(4) for z in range(4)]
    return lax.ppermute(value, ("loop", "tgrp"), pairs)


def local_plane(data, templates, masks, offsets, active):
    span = templates.shape[3]
    nb = data.shape[2] // 128
    panel = templates[:, 0].transpose(1, 0, 2)
    keep, send = split(offsets, active, panel)
    panel_c = swapped(keep, 1, 0)
    pieces = data.reshape(3 * nb, 128)
    pieces_y, send = lax.optimization_barrier((swapped(pieces, 2, 0), send))
    pair = jnp.concatenate([pieces, pieces_y], axis=0)
    panel_y = swapped(send, 2, 0)
    near = jnp.concatenate([pair, swapped(pair, 0, 2)], axis=0)
    far = swapped(near, 0, 1)
    mine, mate = make_series(keep, panel_y, near, far, nb, 2 * nb + span // 128 + 8)
    mate = swapped(mate, 1, 0)
    panel_late, _ = lax.optimization_barrier((panel_y, far))
    panel_yc = swapped(panel_late, 1, 0)
    first, second = correlate_stations(
        (keep, panel_c, panel_y, panel_yc), (mine, mate), masks.T, span, nb
    )
    return decode(to_owner(first, 0), to_owner(second, 1))


def solution(mesh):
    placed = (
        P(("parts", "loop"), None, "tgrp"),
        P("tgrp", "loop", None, None),
        P(),
        P(("parts", "loop")),
        P(("parts", "loop"), None),
    )

    def local(data, templates, masks, offsets, active):
        grid = (mesh.shape["loop"], mesh.shape["tgrp"])
        fits = grid == (4, 4) and templates.shape[:2] == (2 * ROWS, 1) and masks.shape[0] == 128
        fits = fits and templates.shape[3] == 2048 and data.shape[0] == 1 and data.shape[2] % 1024 == 0
        plan = local_plane if fits else local_general
        return plan(data, templates, masks, offsets, active)

    return jax.shard_map(
        local, mesh=mesh, in_specs=placed, out_specs=P(("parts", "loop"), "tgrp"), check_vma=False
    )
```

```python
import functools

import jax
import jax.numpy as jnp
from jax import lax
from jax.experimental import pallas as pl
from jax.experimental.pallas import tpu as pltpu
from jax.sharding import PartitionSpec as P

L = 2048


epsilon = 1e-05


def passed_along(value, axis, steps):
    count = lax.axis_size(axis)
    initial, last = (max(0, -steps), min(count, count - steps))
    return lax.ppermute(value, axis, [(source, source + steps) for source in range(initial, last)])


def window_energy(squares, out_len, span):
    inner_len = out_len + span - 128
    nblocks = (inner_len + 127) // 128
    total_len = 128 * (nblocks + 1)
    padded = jnp.concatenate([squares, jnp.zeros((total_len - squares.shape[0],), squares.dtype)])
    first = padded[: 128 * nblocks].reshape(nblocks, 128)
    second = padded[128 : 128 * nblocks + 128].reshape(nblocks, 128)
    segments = jnp.concatenate([first, second], axis=1)
    rows_at = lax.broadcasted_iota(jnp.int32, (256, 128), 0)
    cols_at = lax.broadcasted_iota(jnp.int32, (256, 128), 1)
    gap = rows_at - cols_at
    band = jnp.where((gap >= 0) & (gap < 128), 1.0, 0.0).astype(squares.dtype)
    inner = jnp.dot(segments, band, precision=lax.Precision.HIGHEST).reshape(nblocks * 128)
    energy = jnp.zeros((out_len,), squares.dtype)
    for block_at in range(span // 128):
        energy = energy + inner[128 * block_at : 128 * block_at + out_len]
    return energy


def correlate(panel, window, out_len):
    row_count = panel.shape[0]
    blocks = panel.shape[2] // 128
    span_len = out_len + panel.shape[2] - 128
    unfold = jnp.stack(
        [window[:, shift_by : shift_by + span_len] for shift_by in range(128)], axis=1
    )
    unfold = unfold.reshape(3 * 128, span_len)
    frames = (
        panel.reshape(row_count, 3, blocks, 128)
        .transpose(0, 2, 1, 3)
        .reshape(row_count, blocks, 3 * 128)
    )

    def add_block(block_at, running_sum):
        start_at = (block_at * 128).astype(jnp.int32)
        columns = lax.dynamic_slice_in_dim(unfold, start_at, out_len, 1)
        weights_now = lax.dynamic_index_in_dim(frames, block_at, 1, keepdims=False)
        return running_sum + jnp.dot(weights_now, columns, preferred_element_type=jnp.float32)

    return lax.fori_loop(0, blocks, add_block, jnp.zeros((row_count, out_len), jnp.float32))


def local_general(data, templates, masks, offsets, active):
    local_count = data.shape[0]
    block_len = data.shape[2]
    following = passed_along(data, "tgrp", -1)
    extended = jnp.concatenate([data, following], axis=2)
    loop_at = lax.axis_index("loop")
    first_station = loop_at * local_count
    counts = jnp.sum(masks, axis=1).astype(jnp.float32)
    local_masks = lax.dynamic_slice_in_dim(masks, first_station, local_count, 1)
    weights = local_masks.astype(jnp.float32) * jnp.sqrt(3.0 * L / counts)[:, None]
    station = 0
    channel_on = active[station].astype(jnp.bfloat16)
    series = lax.dynamic_slice(
        extended[station], (jnp.int32(0), offsets[station]), (3, block_len + L)
    )
    window = series * channel_on[:, None]
    wide_window = window.astype(jnp.float32)
    squares = jnp.sum(wide_window * wide_window, axis=0)
    energy = window_energy(squares, block_len, L)
    inv_datas = [1.0 / jnp.sqrt(energy / (3.0 * L) + epsilon)]
    windows = [window]
    channel_sets = [channel_on]
    panel_rows = lax.all_gather(templates, "tgrp", axis=0, tiled=True)
    station = 0
    panel = panel_rows[:, station] * channel_sets[station][None, :, None]
    wide_panel = panel.astype(jnp.float32)
    inv_template = 1.0 / jnp.sqrt(
        jnp.sum(wide_panel * wide_panel, axis=(1, 2)) / (3.0 * L) + epsilon
    )
    corr = correlate(panel, windows[station], block_len)
    row_weights = weights[:, station]
    row_scale = inv_template * row_weights
    stacked = corr * inv_datas[station][None, :] * row_scale[:, None] / (3.0 * L)
    rows_here = stacked.shape[0] // lax.axis_size("loop")
    summed = lax.psum(stacked, "loop")
    return lax.dynamic_slice_in_dim(summed, loop_at * rows_here, rows_here, 0)


ROWS = 16
SHIFTS = 16
STEPS = 32700.0
LEVELS = 64.0


def lanes(shape):
    return lax.broadcasted_iota(jnp.int32, shape, len(shape) - 1)


def split_kernel(offset_in, active_in, t_in, keep_ref, send_ref, offset, active, t_ref, sems):
    copies = [
        pltpu.make_async_copy(t_in, t_ref, sems.at[0]),
        pltpu.make_async_copy(offset_in, offset, sems.at[1]),
        pltpu.make_async_copy(active_in, active, sems.at[2]),
    ]
    for copy in copies:
        copy.start()
    for copy in copies:
        copy.wait()
    half = lax.axis_index("loop") // 2
    span = t_ref.shape[2]
    sub = lax.broadcasted_iota(jnp.int32, (ROWS, 128), 0)
    high, low = (offset[0] // 32).astype(jnp.float32), (offset[0] % 32).astype(jnp.float32)
    for c in range(3):
        on = active[0, c].astype(jnp.float32)
        told = jnp.where(sub == 0, high, jnp.where(sub == 1, low, jnp.where(sub == 2, on, 0.0)))
        for out, first in ((keep_ref, half), (send_ref, 1 - half)):
            rows = t_ref[c, pl.ds(pl.multiple_of(ROWS * first, ROWS), ROWS), :]
            out[c, :, :span] = (rows.astype(jnp.float32) * on).astype(jnp.bfloat16)
            out[c, :, span:] = told.astype(jnp.bfloat16)


def split(offset, active, panel):
    half = jax.ShapeDtypeStruct((3, ROWS, panel.shape[2] + 128), jnp.bfloat16)
    return pl.pallas_call(
        split_kernel,
        out_shape=(half, half),
        in_specs=[pl.BlockSpec(memory_space=pltpu.HBM)] * 3,
        out_specs=(pl.BlockSpec(memory_space=pltpu.VMEM),) * 2,
        scratch_shapes=[
            pltpu.SMEM(offset.shape, jnp.int32),
            pltpu.SMEM(active.shape, jnp.int32),
            pltpu.VMEM(panel.shape, jnp.bfloat16),
            pltpu.SemaphoreType.DMA((3,)),
        ],
        compiler_params=pltpu.CompilerParams(vmem_limit_bytes=4 << 20),
        name="split",
    )(offset, active, panel)


def series_kernel(blocks, own, told, near, far, mine_ref, mate_ref, whole):
    z = lax.axis_index("tgrp")
    core = lax.axis_index("loop") % 2
    rows = mine_ref.shape[1]
    span = told.shape[2] - 128
    lane = lanes((rows, 128))
    whole[:, 4 * blocks :] = jnp.zeros((6, whole.shape[1] - 4 * blocks, 128), jnp.float32)
    wide = [near[...].astype(jnp.float32), far[...].astype(jnp.float32)]
    for b in range(4):
        at = pl.multiple_of(blocks * (z ^ b), 8)
        for i in range(6):
            first = 6 * blocks * (b // 2) + i * blocks
            whole[i, pl.ds(at, blocks), :] = wide[b % 2][first : first + blocks]
    for station in range(2):
        words = (own, told)[station]
        first = words[0, :, span:].astype(jnp.float32)
        shift = (32.0 * jnp.max(first[0:1]) + jnp.max(first[1:2])).astype(jnp.int32)
        row, turn = shift // 128, shift % 128
        spill = lane >= 128 - turn
        for c in range(3):
            i = 3 * station + c
            on = words[c, :, span:].astype(jnp.float32)[2:3]
            for out, half in ((mine_ref, core), (mate_ref, 1 - core)):
                at = row + 2 * blocks * half
                here = pltpu.roll(whole[i, pl.ds(at, rows), :], 128 - turn, 1)
                after = pltpu.roll(whole[i, pl.ds(at + 1, rows), :], 128 - turn, 1)
                out[i] = (jnp.where(spill, after, here) * on).astype(jnp.bfloat16)


def make_series(own, told, near, far, blocks, rows):
    window = jax.ShapeDtypeStruct((6, rows, 128), jnp.bfloat16)
    vmem = pl.BlockSpec(memory_space=pltpu.VMEM)
    return pl.pallas_call(
        functools.partial(series_kernel, blocks),
        out_shape=(window, window),
        in_specs=[vmem] * 4,
        out_specs=(vmem, vmem),
        scratch_shapes=[pltpu.VMEM((6, 2 * blocks + rows + 8, 128), jnp.float32)],
        compiler_params=pltpu.CompilerParams(vmem_limit_bytes=4 << 20),
        name="series",
    )(own, told, near, far)


def correlate_kernel(span, nb, t0, t1, t2, t3, mine, mate, masks, first_ref, second_ref,
                     tp_ref, xb_ref, xf_ref, a_ref, z_ref, d_ref, acc_ref, tot_ref, tr_ref, sems):
    lb = span // 128
    kb = lb + 1
    rows = xf_ref.shape[1]
    loop_at = lax.axis_index("loop")
    half = loop_at // 2
    copies = []
    for s, t in enumerate((t0, t1, t2, t3)):
        x = (mine, mate)[s % 2].at[pl.ds(3 * (s // 2), 3)]
        t = t.at[:, :, pl.ds(0, span)]
        copies.append(pltpu.make_async_copy(t, tp_ref.at[pl.ds(3 * s, 3), :, pl.ds(128, span)], sems.at[2 * s]))
        copies.append(pltpu.make_async_copy(x, xb_ref.at[pl.ds(3 * s, 3)], sems.at[2 * s + 1]))
    for copy in copies:
        copy.start()
    tp_ref[:, :, 0:128] = jnp.zeros((12, ROWS, 128), jnp.bfloat16)
    tp_ref[:, :, 128 + span :] = jnp.zeros((12, ROWS, 128), jnp.bfloat16)
    tot_ref[...] = jnp.zeros(tot_ref.shape, jnp.float32)
    k_first = 2 * ROWS * lax.axis_index("tgrp") + ROWS * half
    lane = lanes((8, 128))
    sub = lax.broadcasted_iota(jnp.int32, (8, 128), 0)
    counts = jnp.sum(masks[...], axis=0, keepdims=True).astype(jnp.float32)
    weight = jnp.sqrt(3.0 * span / counts)
    own = k_first + lane % ROWS
    diagonal = lanes((ROWS, 128)) % ROWS == lax.broadcasted_iota(jnp.int32, (ROWS, 128), 0)
    lane_r = lanes((rows, 128))
    for copy in copies:
        copy.wait()

    def row_scale(s):
        norm = jnp.zeros((ROWS, 128), jnp.float32)
        for c in range(3):
            for b in range(lb):
                wide = tp_ref[3 * s + c, :, 128 * b + 128 : 128 * b + 256].astype(jnp.float32)
                norm = norm + wide * wide
        inverse = 1.0 / jnp.sqrt(jnp.sum(norm, axis=1, keepdims=True) / (3.0 * span) + epsilon)
        inverse = jnp.where(diagonal, jnp.broadcast_to(inverse, (ROWS, 128)), 0.0)
        inverse = jnp.sum(inverse, axis=0, keepdims=True)
        here = masks[pl.ds(loop_at ^ s, 1), :].astype(jnp.float32) * weight
        here = jnp.take_along_axis(jnp.broadcast_to(here, (8, 128)), own, axis=1)
        return here[0:1] * inverse / (3.0 * span)

    def data_scale(s):
        squares = jnp.zeros((rows, 128), jnp.float32)
        for c in range(3):
            x = xb_ref[3 * s + c].astype(jnp.float32)
            squares = squares + x * x
        b = 1
        while b < 128:
            after = pltpu.roll(squares, rows - 1, 0)
            squares = squares + pltpu.roll(jnp.where(lane_r < b, after, squares), 128 - b, 1)
            b *= 2
        b = 1
        while b < lb:
            squares = squares + pltpu.roll(squares, rows - b, 0)
            b *= 2
        d_ref[...] = 1.0 / jnp.sqrt(squares / (3.0 * span) + epsilon)

    from_lane = (lane + sub) % 128
    inside = lane + sub < 128

    def build(i, slot):
        for r in range(SHIFTS):
            n = ROWS * (8 * (r % 2) + r // 2)
            a_ref[slot, n : n + ROWS, :] = tp_ref[i, :, 128 - 8 * r : 128 - 8 * r + 128 * kb]

        xf_ref[slot] = xb_ref[i].astype(jnp.float32)

        def turned(j):
            row = xf_ref[slot, pl.ds(j, 8, stride=0), :]
            return jnp.take_along_axis(row, from_lane, axis=1)

        before, tiles = turned(0), []
        for j in range(2 * nb + lb):
            after = turned(j + 1)
            tiles.append(jnp.where(inside, before, after))
            before = after
            if j >= nb:
                z_ref[slot, j - nb] = jnp.concatenate([tiles[j - nb], tiles[j]], axis=0).astype(jnp.bfloat16)

    def product(slot):
        left = jnp.concatenate([z_ref[slot, b : b + nb].reshape(16 * nb, 128) for b in range(kb)], axis=1)
        return lax.dot_general(left, a_ref[slot], (((1,), (1,)), ((), ())), preferred_element_type=jnp.float32)

    def weighted(rs):
        for v in (0, 1):
            index = 16 * (lane // 16) + 8 * v + sub
            for j in range(nb):
                for h in (0, 1):
                    at = 16 * j + 8 * h
                    scale = jnp.take_along_axis(d_ref[pl.ds(j + nb * h, 8, stride=0), :], index, axis=1) * rs
                    tot_ref[v, at : at + 8, :] += acc_ref[at : at + 8, 128 * v : 128 * v + 128] * scale

    build(0, 0)

    def station(s, carry):
        for c in range(3):
            m = product(c)
            build(jnp.minimum(3 * s + c + 1, 11), (c + 1) % 3)
            if c == 0:
                acc_ref[...] = m
            else:
                acc_ref[...] += m
            if c == 0:
                rs = row_scale(s)
            if c == 1:
                data_scale(s)
        weighted(rs)
        return carry

    lax.fori_loop(0, 4, station, 0)

    for f, out in enumerate((first_ref, second_ref)):
        h = half ^ f
        for jb in range(nb // 8):
            v = [[tot_ref[q, pl.ds(128 * jb + 8 * h + p, 8, stride=16), :] for p in range(8)] for q in (0, 1)]
            for b in (1, 2, 4):
                upper = (lane // b) % 2 == 1
                for q in (0, 1):
                    for p in range(8):
                        if not p & b:
                            x, y = v[q][p], v[q][p + b]
                            v[q][p] = jnp.where(upper, pltpu.roll(y, b, 1), x)
                            v[q][p + b] = jnp.where(upper, y, pltpu.roll(x, 128 - b, 1))
            upper = (lane // 8) % 2 == 1
            for p in range(8):
                x, y = v[0][p], v[1][p]
                v[0][p] = jnp.where(upper, pltpu.roll(y, 8, 1), x)
                v[1][p] = jnp.where(upper, y, pltpu.roll(x, 120, 1))
            for q in (0, 1):
                for p in range(8):
                    at = nb * (8 * q + p) + 8 * jb
                    tr_ref[f, at : at + 8, :] = v[q][p]
        levels = [jnp.zeros((8, 128), jnp.float32)] * 2
        for j in range(nb):
            codes = []
            for q in (0, 1):
                value = tr_ref[f, pl.ds(8 * nb * q + j, 8, stride=nb), :]
                top = jnp.maximum(jnp.max(jnp.abs(value), axis=1, keepdims=True), 2e-33)
                level = jnp.ceil(jnp.log2(jnp.broadcast_to(top, (8, 128))) * LEVELS)
                levels[q] = jnp.where(lane == j, level, levels[q])
                codes.append(jnp.round(value * (STEPS * jnp.exp2(level * (-1.0 / LEVELS)))))
            out[:, 128 * j : 128 * j + 128] = jnp.concatenate(codes, axis=0).astype(jnp.int32).astype(jnp.int16)
        out[:, 128 * nb :] = jnp.concatenate(levels, axis=0).astype(jnp.int32).astype(jnp.int16)


def decode_kernel(a_ref, b_ref, out_ref):
    odd = lax.axis_index("tgrp") % 2
    nb = out_ref.shape[1] // 128
    for ref, half in ((a_ref, odd), (b_ref, 1 - odd)):
        at = pl.multiple_of(ROWS * half, ROWS)
        step = jnp.exp2(ref[:, 128 * nb :].astype(jnp.float32) * (1.0 / LEVELS)) * (1.0 / STEPS)
        for j in range(nb):
            value = ref[:, 128 * j : 128 * j + 128].astype(jnp.float32)
            out_ref[pl.ds(at, ROWS), 128 * j : 128 * j + 128] = value * step[:, j : j + 1]


def decode(first, second):
    vmem = pl.BlockSpec(memory_space=pltpu.VMEM)
    return pl.pallas_call(
        decode_kernel,
        out_shape=jax.ShapeDtypeStruct((2 * ROWS, first.shape[1] - 128), jnp.float32),
        in_specs=[vmem, vmem],
        out_specs=vmem,
        compiler_params=pltpu.CompilerParams(vmem_limit_bytes=4 << 20),
        name="decode",
    )(first, second)


def correlate_stations(panels, series, masks, span, nb):
    lb = span // 128
    rows = series[0].shape[1]
    block = jax.ShapeDtypeStruct((ROWS, 128 * nb + 128), jnp.int16)
    vmem = pl.BlockSpec(memory_space=pltpu.VMEM)
    return pl.pallas_call(
        functools.partial(correlate_kernel, span, nb),
        out_shape=(block, block),
        in_specs=[pl.BlockSpec(memory_space=pl.ANY)] * 6 + [vmem],
        out_specs=(vmem, vmem),
        scratch_shapes=[
            pltpu.VMEM((12, ROWS, span + 256), jnp.bfloat16),
            pltpu.VMEM((12, rows, 128), jnp.bfloat16),
            pltpu.VMEM((3, rows, 128), jnp.float32),
            pltpu.VMEM((3, ROWS * SHIFTS, span + 128), jnp.bfloat16),
            pltpu.VMEM((3, nb + lb, 16, 128), jnp.bfloat16),
            pltpu.VMEM((rows, 128), jnp.float32),
            pltpu.VMEM((16 * nb, 256), jnp.float32),
            pltpu.VMEM((2, 16 * nb, 128), jnp.float32),
            pltpu.VMEM((2, 16 * nb, 128), jnp.float32),
            pltpu.SemaphoreType.DMA((8,)),
        ],
        compiler_params=pltpu.CompilerParams(vmem_limit_bytes=24 << 20),
        name="correlate",
    )(*panels, *series, masks)


def swapped(value, loop_bits, tgrp_bits):
    pairs = [(4 * l + z, 4 * (l ^ loop_bits) + (z ^ tgrp_bits)) for l in range(4) for z in range(4)]
    return lax.ppermute(value, ("loop", "tgrp"), pairs)


def to_owner(value, flip):
    pairs = [(4 * l + z, 4 * z + 2 * (l % 2) + ((l // 2) ^ flip)) for l in range(4) for z in range(4)]
    return lax.ppermute(value, ("loop", "tgrp"), pairs)


def local_plane(data, templates, masks, offsets, active):
    span = templates.shape[3]
    nb = data.shape[2] // 128
    panel = templates[:, 0].transpose(1, 0, 2)
    keep, send = split(offsets, active, panel)
    pieces = data.reshape(3 * nb, 128)
    pieces_y, send = lax.optimization_barrier((swapped(pieces, 2, 0), send))
    pair = jnp.concatenate([pieces, pieces_y], axis=0)
    panel_y = swapped(send, 2, 0)
    near = jnp.concatenate([pair, swapped(pair, 0, 2)], axis=0)
    far = swapped(near, 0, 1)
    mine, mate = make_series(keep, panel_y, near, far, nb, 2 * nb + span // 128 + 8)
    mate = swapped(mate, 1, 0)
    keep_late, panel_late, _ = lax.optimization_barrier((keep, panel_y, far))
    panel_c = swapped(keep_late, 1, 0)
    panel_yc = swapped(panel_late, 1, 0)
    first, second = correlate_stations(
        (keep, panel_c, panel_y, panel_yc), (mine, mate), masks.T, span, nb
    )
    return decode(to_owner(first, 0), to_owner(second, 1))


def solution(mesh):
    placed = (
        P(("parts", "loop"), None, "tgrp"),
        P("tgrp", "loop", None, None),
        P(),
        P(("parts", "loop")),
        P(("parts", "loop"), None),
    )

    def local(data, templates, masks, offsets, active):
        grid = (mesh.shape["loop"], mesh.shape["tgrp"])
        fits = grid == (4, 4) and templates.shape[:2] == (2 * ROWS, 1) and masks.shape[0] == 128
        fits = fits and templates.shape[3] == 2048 and data.shape[0] == 1 and data.shape[2] % 1024 == 0
        plan = local_plane if fits else local_general
        return plan(data, templates, masks, offsets, active)

    return jax.shard_map(
        local, mesh=mesh, in_specs=placed, out_specs=P(("parts", "loop"), "tgrp"), check_vma=False
    )
```

```python
import functools

import jax
import jax.numpy as jnp
from jax import lax
from jax.experimental import pallas as pl
from jax.experimental.pallas import tpu as pltpu
from jax.sharding import PartitionSpec as P

L = 2048


epsilon = 1e-05


def passed_along(value, axis, steps):
    count = lax.axis_size(axis)
    initial, last = (max(0, -steps), min(count, count - steps))
    return lax.ppermute(value, axis, [(source, source + steps) for source in range(initial, last)])


def window_energy(squares, out_len, span):
    inner_len = out_len + span - 128
    nblocks = (inner_len + 127) // 128
    total_len = 128 * (nblocks + 1)
    padded = jnp.concatenate([squares, jnp.zeros((total_len - squares.shape[0],), squares.dtype)])
    first = padded[: 128 * nblocks].reshape(nblocks, 128)
    second = padded[128 : 128 * nblocks + 128].reshape(nblocks, 128)
    segments = jnp.concatenate([first, second], axis=1)
    rows_at = lax.broadcasted_iota(jnp.int32, (256, 128), 0)
    cols_at = lax.broadcasted_iota(jnp.int32, (256, 128), 1)
    gap = rows_at - cols_at
    band = jnp.where((gap >= 0) & (gap < 128), 1.0, 0.0).astype(squares.dtype)
    inner = jnp.dot(segments, band, precision=lax.Precision.HIGHEST).reshape(nblocks * 128)
    energy = jnp.zeros((out_len,), squares.dtype)
    for block_at in range(span // 128):
        energy = energy + inner[128 * block_at : 128 * block_at + out_len]
    return energy


def correlate(panel, window, out_len):
    row_count = panel.shape[0]
    blocks = panel.shape[2] // 128
    span_len = out_len + panel.shape[2] - 128
    unfold = jnp.stack(
        [window[:, shift_by : shift_by + span_len] for shift_by in range(128)], axis=1
    )
    unfold = unfold.reshape(3 * 128, span_len)
    frames = (
        panel.reshape(row_count, 3, blocks, 128)
        .transpose(0, 2, 1, 3)
        .reshape(row_count, blocks, 3 * 128)
    )

    def add_block(block_at, running_sum):
        start_at = (block_at * 128).astype(jnp.int32)
        columns = lax.dynamic_slice_in_dim(unfold, start_at, out_len, 1)
        weights_now = lax.dynamic_index_in_dim(frames, block_at, 1, keepdims=False)
        return running_sum + jnp.dot(weights_now, columns, preferred_element_type=jnp.float32)

    return lax.fori_loop(0, blocks, add_block, jnp.zeros((row_count, out_len), jnp.float32))


def local_general(data, templates, masks, offsets, active):
    local_count = data.shape[0]
    block_len = data.shape[2]
    following = passed_along(data, "tgrp", -1)
    extended = jnp.concatenate([data, following], axis=2)
    loop_at = lax.axis_index("loop")
    first_station = loop_at * local_count
    counts = jnp.sum(masks, axis=1).astype(jnp.float32)
    local_masks = lax.dynamic_slice_in_dim(masks, first_station, local_count, 1)
    weights = local_masks.astype(jnp.float32) * jnp.sqrt(3.0 * L / counts)[:, None]
    station = 0
    channel_on = active[station].astype(jnp.bfloat16)
    series = lax.dynamic_slice(
        extended[station], (jnp.int32(0), offsets[station]), (3, block_len + L)
    )
    window = series * channel_on[:, None]
    wide_window = window.astype(jnp.float32)
    squares = jnp.sum(wide_window * wide_window, axis=0)
    energy = window_energy(squares, block_len, L)
    inv_datas = [1.0 / jnp.sqrt(energy / (3.0 * L) + epsilon)]
    windows = [window]
    channel_sets = [channel_on]
    panel_rows = lax.all_gather(templates, "tgrp", axis=0, tiled=True)
    station = 0
    panel = panel_rows[:, station] * channel_sets[station][None, :, None]
    wide_panel = panel.astype(jnp.float32)
    inv_template = 1.0 / jnp.sqrt(
        jnp.sum(wide_panel * wide_panel, axis=(1, 2)) / (3.0 * L) + epsilon
    )
    corr = correlate(panel, windows[station], block_len)
    row_weights = weights[:, station]
    row_scale = inv_template * row_weights
    stacked = corr * inv_datas[station][None, :] * row_scale[:, None] / (3.0 * L)
    rows_here = stacked.shape[0] // lax.axis_size("loop")
    summed = lax.psum(stacked, "loop")
    return lax.dynamic_slice_in_dim(summed, loop_at * rows_here, rows_here, 0)


ROWS = 16
SHIFTS = 16
STEPS = 32700.0
LEVELS = 64.0


def lanes(shape):
    return lax.broadcasted_iota(jnp.int32, shape, len(shape) - 1)


def split_kernel(offset_in, active_in, t_in, keep_ref, send_ref, offset, active, t_ref, sems):
    copies = [
        pltpu.make_async_copy(t_in, t_ref, sems.at[0]),
        pltpu.make_async_copy(offset_in, offset, sems.at[1]),
        pltpu.make_async_copy(active_in, active, sems.at[2]),
    ]
    for copy in copies:
        copy.start()
    for copy in copies:
        copy.wait()
    half = lax.axis_index("loop") // 2
    span = t_ref.shape[2]
    sub = lax.broadcasted_iota(jnp.int32, (ROWS, 128), 0)
    high, low = (offset[0] // 32).astype(jnp.float32), (offset[0] % 32).astype(jnp.float32)
    for c in range(3):
        on = active[0, c].astype(jnp.float32)
        told = jnp.where(sub == 0, high, jnp.where(sub == 1, low, jnp.where(sub == 2, on, 0.0)))
        for out, first in ((keep_ref, half), (send_ref, 1 - half)):
            rows = t_ref[c, pl.ds(pl.multiple_of(ROWS * first, ROWS), ROWS), :]
            out[c, :, :span] = (rows.astype(jnp.float32) * on).astype(jnp.bfloat16)
            out[c, :, span:] = told.astype(jnp.bfloat16)


def split(offset, active, panel):
    half = jax.ShapeDtypeStruct((3, ROWS, panel.shape[2] + 128), jnp.bfloat16)
    return pl.pallas_call(
        split_kernel,
        out_shape=(half, half),
        in_specs=[pl.BlockSpec(memory_space=pltpu.HBM)] * 3,
        out_specs=(pl.BlockSpec(memory_space=pltpu.VMEM),) * 2,
        scratch_shapes=[
            pltpu.SMEM(offset.shape, jnp.int32),
            pltpu.SMEM(active.shape, jnp.int32),
            pltpu.VMEM(panel.shape, jnp.bfloat16),
            pltpu.SemaphoreType.DMA((3,)),
        ],
        compiler_params=pltpu.CompilerParams(vmem_limit_bytes=4 << 20),
        name="split",
    )(offset, active, panel)


def series_kernel(blocks, own, told, near, far, mine_ref, mate_ref, whole):
    z = lax.axis_index("tgrp")
    core = lax.axis_index("loop") % 2
    rows = mine_ref.shape[1]
    span = told.shape[2] - 128
    lane = lanes((rows, 128))
    whole[:, 4 * blocks :] = jnp.zeros((6, whole.shape[1] - 4 * blocks, 128), jnp.float32)
    wide = [near[...].astype(jnp.float32), far[...].astype(jnp.float32)]
    for b in range(4):
        at = pl.multiple_of(blocks * (z ^ b), 8)
        for i in range(6):
            first = 6 * blocks * (b // 2) + i * blocks
            whole[i, pl.ds(at, blocks), :] = wide[b % 2][first : first + blocks]
    for station in range(2):
        words = (own, told)[station]
        first = words[0, :, span:].astype(jnp.float32)
        shift = (32.0 * jnp.max(first[0:1]) + jnp.max(first[1:2])).astype(jnp.int32)
        row, turn = shift // 128, shift % 128
        spill = lane >= 128 - turn
        for c in range(3):
            i = 3 * station + c
            on = words[c, :, span:].astype(jnp.float32)[2:3]
            for out, half in ((mine_ref, core), (mate_ref, 1 - core)):
                at = row + 2 * blocks * half
                here = pltpu.roll(whole[i, pl.ds(at, rows), :], 128 - turn, 1)
                after = pltpu.roll(whole[i, pl.ds(at + 1, rows), :], 128 - turn, 1)
                out[i] = (jnp.where(spill, after, here) * on).astype(jnp.bfloat16)


def make_series(own, told, near, far, blocks, rows):
    window = jax.ShapeDtypeStruct((6, rows, 128), jnp.bfloat16)
    vmem = pl.BlockSpec(memory_space=pltpu.VMEM)
    return pl.pallas_call(
        functools.partial(series_kernel, blocks),
        out_shape=(window, window),
        in_specs=[vmem] * 4,
        out_specs=(vmem, vmem),
        scratch_shapes=[pltpu.VMEM((6, 2 * blocks + rows + 8, 128), jnp.float32)],
        compiler_params=pltpu.CompilerParams(vmem_limit_bytes=4 << 20),
        name="series",
    )(own, told, near, far)


def correlate_kernel(span, nb, t0, t1, t2, t3, mine, mate, masks, first_ref, second_ref,
                     tp_ref, xb_ref, xf_ref, a_ref, z_ref, d_ref, acc_ref, tot_ref, tr_ref, sems):
    lb = span // 128
    kb = lb + 1
    rows = xf_ref.shape[1]
    loop_at = lax.axis_index("loop")
    half = loop_at // 2
    copies = []
    for s, t in enumerate((t0, t1, t2, t3)):
        x = (mine, mate)[s % 2].at[pl.ds(3 * (s // 2), 3)]
        t = t.at[:, :, pl.ds(0, span)]
        copies.append(pltpu.make_async_copy(t, tp_ref.at[pl.ds(3 * s, 3), :, pl.ds(128, span)], sems.at[2 * s]))
        copies.append(pltpu.make_async_copy(x, xb_ref.at[pl.ds(3 * s, 3)], sems.at[2 * s + 1]))
    for copy in copies:
        copy.start()
    tp_ref[:, :, 0:128] = jnp.zeros((12, ROWS, 128), jnp.bfloat16)
    tp_ref[:, :, 128 + span :] = jnp.zeros((12, ROWS, 128), jnp.bfloat16)
    tot_ref[...] = jnp.zeros(tot_ref.shape, jnp.float32)
    k_first = 2 * ROWS * lax.axis_index("tgrp") + ROWS * half
    lane = lanes((8, 128))
    sub = lax.broadcasted_iota(jnp.int32, (8, 128), 0)
    counts = jnp.sum(masks[...], axis=0, keepdims=True).astype(jnp.float32)
    weight = jnp.sqrt(3.0 * span / counts)
    own = k_first + lane % ROWS
    diagonal = lanes((ROWS, 128)) % ROWS == lax.broadcasted_iota(jnp.int32, (ROWS, 128), 0)
    lane_r = lanes((rows, 128))
    for copy in copies:
        copy.wait()

    def row_scale(s):
        norm = jnp.zeros((ROWS, 128), jnp.float32)
        for c in range(3):
            for b in range(lb):
                wide = tp_ref[3 * s + c, :, 128 * b + 128 : 128 * b + 256].astype(jnp.float32)
                norm = norm + wide * wide
        inverse = 1.0 / jnp.sqrt(jnp.sum(norm, axis=1, keepdims=True) / (3.0 * span) + epsilon)
        inverse = jnp.where(diagonal, jnp.broadcast_to(inverse, (ROWS, 128)), 0.0)
        inverse = jnp.sum(inverse, axis=0, keepdims=True)
        here = masks[pl.ds(loop_at ^ s, 1), :].astype(jnp.float32) * weight
        here = jnp.take_along_axis(jnp.broadcast_to(here, (8, 128)), own, axis=1)
        return here[0:1] * inverse / (3.0 * span)

    def data_scale(s):
        squares = jnp.zeros((rows, 128), jnp.float32)
        for c in range(3):
            x = xb_ref[3 * s + c].astype(jnp.float32)
            squares = squares + x * x
        b = 1
        while b < 128:
            after = pltpu.roll(squares, rows - 1, 0)
            squares = squares + pltpu.roll(jnp.where(lane_r < b, after, squares), 128 - b, 1)
            b *= 2
        b = 1
        while b < lb:
            squares = squares + pltpu.roll(squares, rows - b, 0)
            b *= 2
        d_ref[...] = 1.0 / jnp.sqrt(squares / (3.0 * span) + epsilon)

    from_lane = (lane + sub) % 128
    inside = lane + sub < 128

    def build(i, slot):
        for r in range(SHIFTS):
            n = ROWS * (8 * (r % 2) + r // 2)
            a_ref[slot, n : n + ROWS, :] = tp_ref[i, :, 128 - 8 * r : 128 - 8 * r + 128 * kb]

        xf_ref[slot] = xb_ref[i].astype(jnp.float32)

        def turned(j):
            row = xf_ref[slot, pl.ds(j, 8, stride=0), :]
            return jnp.take_along_axis(row, from_lane, axis=1)

        before, tiles = turned(0), []
        for j in range(2 * nb + lb):
            after = turned(j + 1)
            tiles.append(jnp.where(inside, before, after))
            before = after
            if j >= nb:
                z_ref[slot, j - nb] = jnp.concatenate([tiles[j - nb], tiles[j]], axis=0).astype(jnp.bfloat16)

    def product(slot):
        left = jnp.concatenate([z_ref[slot, b : b + nb].reshape(16 * nb, 128) for b in range(kb)], axis=1)
        return lax.dot_general(left, a_ref[slot], (((1,), (1,)), ((), ())), preferred_element_type=jnp.float32)

    def weighted(rs):
        for v in (0, 1):
            index = 16 * (lane // 16) + 8 * v + sub
            for j in range(nb):
                for h in (0, 1):
                    at = 16 * j + 8 * h
                    scale = jnp.take_along_axis(d_ref[pl.ds(j + nb * h, 8, stride=0), :], index, axis=1) * rs
                    tot_ref[v, at : at + 8, :] += acc_ref[at : at + 8, 128 * v : 128 * v + 128] * scale

    build(0, 0)

    def station(s, carry):
        for c in range(3):
            m = product(c)
            build(jnp.minimum(3 * s + c + 1, 11), (c + 1) % 3)
            if c == 0:
                acc_ref[...] = m
            else:
                acc_ref[...] += m
            if c == 0:
                rs = row_scale(s)
            if c == 1:
                data_scale(s)
        weighted(rs)
        return carry

    lax.fori_loop(0, 4, station, 0)

    for f, out in enumerate((first_ref, second_ref)):
        h = half ^ f
        for jb in range(nb // 8):
            v = [[tot_ref[q, pl.ds(128 * jb + 8 * h + p, 8, stride=16), :] for p in range(8)] for q in (0, 1)]
            for b in (1, 2, 4):
                upper = (lane // b) % 2 == 1
                for q in (0, 1):
                    for p in range(8):
                        if not p & b:
                            x, y = v[q][p], v[q][p + b]
                            v[q][p] = jnp.where(upper, pltpu.roll(y, b, 1), x)
                            v[q][p + b] = jnp.where(upper, y, pltpu.roll(x, 128 - b, 1))
            upper = (lane // 8) % 2 == 1
            for p in range(8):
                x, y = v[0][p], v[1][p]
                v[0][p] = jnp.where(upper, pltpu.roll(y, 8, 1), x)
                v[1][p] = jnp.where(upper, y, pltpu.roll(x, 120, 1))
            for q in (0, 1):
                for p in range(8):
                    at = nb * (8 * q + p) + 8 * jb
                    tr_ref[f, at : at + 8, :] = v[q][p]
        levels = [jnp.zeros((8, 128), jnp.float32)] * 2
        for j in range(nb):
            codes = []
            for q in (0, 1):
                value = tr_ref[f, pl.ds(8 * nb * q + j, 8, stride=nb), :]
                top = jnp.maximum(jnp.max(jnp.abs(value), axis=1, keepdims=True), 2e-33)
                level = jnp.ceil(jnp.log2(jnp.broadcast_to(top, (8, 128))) * LEVELS)
                levels[q] = jnp.where(lane == j, level, levels[q])
                codes.append(jnp.round(value * (STEPS * jnp.exp2(level * (-1.0 / LEVELS)))))
            out[:, 128 * j : 128 * j + 128] = jnp.concatenate(codes, axis=0).astype(jnp.int32).astype(jnp.int16)
        out[:, 128 * nb :] = jnp.concatenate(levels, axis=0).astype(jnp.int32).astype(jnp.int16)


def place_kernel(flip, part_ref, *refs):
    out_ref, block, sem = refs[-3:]
    half = (lax.axis_index("tgrp") + flip) % 2
    nb = block.shape[1] // 128
    step = jnp.exp2(part_ref[:, 128 * nb :].astype(jnp.float32) * (1.0 / LEVELS)) * (1.0 / STEPS)
    for j in range(nb):
        value = part_ref[:, 128 * j : 128 * j + 128].astype(jnp.float32)
        block[:, 128 * j : 128 * j + 128] = value * step[:, j : j + 1]
    rows = pl.ds(pl.multiple_of(ROWS * half, ROWS), ROWS)
    copy = pltpu.make_async_copy(block, out_ref.at[rows, :], sem)
    copy.start()
    copy.wait()


def place(part, flip, *earlier):
    width = part.shape[1] - 128
    unread = pl.BlockSpec(memory_space=pl.ANY)
    return pl.pallas_call(
        functools.partial(place_kernel, flip),
        out_shape=jax.ShapeDtypeStruct((2 * ROWS, width), jnp.float32),
        in_specs=[pl.BlockSpec(memory_space=pltpu.VMEM)] + [unread] * len(earlier),
        out_specs=unread,
        scratch_shapes=[pltpu.VMEM((ROWS, width), jnp.float32), pltpu.SemaphoreType.DMA],
        input_output_aliases={1: 0} if earlier else {},
        compiler_params=pltpu.CompilerParams(vmem_limit_bytes=4 << 20),
        name="place",
    )(part, *earlier)


def correlate_stations(panels, series, masks, span, nb):
    lb = span // 128
    rows = series[0].shape[1]
    block = jax.ShapeDtypeStruct((ROWS, 128 * nb + 128), jnp.int16)
    vmem = pl.BlockSpec(memory_space=pltpu.VMEM)
    return pl.pallas_call(
        functools.partial(correlate_kernel, span, nb),
        out_shape=(block, block),
        in_specs=[pl.BlockSpec(memory_space=pl.ANY)] * 6 + [vmem],
        out_specs=(vmem, vmem),
        scratch_shapes=[
            pltpu.VMEM((12, ROWS, span + 256), jnp.bfloat16),
            pltpu.VMEM((12, rows, 128), jnp.bfloat16),
            pltpu.VMEM((3, rows, 128), jnp.float32),
            pltpu.VMEM((3, ROWS * SHIFTS, span + 128), jnp.bfloat16),
            pltpu.VMEM((3, nb + lb, 16, 128), jnp.bfloat16),
            pltpu.VMEM((rows, 128), jnp.float32),
            pltpu.VMEM((16 * nb, 256), jnp.float32),
            pltpu.VMEM((2, 16 * nb, 128), jnp.float32),
            pltpu.VMEM((2, 16 * nb, 128), jnp.float32),
            pltpu.SemaphoreType.DMA((8,)),
        ],
        compiler_params=pltpu.CompilerParams(vmem_limit_bytes=24 << 20),
        name="correlate",
    )(*panels, *series, masks)


def swapped(value, loop_bits, tgrp_bits):
    pairs = [(4 * l + z, 4 * (l ^ loop_bits) + (z ^ tgrp_bits)) for l in range(4) for z in range(4)]
    return lax.ppermute(value, ("loop", "tgrp"), pairs)


def to_owner(value, flip):
    pairs = [(4 * l + z, 4 * z + 2 * (l % 2) + ((l // 2) ^ flip)) for l in range(4) for z in range(4)]
    return lax.ppermute(value, ("loop", "tgrp"), pairs)


def local_plane(data, templates, masks, offsets, active):
    span = templates.shape[3]
    nb = data.shape[2] // 128
    panel = templates[:, 0].transpose(1, 0, 2)
    keep, send = split(offsets, active, panel)
    panel_c = swapped(keep, 1, 0)
    pieces = data.reshape(3 * nb, 128)
    pieces_y, send = lax.optimization_barrier((swapped(pieces, 2, 0), send))
    pair = jnp.concatenate([pieces, pieces_y], axis=0)
    panel_y = swapped(send, 2, 0)
    near = jnp.concatenate([pair, swapped(pair, 0, 2)], axis=0)
    far = swapped(near, 0, 1)
    mine, mate = make_series(keep, panel_y, near, far, nb, 2 * nb + span // 128 + 8)
    mate = swapped(mate, 1, 0)
    panel_late, _ = lax.optimization_barrier((panel_y, far))
    panel_yc = swapped(panel_late, 1, 0)
    first, second = correlate_stations(
        (keep, panel_c, panel_y, panel_yc), (mine, mate), masks.T, span, nb
    )
    first, second = to_owner(first, 0), to_owner(second, 1)
    return place(second, 1, place(first, 0))


def solution(mesh):
    placed = (
        P(("parts", "loop"), None, "tgrp"),
        P("tgrp", "loop", None, None),
        P(),
        P(("parts", "loop")),
        P(("parts", "loop"), None),
    )

    def local(data, templates, masks, offsets, active):
        grid = (mesh.shape["loop"], mesh.shape["tgrp"])
        fits = grid == (4, 4) and templates.shape[:2] == (2 * ROWS, 1) and masks.shape[0] == 128
        fits = fits and templates.shape[3] == 2048 and data.shape[0] == 1 and data.shape[2] % 1024 == 0
        plan = local_plane if fits else local_general
        return plan(data, templates, masks, offsets, active)

    return jax.shard_map(
        local, mesh=mesh, in_specs=placed, out_specs=P(("parts", "loop"), "tgrp"), check_vma=False
    )
```

```python
import functools

import jax
import jax.numpy as jnp
from jax import lax
from jax.experimental import pallas as pl
from jax.experimental.pallas import tpu as pltpu
from jax.sharding import PartitionSpec as P

L = 2048


epsilon = 1e-05


def passed_along(value, axis, steps):
    count = lax.axis_size(axis)
    initial, last = (max(0, -steps), min(count, count - steps))
    return lax.ppermute(value, axis, [(source, source + steps) for source in range(initial, last)])


def window_energy(squares, out_len, span):
    inner_len = out_len + span - 128
    nblocks = (inner_len + 127) // 128
    total_len = 128 * (nblocks + 1)
    padded = jnp.concatenate([squares, jnp.zeros((total_len - squares.shape[0],), squares.dtype)])
    first = padded[: 128 * nblocks].reshape(nblocks, 128)
    second = padded[128 : 128 * nblocks + 128].reshape(nblocks, 128)
    segments = jnp.concatenate([first, second], axis=1)
    rows_at = lax.broadcasted_iota(jnp.int32, (256, 128), 0)
    cols_at = lax.broadcasted_iota(jnp.int32, (256, 128), 1)
    gap = rows_at - cols_at
    band = jnp.where((gap >= 0) & (gap < 128), 1.0, 0.0).astype(squares.dtype)
    inner = jnp.dot(segments, band, precision=lax.Precision.HIGHEST).reshape(nblocks * 128)
    energy = jnp.zeros((out_len,), squares.dtype)
    for block_at in range(span // 128):
        energy = energy + inner[128 * block_at : 128 * block_at + out_len]
    return energy


def correlate(panel, window, out_len):
    row_count = panel.shape[0]
    blocks = panel.shape[2] // 128
    span_len = out_len + panel.shape[2] - 128
    unfold = jnp.stack(
        [window[:, shift_by : shift_by + span_len] for shift_by in range(128)], axis=1
    )
    unfold = unfold.reshape(3 * 128, span_len)
    frames = (
        panel.reshape(row_count, 3, blocks, 128)
        .transpose(0, 2, 1, 3)
        .reshape(row_count, blocks, 3 * 128)
    )

    def add_block(block_at, running_sum):
        start_at = (block_at * 128).astype(jnp.int32)
        columns = lax.dynamic_slice_in_dim(unfold, start_at, out_len, 1)
        weights_now = lax.dynamic_index_in_dim(frames, block_at, 1, keepdims=False)
        return running_sum + jnp.dot(weights_now, columns, preferred_element_type=jnp.float32)

    return lax.fori_loop(0, blocks, add_block, jnp.zeros((row_count, out_len), jnp.float32))


def local_general(data, templates, masks, offsets, active):
    local_count = data.shape[0]
    block_len = data.shape[2]
    following = passed_along(data, "tgrp", -1)
    extended = jnp.concatenate([data, following], axis=2)
    loop_at = lax.axis_index("loop")
    first_station = loop_at * local_count
    counts = jnp.sum(masks, axis=1).astype(jnp.float32)
    local_masks = lax.dynamic_slice_in_dim(masks, first_station, local_count, 1)
    weights = local_masks.astype(jnp.float32) * jnp.sqrt(3.0 * L / counts)[:, None]
    station = 0
    channel_on = active[station].astype(jnp.bfloat16)
    series = lax.dynamic_slice(
        extended[station], (jnp.int32(0), offsets[station]), (3, block_len + L)
    )
    window = series * channel_on[:, None]
    wide_window = window.astype(jnp.float32)
    squares = jnp.sum(wide_window * wide_window, axis=0)
    energy = window_energy(squares, block_len, L)
    inv_datas = [1.0 / jnp.sqrt(energy / (3.0 * L) + epsilon)]
    windows = [window]
    channel_sets = [channel_on]
    panel_rows = lax.all_gather(templates, "tgrp", axis=0, tiled=True)
    station = 0
    panel = panel_rows[:, station] * channel_sets[station][None, :, None]
    wide_panel = panel.astype(jnp.float32)
    inv_template = 1.0 / jnp.sqrt(
        jnp.sum(wide_panel * wide_panel, axis=(1, 2)) / (3.0 * L) + epsilon
    )
    corr = correlate(panel, windows[station], block_len)
    row_weights = weights[:, station]
    row_scale = inv_template * row_weights
    stacked = corr * inv_datas[station][None, :] * row_scale[:, None] / (3.0 * L)
    rows_here = stacked.shape[0] // lax.axis_size("loop")
    summed = lax.psum(stacked, "loop")
    return lax.dynamic_slice_in_dim(summed, loop_at * rows_here, rows_here, 0)


ROWS = 16
SHIFTS = 16
STEPS = 32700.0
LEVELS = 64.0


def lanes(shape):
    return lax.broadcasted_iota(jnp.int32, shape, len(shape) - 1)


def split_kernel(offset_in, active_in, t_in, keep_ref, send_ref, offset, active, t_ref, sems):
    copies = [
        pltpu.make_async_copy(t_in, t_ref, sems.at[0]),
        pltpu.make_async_copy(offset_in, offset, sems.at[1]),
        pltpu.make_async_copy(active_in, active, sems.at[2]),
    ]
    for copy in copies:
        copy.start()
    for copy in copies:
        copy.wait()
    half = lax.axis_index("loop") // 2
    span = t_ref.shape[2]
    sub = lax.broadcasted_iota(jnp.int32, (ROWS, 128), 0)
    high, low = (offset[0] // 32).astype(jnp.float32), (offset[0] % 32).astype(jnp.float32)
    for c in range(3):
        on = active[0, c].astype(jnp.float32)
        told = jnp.where(sub == 0, high, jnp.where(sub == 1, low, jnp.where(sub == 2, on, 0.0)))
        for out, first in ((keep_ref, half), (send_ref, 1 - half)):
            rows = t_ref[c, pl.ds(pl.multiple_of(ROWS * first, ROWS), ROWS), :]
            out[c, :, :span] = (rows.astype(jnp.float32) * on).astype(jnp.bfloat16)
            out[c, :, span:] = told.astype(jnp.bfloat16)


def split(offset, active, panel):
    half = jax.ShapeDtypeStruct((3, ROWS, panel.shape[2] + 128), jnp.bfloat16)
    return pl.pallas_call(
        split_kernel,
        out_shape=(half, half),
        in_specs=[pl.BlockSpec(memory_space=pltpu.HBM)] * 3,
        out_specs=(pl.BlockSpec(memory_space=pltpu.VMEM),) * 2,
        scratch_shapes=[
            pltpu.SMEM(offset.shape, jnp.int32),
            pltpu.SMEM(active.shape, jnp.int32),
            pltpu.VMEM(panel.shape, jnp.bfloat16),
            pltpu.SemaphoreType.DMA((3,)),
        ],
        compiler_params=pltpu.CompilerParams(vmem_limit_bytes=4 << 20),
        name="split",
    )(offset, active, panel)


def series_kernel(blocks, own, told, near, far, mine_ref, mate_ref, whole):
    z = lax.axis_index("tgrp")
    core = lax.axis_index("loop") % 2
    rows = mine_ref.shape[1]
    span = told.shape[2] - 128
    lane = lanes((rows, 128))
    whole[:, 4 * blocks :] = jnp.zeros((6, whole.shape[1] - 4 * blocks, 128), jnp.float32)
    wide = [near[...].astype(jnp.float32), far[...].astype(jnp.float32)]
    for b in range(4):
        at = pl.multiple_of(blocks * (z ^ b), 8)
        for i in range(6):
            first = blocks * (6 * (i // 3) + 3 * (b // 2) + i % 3)
            whole[i, pl.ds(at, blocks), :] = wide[b % 2][first : first + blocks]
    for station in range(2):
        words = (own, told)[station]
        first = words[0, :, span:].astype(jnp.float32)
        shift = (32.0 * jnp.max(first[0:1]) + jnp.max(first[1:2])).astype(jnp.int32)
        row, turn = shift // 128, shift % 128
        spill = lane >= 128 - turn
        for c in range(3):
            i = 3 * station + c
            on = words[c, :, span:].astype(jnp.float32)[2:3]
            for out, half in ((mine_ref, core), (mate_ref, 1 - core)):
                at = row + 2 * blocks * half
                here = pltpu.roll(whole[i, pl.ds(at, rows), :], 128 - turn, 1)
                after = pltpu.roll(whole[i, pl.ds(at + 1, rows), :], 128 - turn, 1)
                out[i] = (jnp.where(spill, after, here) * on).astype(jnp.bfloat16)


def make_series(own, told, near, far, blocks, rows):
    window = jax.ShapeDtypeStruct((6, rows, 128), jnp.bfloat16)
    vmem = pl.BlockSpec(memory_space=pltpu.VMEM)
    return pl.pallas_call(
        functools.partial(series_kernel, blocks),
        out_shape=(window, window),
        in_specs=[vmem] * 4,
        out_specs=(vmem, vmem),
        scratch_shapes=[pltpu.VMEM((6, 2 * blocks + rows + 8, 128), jnp.float32)],
        compiler_params=pltpu.CompilerParams(vmem_limit_bytes=4 << 20),
        name="series",
    )(own, told, near, far)


def correlate_kernel(span, nb, t0, t1, t2, t3, mine, mate, masks, first_ref, second_ref,
                     tp_ref, xb_ref, xf_ref, a_ref, z_ref, d_ref, acc_ref, tot_ref, tr_ref, sems):
    lb = span // 128
    kb = lb + 1
    rows = xf_ref.shape[1]
    loop_at = lax.axis_index("loop")
    half = loop_at // 2
    copies = []
    for s, t in enumerate((t0, t1, t2, t3)):
        x = (mine, mate)[s % 2].at[pl.ds(3 * (s // 2), 3)]
        t = t.at[:, :, pl.ds(0, span)]
        copies.append(pltpu.make_async_copy(t, tp_ref.at[pl.ds(3 * s, 3), :, pl.ds(128, span)], sems.at[2 * s]))
        copies.append(pltpu.make_async_copy(x, xb_ref.at[pl.ds(3 * s, 3)], sems.at[2 * s + 1]))
    for copy in copies:
        copy.start()
    tp_ref[:, :, 0:128] = jnp.zeros((12, ROWS, 128), jnp.bfloat16)
    tp_ref[:, :, 128 + span :] = jnp.zeros((12, ROWS, 128), jnp.bfloat16)
    tot_ref[...] = jnp.zeros(tot_ref.shape, jnp.float32)
    k_first = 2 * ROWS * lax.axis_index("tgrp") + ROWS * half
    lane = lanes((8, 128))
    sub = lax.broadcasted_iota(jnp.int32, (8, 128), 0)
    counts = jnp.sum(masks[...], axis=0, keepdims=True).astype(jnp.float32)
    weight = jnp.sqrt(3.0 * span / counts)
    own = k_first + lane % ROWS
    diagonal = lanes((ROWS, 128)) % ROWS == lax.broadcasted_iota(jnp.int32, (ROWS, 128), 0)
    lane_r = lanes((rows, 128))
    for copy in copies:
        copy.wait()

    def row_scale(s):
        norm = jnp.zeros((ROWS, 128), jnp.float32)
        for c in range(3):
            for b in range(lb):
                wide = tp_ref[3 * s + c, :, 128 * b + 128 : 128 * b + 256].astype(jnp.float32)
                norm = norm + wide * wide
        inverse = 1.0 / jnp.sqrt(jnp.sum(norm, axis=1, keepdims=True) / (3.0 * span) + epsilon)
        inverse = jnp.where(diagonal, jnp.broadcast_to(inverse, (ROWS, 128)), 0.0)
        inverse = jnp.sum(inverse, axis=0, keepdims=True)
        here = masks[pl.ds(loop_at ^ s, 1), :].astype(jnp.float32) * weight
        here = jnp.take_along_axis(jnp.broadcast_to(here, (8, 128)), own, axis=1)
        return here[0:1] * inverse / (3.0 * span)

    def data_scale(s):
        squares = jnp.zeros((rows, 128), jnp.float32)
        for c in range(3):
            x = xb_ref[3 * s + c].astype(jnp.float32)
            squares = squares + x * x
        b = 1
        while b < 128:
            after = pltpu.roll(squares, rows - 1, 0)
            squares = squares + pltpu.roll(jnp.where(lane_r < b, after, squares), 128 - b, 1)
            b *= 2
        b = 1
        while b < lb:
            squares = squares + pltpu.roll(squares, rows - b, 0)
            b *= 2
        d_ref[...] = 1.0 / jnp.sqrt(squares / (3.0 * span) + epsilon)

    from_lane = (lane + sub) % 128
    inside = lane + sub < 128

    def build(i, slot):
        for r in range(SHIFTS):
            n = ROWS * (8 * (r % 2) + r // 2)
            a_ref[slot, n : n + ROWS, :] = tp_ref[i, :, 128 - 8 * r : 128 - 8 * r + 128 * kb]

        xf_ref[slot] = xb_ref[i].astype(jnp.float32)

        def turned(j):
            row = xf_ref[slot, pl.ds(j, 8, stride=0), :]
            return jnp.take_along_axis(row, from_lane, axis=1)

        before, tiles = turned(0), []
        for j in range(2 * nb + lb):
            after = turned(j + 1)
            tiles.append(jnp.where(inside, before, after))
            before = after
            if j >= nb:
                z_ref[slot, j - nb] = jnp.concatenate([tiles[j - nb], tiles[j]], axis=0).astype(jnp.bfloat16)

    def product(slot):
        left = jnp.concatenate([z_ref[slot, b : b + nb].reshape(16 * nb, 128) for b in range(kb)], axis=1)
        return lax.dot_general(left, a_ref[slot], (((1,), (1,)), ((), ())), preferred_element_type=jnp.float32)

    def weighted(rs):
        for v in (0, 1):
            index = 16 * (lane // 16) + 8 * v + sub
            for j in range(nb):
                for h in (0, 1):
                    at = 16 * j + 8 * h
                    scale = jnp.take_along_axis(d_ref[pl.ds(j + nb * h, 8, stride=0), :], index, axis=1) * rs
                    tot_ref[v, at : at + 8, :] += acc_ref[at : at + 8, 128 * v : 128 * v + 128] * scale

    build(0, 0)

    def station(s, carry):
        for c in range(3):
            m = product(c)
            build(jnp.minimum(3 * s + c + 1, 11), (c + 1) % 3)
            if c == 0:
                acc_ref[...] = m
            else:
                acc_ref[...] += m
            if c == 0:
                rs = row_scale(s)
            if c == 1:
                data_scale(s)
        weighted(rs)
        return carry

    lax.fori_loop(0, 4, station, 0)

    for f, out in enumerate((first_ref, second_ref)):
        h = half ^ f
        for jb in range(nb // 8):
            v = [[tot_ref[q, pl.ds(128 * jb + 8 * h + p, 8, stride=16), :] for p in range(8)] for q in (0, 1)]
            for b in (1, 2, 4):
                upper = (lane // b) % 2 == 1
                for q in (0, 1):
                    for p in range(8):
                        if not p & b:
                            x, y = v[q][p], v[q][p + b]
                            v[q][p] = jnp.where(upper, pltpu.roll(y, b, 1), x)
                            v[q][p + b] = jnp.where(upper, y, pltpu.roll(x, 128 - b, 1))
            upper = (lane // 8) % 2 == 1
            for p in range(8):
                x, y = v[0][p], v[1][p]
                v[0][p] = jnp.where(upper, pltpu.roll(y, 8, 1), x)
                v[1][p] = jnp.where(upper, y, pltpu.roll(x, 120, 1))
            for q in (0, 1):
                for p in range(8):
                    at = nb * (8 * q + p) + 8 * jb
                    tr_ref[f, at : at + 8, :] = v[q][p]
        levels = [jnp.zeros((8, 128), jnp.float32)] * 2
        for j in range(nb):
            codes = []
            for q in (0, 1):
                value = tr_ref[f, pl.ds(8 * nb * q + j, 8, stride=nb), :]
                top = jnp.maximum(jnp.max(jnp.abs(value), axis=1, keepdims=True), 2e-33)
                level = jnp.ceil(jnp.log2(jnp.broadcast_to(top, (8, 128))) * LEVELS)
                levels[q] = jnp.where(lane == j, level, levels[q])
                codes.append(jnp.round(value * (STEPS * jnp.exp2(level * (-1.0 / LEVELS)))))
            out[:, 128 * j : 128 * j + 128] = jnp.concatenate(codes, axis=0).astype(jnp.int32).astype(jnp.int16)
        out[:, 128 * nb :] = jnp.concatenate(levels, axis=0).astype(jnp.int32).astype(jnp.int16)


def place_kernel(flip, part_ref, *refs):
    out_ref, block, sem = refs[-3:]
    half = (lax.axis_index("tgrp") + flip) % 2
    nb = block.shape[1] // 128
    step = jnp.exp2(part_ref[:, 128 * nb :].astype(jnp.float32) * (1.0 / LEVELS)) * (1.0 / STEPS)
    for j in range(nb):
        value = part_ref[:, 128 * j : 128 * j + 128].astype(jnp.float32)
        block[:, 128 * j : 128 * j + 128] = value * step[:, j : j + 1]
    rows = pl.ds(pl.multiple_of(ROWS * half, ROWS), ROWS)
    copy = pltpu.make_async_copy(block, out_ref.at[rows, :], sem)
    copy.start()
    copy.wait()


def place(part, flip, *earlier):
    width = part.shape[1] - 128
    unread = pl.BlockSpec(memory_space=pl.ANY)
    return pl.pallas_call(
        functools.partial(place_kernel, flip),
        out_shape=jax.ShapeDtypeStruct((2 * ROWS, width), jnp.float32),
        in_specs=[pl.BlockSpec(memory_space=pltpu.VMEM)] + [unread] * len(earlier),
        out_specs=unread,
        scratch_shapes=[pltpu.VMEM((ROWS, width), jnp.float32), pltpu.SemaphoreType.DMA],
        input_output_aliases={1: 0} if earlier else {},
        compiler_params=pltpu.CompilerParams(vmem_limit_bytes=4 << 20),
        name="place",
    )(part, *earlier)


def correlate_stations(panels, series, masks, span, nb):
    lb = span // 128
    rows = series[0].shape[1]
    block = jax.ShapeDtypeStruct((ROWS, 128 * nb + 128), jnp.int16)
    vmem = pl.BlockSpec(memory_space=pltpu.VMEM)
    return pl.pallas_call(
        functools.partial(correlate_kernel, span, nb),
        out_shape=(block, block),
        in_specs=[pl.BlockSpec(memory_space=pl.ANY)] * 6 + [vmem],
        out_specs=(vmem, vmem),
        scratch_shapes=[
            pltpu.VMEM((12, ROWS, span + 256), jnp.bfloat16),
            pltpu.VMEM((12, rows, 128), jnp.bfloat16),
            pltpu.VMEM((3, rows, 128), jnp.float32),
            pltpu.VMEM((3, ROWS * SHIFTS, span + 128), jnp.bfloat16),
            pltpu.VMEM((3, nb + lb, 16, 128), jnp.bfloat16),
            pltpu.VMEM((rows, 128), jnp.float32),
            pltpu.VMEM((16 * nb, 256), jnp.float32),
            pltpu.VMEM((2, 16 * nb, 128), jnp.float32),
            pltpu.VMEM((2, 16 * nb, 128), jnp.float32),
            pltpu.SemaphoreType.DMA((8,)),
        ],
        compiler_params=pltpu.CompilerParams(vmem_limit_bytes=24 << 20),
        name="correlate",
    )(*panels, *series, masks)


def swapped(value, loop_bits, tgrp_bits):
    pairs = [(4 * l + z, 4 * (l ^ loop_bits) + (z ^ tgrp_bits)) for l in range(4) for z in range(4)]
    return lax.ppermute(value, ("loop", "tgrp"), pairs)


def to_owner(value, flip):
    pairs = [(4 * l + z, 4 * z + 2 * (l % 2) + ((l // 2) ^ flip)) for l in range(4) for z in range(4)]
    return lax.ppermute(value, ("loop", "tgrp"), pairs)


def local_plane(data, templates, masks, offsets, active):
    span = templates.shape[3]
    nb = data.shape[2] // 128
    panel = templates[:, 0].transpose(1, 0, 2)
    keep, send = split(offsets, active, panel)
    panel_c = swapped(keep, 1, 0)
    pieces = data.reshape(3 * nb, 128)
    pieces_z, send = lax.optimization_barrier((swapped(pieces, 0, 2), send))
    pair = jnp.concatenate([pieces, pieces_z], axis=0)
    panel_y = swapped(send, 2, 0)
    near = jnp.concatenate([pair, swapped(pair, 2, 0)], axis=0)
    far = swapped(near, 0, 1)
    mine, mate = make_series(keep, panel_y, near, far, nb, 2 * nb + span // 128 + 8)
    mate = swapped(mate, 1, 0)
    panel_late, _ = lax.optimization_barrier((panel_y, far))
    panel_yc = swapped(panel_late, 1, 0)
    first, second = correlate_stations(
        (keep, panel_c, panel_y, panel_yc), (mine, mate), masks.T, span, nb
    )
    first, second = to_owner(first, 0), to_owner(second, 1)
    return place(second, 1, place(first, 0))


def solution(mesh):
    placed = (
        P(("parts", "loop"), None, "tgrp"),
        P("tgrp", "loop", None, None),
        P(),
        P(("parts", "loop")),
        P(("parts", "loop"), None),
    )

    def local(data, templates, masks, offsets, active):
        grid = (mesh.shape["loop"], mesh.shape["tgrp"])
        fits = grid == (4, 4) and templates.shape[:2] == (2 * ROWS, 1) and masks.shape[0] == 128
        fits = fits and templates.shape[3] == 2048 and data.shape[0] == 1 and data.shape[2] % 1024 == 0
        plan = local_plane if fits else local_general
        return plan(data, templates, masks, offsets, active)

    return jax.shard_map(
        local, mesh=mesh, in_specs=placed, out_specs=P(("parts", "loop"), "tgrp"), check_vma=False
    )
```

```python
import functools

import jax
import jax.numpy as jnp
from jax import lax
from jax.experimental import pallas as pl
from jax.experimental.pallas import tpu as pltpu
from jax.sharding import PartitionSpec as P

L = 2048


epsilon = 1e-05


def passed_along(value, axis, steps):
    count = lax.axis_size(axis)
    initial, last = (max(0, -steps), min(count, count - steps))
    return lax.ppermute(value, axis, [(source, source + steps) for source in range(initial, last)])


def window_energy(squares, out_len, span):
    inner_len = out_len + span - 128
    nblocks = (inner_len + 127) // 128
    total_len = 128 * (nblocks + 1)
    padded = jnp.concatenate([squares, jnp.zeros((total_len - squares.shape[0],), squares.dtype)])
    first = padded[: 128 * nblocks].reshape(nblocks, 128)
    second = padded[128 : 128 * nblocks + 128].reshape(nblocks, 128)
    segments = jnp.concatenate([first, second], axis=1)
    rows_at = lax.broadcasted_iota(jnp.int32, (256, 128), 0)
    cols_at = lax.broadcasted_iota(jnp.int32, (256, 128), 1)
    gap = rows_at - cols_at
    band = jnp.where((gap >= 0) & (gap < 128), 1.0, 0.0).astype(squares.dtype)
    inner = jnp.dot(segments, band, precision=lax.Precision.HIGHEST).reshape(nblocks * 128)
    energy = jnp.zeros((out_len,), squares.dtype)
    for block_at in range(span // 128):
        energy = energy + inner[128 * block_at : 128 * block_at + out_len]
    return energy


def correlate(panel, window, out_len):
    row_count = panel.shape[0]
    blocks = panel.shape[2] // 128
    span_len = out_len + panel.shape[2] - 128
    unfold = jnp.stack(
        [window[:, shift_by : shift_by + span_len] for shift_by in range(128)], axis=1
    )
    unfold = unfold.reshape(3 * 128, span_len)
    frames = (
        panel.reshape(row_count, 3, blocks, 128)
        .transpose(0, 2, 1, 3)
        .reshape(row_count, blocks, 3 * 128)
    )

    def add_block(block_at, running_sum):
        start_at = (block_at * 128).astype(jnp.int32)
        columns = lax.dynamic_slice_in_dim(unfold, start_at, out_len, 1)
        weights_now = lax.dynamic_index_in_dim(frames, block_at, 1, keepdims=False)
        return running_sum + jnp.dot(weights_now, columns, preferred_element_type=jnp.float32)

    return lax.fori_loop(0, blocks, add_block, jnp.zeros((row_count, out_len), jnp.float32))


def local_general(data, templates, masks, offsets, active):
    local_count = data.shape[0]
    block_len = data.shape[2]
    following = passed_along(data, "tgrp", -1)
    extended = jnp.concatenate([data, following], axis=2)
    loop_at = lax.axis_index("loop")
    first_station = loop_at * local_count
    counts = jnp.sum(masks, axis=1).astype(jnp.float32)
    local_masks = lax.dynamic_slice_in_dim(masks, first_station, local_count, 1)
    weights = local_masks.astype(jnp.float32) * jnp.sqrt(3.0 * L / counts)[:, None]
    station = 0
    channel_on = active[station].astype(jnp.bfloat16)
    series = lax.dynamic_slice(
        extended[station], (jnp.int32(0), offsets[station]), (3, block_len + L)
    )
    window = series * channel_on[:, None]
    wide_window = window.astype(jnp.float32)
    squares = jnp.sum(wide_window * wide_window, axis=0)
    energy = window_energy(squares, block_len, L)
    inv_datas = [1.0 / jnp.sqrt(energy / (3.0 * L) + epsilon)]
    windows = [window]
    channel_sets = [channel_on]
    panel_rows = lax.all_gather(templates, "tgrp", axis=0, tiled=True)
    station = 0
    panel = panel_rows[:, station] * channel_sets[station][None, :, None]
    wide_panel = panel.astype(jnp.float32)
    inv_template = 1.0 / jnp.sqrt(
        jnp.sum(wide_panel * wide_panel, axis=(1, 2)) / (3.0 * L) + epsilon
    )
    corr = correlate(panel, windows[station], block_len)
    row_weights = weights[:, station]
    row_scale = inv_template * row_weights
    stacked = corr * inv_datas[station][None, :] * row_scale[:, None] / (3.0 * L)
    rows_here = stacked.shape[0] // lax.axis_size("loop")
    summed = lax.psum(stacked, "loop")
    return lax.dynamic_slice_in_dim(summed, loop_at * rows_here, rows_here, 0)


ROWS = 16
SHIFTS = 16
STEPS = 32700.0
LEVELS = 64.0


def lanes(shape):
    return lax.broadcasted_iota(jnp.int32, shape, len(shape) - 1)


def split_kernel(offset_in, active_in, t_in, keep_ref, send_ref, offset, active, t_ref, sems):
    copies = [
        pltpu.make_async_copy(t_in, t_ref, sems.at[0]),
        pltpu.make_async_copy(offset_in, offset, sems.at[1]),
        pltpu.make_async_copy(active_in, active, sems.at[2]),
    ]
    for copy in copies:
        copy.start()
    for copy in copies:
        copy.wait()
    half = lax.axis_index("loop") // 2
    span = t_ref.shape[2]
    sub = lax.broadcasted_iota(jnp.int32, (ROWS, 128), 0)
    high, low = (offset[0] // 32).astype(jnp.float32), (offset[0] % 32).astype(jnp.float32)
    for c in range(3):
        on = active[0, c].astype(jnp.float32)
        told = jnp.where(sub == 0, high, jnp.where(sub == 1, low, jnp.where(sub == 2, on, 0.0)))
        for out, first in ((keep_ref, half), (send_ref, 1 - half)):
            rows = t_ref[c, pl.ds(pl.multiple_of(ROWS * first, ROWS), ROWS), :]
            out[c, :, :span] = (rows.astype(jnp.float32) * on).astype(jnp.bfloat16)
            out[c, :, span:] = told.astype(jnp.bfloat16)


def split(offset, active, panel):
    half = jax.ShapeDtypeStruct((3, ROWS, panel.shape[2] + 128), jnp.bfloat16)
    return pl.pallas_call(
        split_kernel,
        out_shape=(half, half),
        in_specs=[pl.BlockSpec(memory_space=pltpu.HBM)] * 3,
        out_specs=(pl.BlockSpec(memory_space=pltpu.VMEM),) * 2,
        scratch_shapes=[
            pltpu.SMEM(offset.shape, jnp.int32),
            pltpu.SMEM(active.shape, jnp.int32),
            pltpu.VMEM(panel.shape, jnp.bfloat16),
            pltpu.SemaphoreType.DMA((3,)),
        ],
        compiler_params=pltpu.CompilerParams(vmem_limit_bytes=4 << 20),
        name="split",
    )(offset, active, panel)


def series_kernel(blocks, own, told, near, far, mine_ref, mate_ref, whole):
    z = lax.axis_index("tgrp")
    core = lax.axis_index("loop") % 2
    rows = mine_ref.shape[1]
    span = told.shape[2] - 128
    lane = lanes((rows, 128))
    whole[:, 4 * blocks :] = jnp.zeros((6, whole.shape[1] - 4 * blocks, 128), jnp.float32)
    wide = [near[...].astype(jnp.float32), far[...].astype(jnp.float32)]
    for b in range(4):
        at = pl.multiple_of(blocks * (z ^ b), 8)
        for i in range(6):
            first = 6 * blocks * (b // 2) + i * blocks
            whole[i, pl.ds(at, blocks), :] = wide[b % 2][first : first + blocks]
    for station in range(2):
        words = (own, told)[station]
        first = words[0, :, span:].astype(jnp.float32)
        shift = (32.0 * jnp.max(first[0:1]) + jnp.max(first[1:2])).astype(jnp.int32)
        row, turn = shift // 128, shift % 128
        spill = lane >= 128 - turn
        for c in range(3):
            i = 3 * station + c
            on = words[c, :, span:].astype(jnp.float32)[2:3]
            for out, half in ((mine_ref, core), (mate_ref, 1 - core)):
                at = row + 2 * blocks * half
                here = pltpu.roll(whole[i, pl.ds(at, rows), :], 128 - turn, 1)
                after = pltpu.roll(whole[i, pl.ds(at + 1, rows), :], 128 - turn, 1)
                out[i] = (jnp.where(spill, after, here) * on).astype(jnp.bfloat16)


def make_series(own, told, near, far, blocks, rows):
    window = jax.ShapeDtypeStruct((6, rows, 128), jnp.bfloat16)
    vmem = pl.BlockSpec(memory_space=pltpu.VMEM)
    return pl.pallas_call(
        functools.partial(series_kernel, blocks),
        out_shape=(window, window),
        in_specs=[vmem] * 4,
        out_specs=(vmem, vmem),
        scratch_shapes=[pltpu.VMEM((6, 2 * blocks + rows + 8, 128), jnp.float32)],
        compiler_params=pltpu.CompilerParams(vmem_limit_bytes=4 << 20),
        name="series",
    )(own, told, near, far)


def correlate_kernel(span, nb, t0, t1, t2, t3, mine, mate, masks, first_ref, second_ref,
                     tp_ref, xb_ref, xf_ref, a_ref, z_ref, d_ref, acc_ref, tot_ref, tr_ref, sems):
    lb = span // 128
    kb = lb + 1
    rows = xf_ref.shape[1]
    loop_at = lax.axis_index("loop")
    half = loop_at // 2
    copies = []
    for s, t in enumerate((t0, t1, t2, t3)):
        x = (mine, mate)[s % 2].at[pl.ds(3 * (s // 2), 3)]
        t = t.at[:, :, pl.ds(0, span)]
        copies.append(pltpu.make_async_copy(t, tp_ref.at[pl.ds(3 * s, 3), :, pl.ds(128, span)], sems.at[2 * s]))
        copies.append(pltpu.make_async_copy(x, xb_ref.at[pl.ds(3 * s, 3)], sems.at[2 * s + 1]))
    for copy in copies:
        copy.start()
    tp_ref[:, :, 0:128] = jnp.zeros((12, ROWS, 128), jnp.bfloat16)
    tp_ref[:, :, 128 + span :] = jnp.zeros((12, ROWS, 128), jnp.bfloat16)
    tot_ref[...] = jnp.zeros(tot_ref.shape, jnp.float32)
    k_first = 2 * ROWS * lax.axis_index("tgrp") + ROWS * half
    lane = lanes((8, 128))
    sub = lax.broadcasted_iota(jnp.int32, (8, 128), 0)
    counts = jnp.sum(masks[...], axis=0, keepdims=True).astype(jnp.float32)
    weight = jnp.sqrt(3.0 * span / counts)
    own = k_first + lane % ROWS
    diagonal = lanes((ROWS, 128)) % ROWS == lax.broadcasted_iota(jnp.int32, (ROWS, 128), 0)
    lane_r = lanes((rows, 128))
    for copy in copies:
        copy.wait()

    def row_scale(s):
        norm = jnp.zeros((ROWS, 128), jnp.float32)
        for c in range(3):
            for b in range(lb):
                wide = tp_ref[3 * s + c, :, 128 * b + 128 : 128 * b + 256].astype(jnp.float32)
                norm = norm + wide * wide
        inverse = 1.0 / jnp.sqrt(jnp.sum(norm, axis=1, keepdims=True) / (3.0 * span) + epsilon)
        inverse = jnp.where(diagonal, jnp.broadcast_to(inverse, (ROWS, 128)), 0.0)
        inverse = jnp.sum(inverse, axis=0, keepdims=True)
        here = masks[pl.ds(loop_at ^ s, 1), :].astype(jnp.float32) * weight
        here = jnp.take_along_axis(jnp.broadcast_to(here, (8, 128)), own, axis=1)
        return here[0:1] * inverse / (3.0 * span)

    def data_scale(s):
        squares = jnp.zeros((rows, 128), jnp.float32)
        for c in range(3):
            x = xb_ref[3 * s + c].astype(jnp.float32)
            squares = squares + x * x
        b = 1
        while b < 128:
            after = pltpu.roll(squares, rows - 1, 0)
            squares = squares + pltpu.roll(jnp.where(lane_r < b, after, squares), 128 - b, 1)
            b *= 2
        b = 1
        while b < lb:
            squares = squares + pltpu.roll(squares, rows - b, 0)
            b *= 2
        d_ref[...] = 1.0 / jnp.sqrt(squares / (3.0 * span) + epsilon)

    from_lane = (lane + sub) % 128
    inside = lane + sub < 128

    def build(i, slot):
        for r in range(SHIFTS):
            n = ROWS * (8 * (r % 2) + r // 2)
            a_ref[slot, n : n + ROWS, :] = tp_ref[i, :, 128 - 8 * r : 128 - 8 * r + 128 * kb]

        xf_ref[slot] = xb_ref[i].astype(jnp.float32)

        def turned(j):
            row = xf_ref[slot, pl.ds(j, 8, stride=0), :]
            return jnp.take_along_axis(row, from_lane, axis=1)

        before, tiles = turned(0), []
        for j in range(2 * nb + lb):
            after = turned(j + 1)
            tiles.append(jnp.where(inside, before, after))
            before = after
            if j >= nb:
                z_ref[slot, j - nb] = jnp.concatenate([tiles[j - nb], tiles[j]], axis=0).astype(jnp.bfloat16)

    def product(slot):
        left = jnp.concatenate([z_ref[slot, b : b + nb].reshape(16 * nb, 128) for b in range(kb)], axis=1)
        return lax.dot_general(left, a_ref[slot], (((1,), (1,)), ((), ())), preferred_element_type=jnp.float32)

    def weighted(rs):
        for v in (0, 1):
            index = 16 * (lane // 16) + 8 * v + sub
            for j in range(nb):
                for h in (0, 1):
                    at = 16 * j + 8 * h
                    scale = jnp.take_along_axis(d_ref[pl.ds(j + nb * h, 8, stride=0), :], index, axis=1) * rs
                    tot_ref[v, at : at + 8, :] += acc_ref[at : at + 8, 128 * v : 128 * v + 128] * scale

    build(0, 0)

    def station(s, carry):
        for c in range(3):
            m = product(c)
            build(jnp.minimum(3 * s + c + 1, 11), (c + 1) % 3)
            if c == 0:
                acc_ref[...] = m
            else:
                acc_ref[...] += m
            if c == 0:
                rs = row_scale(s)
            if c == 1:
                data_scale(s)
        weighted(rs)
        return carry

    lax.fori_loop(0, 4, station, 0)

    for f, out in enumerate((first_ref, second_ref)):
        h = half ^ f
        for jb in range(nb // 8):
            v = [[tot_ref[q, pl.ds(128 * jb + 8 * h + p, 8, stride=16), :] for p in range(8)] for q in (0, 1)]
            for b in (1, 2, 4):
                upper = (lane // b) % 2 == 1
                for q in (0, 1):
                    for p in range(8):
                        if not p & b:
                            x, y = v[q][p], v[q][p + b]
                            v[q][p] = jnp.where(upper, pltpu.roll(y, b, 1), x)
                            v[q][p + b] = jnp.where(upper, y, pltpu.roll(x, 128 - b, 1))
            upper = (lane // 8) % 2 == 1
            for p in range(8):
                x, y = v[0][p], v[1][p]
                v[0][p] = jnp.where(upper, pltpu.roll(y, 8, 1), x)
                v[1][p] = jnp.where(upper, y, pltpu.roll(x, 120, 1))
            for q in (0, 1):
                for p in range(8):
                    at = nb * (8 * q + p) + 8 * jb
                    tr_ref[f, at : at + 8, :] = v[q][p]
        levels = [jnp.zeros((8, 128), jnp.float32)] * 2
        for j in range(nb):
            codes = []
            for q in (0, 1):
                value = tr_ref[f, pl.ds(8 * nb * q + j, 8, stride=nb), :]
                top = jnp.maximum(jnp.max(jnp.abs(value), axis=1, keepdims=True), 2e-33)
                level = jnp.ceil(jnp.log2(jnp.broadcast_to(top, (8, 128))) * LEVELS)
                levels[q] = jnp.where(lane == j, level, levels[q])
                codes.append(jnp.round(value * (STEPS * jnp.exp2(level * (-1.0 / LEVELS)))))
            out[:, 128 * j : 128 * j + 128] = jnp.concatenate(codes, axis=0).astype(jnp.int32).astype(jnp.int16)
        out[:, 128 * nb :] = jnp.concatenate(levels, axis=0).astype(jnp.int32).astype(jnp.int16)


def place_kernel(flip, part_ref, *refs):
    out_ref, block, sem = refs[-3:]
    half = (lax.axis_index("tgrp") + flip) % 2
    nb = block.shape[1] // 128
    step = jnp.exp2(part_ref[:, 128 * nb :].astype(jnp.float32) * (1.0 / LEVELS)) * (1.0 / STEPS)
    for j in range(nb):
        value = part_ref[:, 128 * j : 128 * j + 128].astype(jnp.float32)
        block[:, 128 * j : 128 * j + 128] = value * step[:, j : j + 1]
    rows = pl.ds(pl.multiple_of(ROWS * half, ROWS), ROWS)
    copy = pltpu.make_async_copy(block, out_ref.at[rows, :], sem)
    copy.start()
    copy.wait()


def place(part, flip, *earlier):
    width = part.shape[1] - 128
    unread = pl.BlockSpec(memory_space=pl.ANY)
    return pl.pallas_call(
        functools.partial(place_kernel, flip),
        out_shape=jax.ShapeDtypeStruct((2 * ROWS, width), jnp.float32),
        in_specs=[pl.BlockSpec(memory_space=pltpu.VMEM)] + [unread] * len(earlier),
        out_specs=unread,
        scratch_shapes=[pltpu.VMEM((ROWS, width), jnp.float32), pltpu.SemaphoreType.DMA],
        input_output_aliases={1: 0} if earlier else {},
        compiler_params=pltpu.CompilerParams(vmem_limit_bytes=4 << 20),
        name="place",
    )(part, *earlier)


def correlate_stations(panels, series, masks, span, nb):
    lb = span // 128
    rows = series[0].shape[1]
    block = jax.ShapeDtypeStruct((ROWS, 128 * nb + 128), jnp.int16)
    vmem = pl.BlockSpec(memory_space=pltpu.VMEM)
    return pl.pallas_call(
        functools.partial(correlate_kernel, span, nb),
        out_shape=(block, block),
        in_specs=[pl.BlockSpec(memory_space=pl.ANY)] * 6 + [vmem],
        out_specs=(vmem, vmem),
        scratch_shapes=[
            pltpu.VMEM((12, ROWS, span + 256), jnp.bfloat16),
            pltpu.VMEM((12, rows, 128), jnp.bfloat16),
            pltpu.VMEM((3, rows, 128), jnp.float32),
            pltpu.VMEM((3, ROWS * SHIFTS, span + 128), jnp.bfloat16),
            pltpu.VMEM((3, nb + lb, 16, 128), jnp.bfloat16),
            pltpu.VMEM((rows, 128), jnp.float32),
            pltpu.VMEM((16 * nb, 256), jnp.float32),
            pltpu.VMEM((2, 16 * nb, 128), jnp.float32),
            pltpu.VMEM((2, 16 * nb, 128), jnp.float32),
            pltpu.SemaphoreType.DMA((8,)),
        ],
        compiler_params=pltpu.CompilerParams(vmem_limit_bytes=24 << 20),
        name="correlate",
    )(*panels, *series, masks)


def swapped(value, loop_bits, tgrp_bits):
    pairs = [(4 * l + z, 4 * (l ^ loop_bits) + (z ^ tgrp_bits)) for l in range(4) for z in range(4)]
    return lax.ppermute(value, ("loop", "tgrp"), pairs)


def to_owner(value, flip):
    pairs = [(4 * l + z, 4 * z + 2 * (l % 2) + ((l // 2) ^ flip)) for l in range(4) for z in range(4)]
    return lax.ppermute(value, ("loop", "tgrp"), pairs)


def local_plane(data, templates, masks, offsets, active):
    span = templates.shape[3]
    nb = data.shape[2] // 128
    panel = templates[:, 0].transpose(1, 0, 2)
    keep, send = split(offsets, active, panel)
    panel_c = swapped(keep, 1, 0)
    pieces = data.reshape(3 * nb, 128)
    pieces_y, send = lax.optimization_barrier((swapped(pieces, 2, 0), send))
    pair = jnp.concatenate([pieces, pieces_y], axis=0)
    panel_y = swapped(send, 2, 0)
    near = jnp.concatenate([pair, swapped(pair, 0, 2)], axis=0)
    far = swapped(near, 0, 1)
    mine, mate = make_series(keep, panel_y, near, far, nb, 2 * nb + span // 128 + 8)
    mate = swapped(mate, 1, 0)
    panel_late, _ = lax.optimization_barrier((panel_y, far))
    panel_yc = swapped(panel_late, 1, 0)
    first, second = correlate_stations(
        (keep, panel_c, panel_y, panel_yc), (mine, mate), masks.T, span, nb
    )
    second, first = to_owner(second, 1), to_owner(first, 0)
    return place(first, 0, place(second, 1))


def solution(mesh):
    placed = (
        P(("parts", "loop"), None, "tgrp"),
        P("tgrp", "loop", None, None),
        P(),
        P(("parts", "loop")),
        P(("parts", "loop"), None),
    )

    def local(data, templates, masks, offsets, active):
        grid = (mesh.shape["loop"], mesh.shape["tgrp"])
        fits = grid == (4, 4) and templates.shape[:2] == (2 * ROWS, 1) and masks.shape[0] == 128
        fits = fits and templates.shape[3] == 2048 and data.shape[0] == 1 and data.shape[2] % 1024 == 0
        plan = local_plane if fits else local_general
        return plan(data, templates, masks, offsets, active)

    return jax.shard_map(
        local, mesh=mesh, in_specs=placed, out_specs=P(("parts", "loop"), "tgrp"), check_vma=False
    )
```

```python
import functools

import jax
import jax.numpy as jnp
from jax import lax
from jax.experimental import pallas as pl
from jax.experimental.pallas import tpu as pltpu
from jax.sharding import PartitionSpec as P

L = 2048


epsilon = 1e-05


def passed_along(value, axis, steps):
    count = lax.axis_size(axis)
    initial, last = (max(0, -steps), min(count, count - steps))
    return lax.ppermute(value, axis, [(source, source + steps) for source in range(initial, last)])


def window_energy(squares, out_len, span):
    inner_len = out_len + span - 128
    nblocks = (inner_len + 127) // 128
    total_len = 128 * (nblocks + 1)
    padded = jnp.concatenate([squares, jnp.zeros((total_len - squares.shape[0],), squares.dtype)])
    first = padded[: 128 * nblocks].reshape(nblocks, 128)
    second = padded[128 : 128 * nblocks + 128].reshape(nblocks, 128)
    segments = jnp.concatenate([first, second], axis=1)
    rows_at = lax.broadcasted_iota(jnp.int32, (256, 128), 0)
    cols_at = lax.broadcasted_iota(jnp.int32, (256, 128), 1)
    gap = rows_at - cols_at
    band = jnp.where((gap >= 0) & (gap < 128), 1.0, 0.0).astype(squares.dtype)
    inner = jnp.dot(segments, band, precision=lax.Precision.HIGHEST).reshape(nblocks * 128)
    energy = jnp.zeros((out_len,), squares.dtype)
    for block_at in range(span // 128):
        energy = energy + inner[128 * block_at : 128 * block_at + out_len]
    return energy


def correlate(panel, window, out_len):
    row_count = panel.shape[0]
    blocks = panel.shape[2] // 128
    span_len = out_len + panel.shape[2] - 128
    unfold = jnp.stack(
        [window[:, shift_by : shift_by + span_len] for shift_by in range(128)], axis=1
    )
    unfold = unfold.reshape(3 * 128, span_len)
    frames = (
        panel.reshape(row_count, 3, blocks, 128)
        .transpose(0, 2, 1, 3)
        .reshape(row_count, blocks, 3 * 128)
    )

    def add_block(block_at, running_sum):
        start_at = (block_at * 128).astype(jnp.int32)
        columns = lax.dynamic_slice_in_dim(unfold, start_at, out_len, 1)
        weights_now = lax.dynamic_index_in_dim(frames, block_at, 1, keepdims=False)
        return running_sum + jnp.dot(weights_now, columns, preferred_element_type=jnp.float32)

    return lax.fori_loop(0, blocks, add_block, jnp.zeros((row_count, out_len), jnp.float32))


def local_general(data, templates, masks, offsets, active):
    local_count = data.shape[0]
    block_len = data.shape[2]
    following = passed_along(data, "tgrp", -1)
    extended = jnp.concatenate([data, following], axis=2)
    loop_at = lax.axis_index("loop")
    first_station = loop_at * local_count
    counts = jnp.sum(masks, axis=1).astype(jnp.float32)
    local_masks = lax.dynamic_slice_in_dim(masks, first_station, local_count, 1)
    weights = local_masks.astype(jnp.float32) * jnp.sqrt(3.0 * L / counts)[:, None]
    station = 0
    channel_on = active[station].astype(jnp.bfloat16)
    series = lax.dynamic_slice(
        extended[station], (jnp.int32(0), offsets[station]), (3, block_len + L)
    )
    window = series * channel_on[:, None]
    wide_window = window.astype(jnp.float32)
    squares = jnp.sum(wide_window * wide_window, axis=0)
    energy = window_energy(squares, block_len, L)
    inv_datas = [1.0 / jnp.sqrt(energy / (3.0 * L) + epsilon)]
    windows = [window]
    channel_sets = [channel_on]
    panel_rows = lax.all_gather(templates, "tgrp", axis=0, tiled=True)
    station = 0
    panel = panel_rows[:, station] * channel_sets[station][None, :, None]
    wide_panel = panel.astype(jnp.float32)
    inv_template = 1.0 / jnp.sqrt(
        jnp.sum(wide_panel * wide_panel, axis=(1, 2)) / (3.0 * L) + epsilon
    )
    corr = correlate(panel, windows[station], block_len)
    row_weights = weights[:, station]
    row_scale = inv_template * row_weights
    stacked = corr * inv_datas[station][None, :] * row_scale[:, None] / (3.0 * L)
    rows_here = stacked.shape[0] // lax.axis_size("loop")
    summed = lax.psum(stacked, "loop")
    return lax.dynamic_slice_in_dim(summed, loop_at * rows_here, rows_here, 0)


ROWS = 16
SHIFTS = 16
STEPS = 32700.0
LEVELS = 64.0


def lanes(shape):
    return lax.broadcasted_iota(jnp.int32, shape, len(shape) - 1)


def split_kernel(offset_in, active_in, t_in, keep_ref, send_ref, offset, active, t_ref, sems):
    copies = [
        pltpu.make_async_copy(t_in, t_ref, sems.at[0]),
        pltpu.make_async_copy(offset_in, offset, sems.at[1]),
        pltpu.make_async_copy(active_in, active, sems.at[2]),
    ]
    for copy in copies:
        copy.start()
    for copy in copies:
        copy.wait()
    half = lax.axis_index("loop") // 2
    span = t_ref.shape[2]
    sub = lax.broadcasted_iota(jnp.int32, (ROWS, 128), 0)
    high, low = (offset[0] // 32).astype(jnp.float32), (offset[0] % 32).astype(jnp.float32)
    for c in range(3):
        on = active[0, c].astype(jnp.float32)
        told = jnp.where(sub == 0, high, jnp.where(sub == 1, low, jnp.where(sub == 2, on, 0.0)))
        for out, first in ((keep_ref, half), (send_ref, 1 - half)):
            rows = t_ref[c, pl.ds(pl.multiple_of(ROWS * first, ROWS), ROWS), :]
            out[c, :, :span] = (rows.astype(jnp.float32) * on).astype(jnp.bfloat16)
            out[c, :, span:] = told.astype(jnp.bfloat16)


def split(offset, active, panel):
    half = jax.ShapeDtypeStruct((3, ROWS, panel.shape[2] + 128), jnp.bfloat16)
    return pl.pallas_call(
        split_kernel,
        out_shape=(half, half),
        in_specs=[pl.BlockSpec(memory_space=pltpu.HBM)] * 3,
        out_specs=(pl.BlockSpec(memory_space=pltpu.VMEM),) * 2,
        scratch_shapes=[
            pltpu.SMEM(offset.shape, jnp.int32),
            pltpu.SMEM(active.shape, jnp.int32),
            pltpu.VMEM(panel.shape, jnp.bfloat16),
            pltpu.SemaphoreType.DMA((3,)),
        ],
        compiler_params=pltpu.CompilerParams(vmem_limit_bytes=4 << 20),
        name="split",
    )(offset, active, panel)


def series_kernel(blocks, own, told, near, far, mine_ref, mate_ref, whole):
    z = lax.axis_index("tgrp")
    core = lax.axis_index("loop") % 2
    rows = mine_ref.shape[1]
    span = told.shape[2] - 128
    lane = lanes((rows, 128))
    whole[:, 4 * blocks :] = jnp.zeros((6, whole.shape[1] - 4 * blocks, 128), jnp.float32)
    wide = [near[...].astype(jnp.float32), far[...].astype(jnp.float32)]
    for b in range(4):
        at = pl.multiple_of(blocks * (z ^ b), 8)
        for i in range(6):
            first = 6 * blocks * (b // 2) + i * blocks
            whole[i, pl.ds(at, blocks), :] = wide[b % 2][first : first + blocks]
    for station in range(2):
        words = (own, told)[station]
        first = words[0, :, span:].astype(jnp.float32)
        shift = (32.0 * jnp.max(first[0:1]) + jnp.max(first[1:2])).astype(jnp.int32)
        row, turn = shift // 128, shift % 128
        spill = lane >= 128 - turn
        for c in range(3):
            i = 3 * station + c
            on = words[c, :, span:].astype(jnp.float32)[2:3]
            for out, half in ((mine_ref, core), (mate_ref, 1 - core)):
                at = row + 2 * blocks * half
                here = pltpu.roll(whole[i, pl.ds(at, rows), :], 128 - turn, 1)
                after = pltpu.roll(whole[i, pl.ds(at + 1, rows), :], 128 - turn, 1)
                out[i] = (jnp.where(spill, after, here) * on).astype(jnp.bfloat16)


def make_series(own, told, near, far, blocks, rows):
    window = jax.ShapeDtypeStruct((6, rows, 128), jnp.bfloat16)
    vmem = pl.BlockSpec(memory_space=pltpu.VMEM)
    return pl.pallas_call(
        functools.partial(series_kernel, blocks),
        out_shape=(window, window),
        in_specs=[vmem] * 4,
        out_specs=(vmem, vmem),
        scratch_shapes=[pltpu.VMEM((6, 2 * blocks + rows + 8, 128), jnp.float32)],
        compiler_params=pltpu.CompilerParams(vmem_limit_bytes=4 << 20),
        name="series",
    )(own, told, near, far)


def correlate_kernel(span, nb, t0, t1, t2, t3, mine, mate, masks, first_ref, second_ref,
                     tp_ref, xb_ref, xf_ref, a_ref, z_ref, d_ref, acc_ref, tot_ref, tr_ref, sems):
    lb = span // 128
    kb = lb + 1
    rows = xf_ref.shape[1]
    loop_at = lax.axis_index("loop")
    half = loop_at // 2
    copies = []
    for s, t in enumerate((t0, t1, t2, t3)):
        x = (mine, mate)[s % 2].at[pl.ds(3 * (s // 2), 3)]
        t = t.at[:, :, pl.ds(0, span)]
        copies.append(pltpu.make_async_copy(t, tp_ref.at[pl.ds(3 * s, 3), :, pl.ds(128, span)], sems.at[2 * s]))
        copies.append(pltpu.make_async_copy(x, xb_ref.at[pl.ds(3 * s, 3)], sems.at[2 * s + 1]))
    for copy in copies:
        copy.start()
    tp_ref[:, :, 0:128] = jnp.zeros((12, ROWS, 128), jnp.bfloat16)
    tp_ref[:, :, 128 + span :] = jnp.zeros((12, ROWS, 128), jnp.bfloat16)
    tot_ref[...] = jnp.zeros(tot_ref.shape, jnp.float32)
    k_first = 2 * ROWS * lax.axis_index("tgrp") + ROWS * half
    lane = lanes((8, 128))
    sub = lax.broadcasted_iota(jnp.int32, (8, 128), 0)
    counts = jnp.sum(masks[...], axis=0, keepdims=True).astype(jnp.float32)
    weight = jnp.sqrt(3.0 * span / counts)
    own = k_first + lane % ROWS
    diagonal = lanes((ROWS, 128)) % ROWS == lax.broadcasted_iota(jnp.int32, (ROWS, 128), 0)
    lane_r = lanes((rows, 128))
    for copy in copies:
        copy.wait()

    def row_scale(s):
        norm = jnp.zeros((ROWS, 128), jnp.float32)
        for c in range(3):
            for b in range(lb):
                wide = tp_ref[3 * s + c, :, 128 * b + 128 : 128 * b + 256].astype(jnp.float32)
                norm = norm + wide * wide
        inverse = 1.0 / jnp.sqrt(jnp.sum(norm, axis=1, keepdims=True) / (3.0 * span) + epsilon)
        inverse = jnp.where(diagonal, jnp.broadcast_to(inverse, (ROWS, 128)), 0.0)
        inverse = jnp.sum(inverse, axis=0, keepdims=True)
        here = masks[pl.ds(loop_at ^ s, 1), :].astype(jnp.float32) * weight
        here = jnp.take_along_axis(jnp.broadcast_to(here, (8, 128)), own, axis=1)
        return here[0:1] * inverse / (3.0 * span)

    def data_scale(s):
        squares = jnp.zeros((rows, 128), jnp.float32)
        for c in range(3):
            x = xb_ref[3 * s + c].astype(jnp.float32)
            squares = squares + x * x
        b = 1
        while b < 128:
            after = pltpu.roll(squares, rows - 1, 0)
            squares = squares + pltpu.roll(jnp.where(lane_r < b, after, squares), 128 - b, 1)
            b *= 2
        b = 1
        while b < lb:
            squares = squares + pltpu.roll(squares, rows - b, 0)
            b *= 2
        d_ref[...] = 1.0 / jnp.sqrt(squares / (3.0 * span) + epsilon)

    from_lane = (lane + sub) % 128
    inside = lane + sub < 128

    def build(i, slot):
        for r in range(SHIFTS):
            n = ROWS * (8 * (r % 2) + r // 2)
            a_ref[slot, n : n + ROWS, :] = tp_ref[i, :, 128 - 8 * r : 128 - 8 * r + 128 * kb]

        xf_ref[slot] = xb_ref[i].astype(jnp.float32)

        def turned(j):
            row = xf_ref[slot, pl.ds(j, 8, stride=0), :]
            return jnp.take_along_axis(row, from_lane, axis=1)

        before, tiles = turned(0), []
        for j in range(2 * nb + lb):
            after = turned(j + 1)
            tiles.append(jnp.where(inside, before, after))
            before = after
            if j >= nb:
                z_ref[slot, j - nb] = jnp.concatenate([tiles[j - nb], tiles[j]], axis=0).astype(jnp.bfloat16)

    def product(slot):
        left = jnp.concatenate([z_ref[slot, b : b + nb].reshape(16 * nb, 128) for b in range(kb)], axis=1)
        return lax.dot_general(left, a_ref[slot], (((1,), (1,)), ((), ())), preferred_element_type=jnp.float32)

    def weighted(rs):
        for v in (0, 1):
            index = 16 * (lane // 16) + 8 * v + sub
            for j in range(nb):
                for h in (0, 1):
                    at = 16 * j + 8 * h
                    scale = jnp.take_along_axis(d_ref[pl.ds(j + nb * h, 8, stride=0), :], index, axis=1) * rs
                    tot_ref[v, at : at + 8, :] += acc_ref[at : at + 8, 128 * v : 128 * v + 128] * scale

    build(0, 0)

    def station(s, carry):
        for c in range(3):
            m = product(c)
            build(jnp.minimum(3 * s + c + 1, 11), (c + 1) % 3)
            if c == 0:
                acc_ref[...] = m
            else:
                acc_ref[...] += m
            if c == 0:
                rs = row_scale(s)
            if c == 1:
                data_scale(s)
        weighted(rs)
        return carry

    lax.fori_loop(0, 4, station, 0)

    for f, out in enumerate((first_ref, second_ref)):
        h = half ^ f
        for jb in range(nb // 8):
            v = [[tot_ref[q, pl.ds(128 * jb + 8 * h + p, 8, stride=16), :] for p in range(8)] for q in (0, 1)]
            for b in (1, 2, 4):
                upper = (lane // b) % 2 == 1
                for q in (0, 1):
                    for p in range(8):
                        if not p & b:
                            x, y = v[q][p], v[q][p + b]
                            v[q][p] = jnp.where(upper, pltpu.roll(y, b, 1), x)
                            v[q][p + b] = jnp.where(upper, y, pltpu.roll(x, 128 - b, 1))
            upper = (lane // 8) % 2 == 1
            for p in range(8):
                x, y = v[0][p], v[1][p]
                v[0][p] = jnp.where(upper, pltpu.roll(y, 8, 1), x)
                v[1][p] = jnp.where(upper, y, pltpu.roll(x, 120, 1))
            for q in (0, 1):
                for p in range(8):
                    at = nb * (8 * q + p) + 8 * jb
                    tr_ref[f, at : at + 8, :] = v[q][p]
        levels = [jnp.zeros((8, 128), jnp.float32)] * 2
        for j in range(nb):
            codes = []
            for q in (0, 1):
                value = tr_ref[f, pl.ds(8 * nb * q + j, 8, stride=nb), :]
                top = jnp.maximum(jnp.max(jnp.abs(value), axis=1, keepdims=True), 2e-33)
                level = jnp.ceil(jnp.log2(jnp.broadcast_to(top, (8, 128))) * LEVELS)
                levels[q] = jnp.where(lane == j, level, levels[q])
                codes.append(jnp.round(value * (STEPS * jnp.exp2(level * (-1.0 / LEVELS)))))
            out[:, 128 * j : 128 * j + 128] = jnp.concatenate(codes, axis=0).astype(jnp.int32).astype(jnp.int16)
        out[:, 128 * nb :] = jnp.concatenate(levels, axis=0).astype(jnp.int32).astype(jnp.int16)


def place_kernel(flip, part_ref, *refs):
    out_ref, block, sems = refs[-3:]
    half = (lax.axis_index("tgrp") + flip) % 2
    nb = block.shape[1] // 128
    step = jnp.exp2(part_ref[:, 128 * nb :].astype(jnp.float32) * (1.0 / LEVELS)) * (1.0 / STEPS)
    rows = pl.ds(pl.multiple_of(ROWS * half, ROWS), ROWS)
    copies = []
    for chunk, (low, high) in enumerate(((0, nb // 2), (nb // 2, nb))):
        for j in range(low, high):
            value = part_ref[:, 128 * j : 128 * j + 128].astype(jnp.float32)
            block[:, 128 * j : 128 * j + 128] = value * step[:, j : j + 1]
        columns = pl.ds(128 * low, 128 * (high - low))
        copies.append(pltpu.make_async_copy(block.at[:, columns], out_ref.at[rows, columns], sems.at[chunk]))
        copies[-1].start()
    for copy in copies:
        copy.wait()


def place(part, flip, *earlier):
    width = part.shape[1] - 128
    unread = pl.BlockSpec(memory_space=pl.ANY)
    return pl.pallas_call(
        functools.partial(place_kernel, flip),
        out_shape=jax.ShapeDtypeStruct((2 * ROWS, width), jnp.float32),
        in_specs=[pl.BlockSpec(memory_space=pltpu.VMEM)] + [unread] * len(earlier),
        out_specs=unread,
        scratch_shapes=[pltpu.VMEM((ROWS, width), jnp.float32), pltpu.SemaphoreType.DMA((2,))],
        input_output_aliases={1: 0} if earlier else {},
        compiler_params=pltpu.CompilerParams(vmem_limit_bytes=4 << 20),
        name="place",
    )(part, *earlier)


def correlate_stations(panels, series, masks, span, nb):
    lb = span // 128
    rows = series[0].shape[1]
    block = jax.ShapeDtypeStruct((ROWS, 128 * nb + 128), jnp.int16)
    vmem = pl.BlockSpec(memory_space=pltpu.VMEM)
    return pl.pallas_call(
        functools.partial(correlate_kernel, span, nb),
        out_shape=(block, block),
        in_specs=[pl.BlockSpec(memory_space=pl.ANY)] * 6 + [vmem],
        out_specs=(vmem, vmem),
        scratch_shapes=[
            pltpu.VMEM((12, ROWS, span + 256), jnp.bfloat16),
            pltpu.VMEM((12, rows, 128), jnp.bfloat16),
            pltpu.VMEM((3, rows, 128), jnp.float32),
            pltpu.VMEM((3, ROWS * SHIFTS, span + 128), jnp.bfloat16),
            pltpu.VMEM((3, nb + lb, 16, 128), jnp.bfloat16),
            pltpu.VMEM((rows, 128), jnp.float32),
            pltpu.VMEM((16 * nb, 256), jnp.float32),
            pltpu.VMEM((2, 16 * nb, 128), jnp.float32),
            pltpu.VMEM((2, 16 * nb, 128), jnp.float32),
            pltpu.SemaphoreType.DMA((8,)),
        ],
        compiler_params=pltpu.CompilerParams(vmem_limit_bytes=24 << 20),
        name="correlate",
    )(*panels, *series, masks)


def swapped(value, loop_bits, tgrp_bits):
    pairs = [(4 * l + z, 4 * (l ^ loop_bits) + (z ^ tgrp_bits)) for l in range(4) for z in range(4)]
    return lax.ppermute(value, ("loop", "tgrp"), pairs)


def to_owner(value, flip):
    pairs = [(4 * l + z, 4 * z + 2 * (l % 2) + ((l // 2) ^ flip)) for l in range(4) for z in range(4)]
    return lax.ppermute(value, ("loop", "tgrp"), pairs)


def local_plane(data, templates, masks, offsets, active):
    span = templates.shape[3]
    nb = data.shape[2] // 128
    panel = templates[:, 0].transpose(1, 0, 2)
    keep, send = split(offsets, active, panel)
    panel_c = swapped(keep, 1, 0)
    pieces = data.reshape(3 * nb, 128)
    pieces_y, send = lax.optimization_barrier((swapped(pieces, 2, 0), send))
    pair = jnp.concatenate([pieces, pieces_y], axis=0)
    panel_y = swapped(send, 2, 0)
    near = jnp.concatenate([pair, swapped(pair, 0, 2)], axis=0)
    far = swapped(near, 0, 1)
    mine, mate = make_series(keep, panel_y, near, far, nb, 2 * nb + span // 128 + 8)
    mate = swapped(mate, 1, 0)
    panel_late, _ = lax.optimization_barrier((panel_y, far))
    panel_yc = swapped(panel_late, 1, 0)
    first, second = correlate_stations(
        (keep, panel_c, panel_y, panel_yc), (mine, mate), masks.T, span, nb
    )
    second, first = to_owner(second, 1), to_owner(first, 0)
    return place(first, 0, place(second, 1))


def solution(mesh):
    placed = (
        P(("parts", "loop"), None, "tgrp"),
        P("tgrp", "loop", None, None),
        P(),
        P(("parts", "loop")),
        P(("parts", "loop"), None),
    )

    def local(data, templates, masks, offsets, active):
        grid = (mesh.shape["loop"], mesh.shape["tgrp"])
        fits = grid == (4, 4) and templates.shape[:2] == (2 * ROWS, 1) and masks.shape[0] == 128
        fits = fits and templates.shape[3] == 2048 and data.shape[0] == 1 and data.shape[2] % 1024 == 0
        plan = local_plane if fits else local_general
        return plan(data, templates, masks, offsets, active)

    return jax.shard_map(
        local, mesh=mesh, in_specs=placed, out_specs=P(("parts", "loop"), "tgrp"), check_vma=False
    )
```
